256 devices in a mesh: pos: 32 (over x, y, core), freq: 8 (over z).
Axes of the slice: x: 4, y: 4, z: 8, core: 2. Of those that a mesh axis runs over, the one named last changes fastest.
Arguments:
- footprint: int32 [64, 32], replicated, may hold values from 0 to 1023, as said below
- basis: bfloat16 [64, 16, 2048, 256], P('pos', 'freq'), may hold values from -0.125 to 0.125
- weights: float32 [256], replicated, may hold values from 0.1 to 10
- conduct: float32 [2, 128, 256], P(None, 'pos', 'freq'), may hold values from 0.08 to 0.24
- baseline: float32 [128, 256], P('pos', 'freq'), may hold values from 0.2 to 2
Outputs:
- image: float32 [128, 256], P('pos', 'freq')
The draws below stay inside these ranges and needn't reach their ends.
Inputs may be any that keep to these rules, and one draw needn't show every extreme that they name: `footprint`: tile t belongs to owner t // 32. Among the 64 entries of the rows of one index of pos, at most 4 lie in one owner's tiles, and in every draw one owner gets exactly 4 from every index of pos. Entries may repeat.
All inputs are finite; a program needn't handle non-finite values.
Results may differ from the reference program's by a relative error of at most 0.0003.
Values sent between devices are 32-bit elements; how exact they have to be, the bound alone decides.
A program may use at most 64 MiB of HBM per device.

```python
import math
import jax
import jax.numpy as jnp
from jax import lax

ELEM = 1024
R = 256
FREQS = 16
POS_DEV = 2
FOOT = 32
TH = 4
TW = 8
TILE_DEV = 32
PASSES = 3
POSITIONS = 64
TILES = 1024
CAP = 4
NX = 128
NZ = 256
N_POS = 32


def draw_footprint(key, part):
    owner_count = TILES // TILE_DEV
    block_rows = POS_DEV * FOOT
    slot_count = owner_count * CAP
    hot_owner = jax.random.randint(jax.random.fold_in(key, 1), (), 0, owner_count)

    def one_block(block_key):
        slot_ids = jnp.arange(slot_count)
        slot_owner = slot_ids // CAP
        shuffled = jax.random.permutation(jax.random.fold_in(block_key, 2), slot_count)
        forced = (slot_ids == 0) | (slot_ids == slot_count - CAP)
        score = jnp.where(slot_owner == hot_owner, slot_ids - 2 * slot_count, jnp.where(forced, slot_ids - slot_count, shuffled))
        picked = slot_owner[jnp.argsort(score)[:block_rows]]
        within = jax.random.randint(jax.random.fold_in(block_key, 3), (block_rows,), 0, TILE_DEV)
        within = within.at[jnp.argmax(picked == owner_count - 1)].set(TILE_DEV - 1)
        within = within.at[jnp.argmax(picked == 0)].set(0)
        mixing = jax.random.permutation(jax.random.fold_in(block_key, 4), block_rows)
        return (picked * TILE_DEV + within)[mixing]
    block_keys = jax.vmap(lambda index: jax.random.fold_in(key, index + 10))(jnp.arange(POSITIONS // POS_DEV))
    return jax.vmap(one_block)(block_keys).reshape(POSITIONS, FOOT).astype(jnp.int32)


def steps_of(own_key, dims, cuts, smallest, high):
    gain = 1.0
    for dim, parts in cuts:
        heights = jax.random.uniform(jax.random.fold_in(jax.random.fold_in(own_key, 6), dim), (parts,), jnp.float32, smallest / len(cuts), high / len(cuts))
        gain = gain * jnp.repeat(jnp.exp(heights), dims[dim] // parts).reshape((-1,) + (1,) * (len(dims) - 1 - dim))
    return gain


def noise(rng, dims, spread, limit, split=(), held_as=jnp.bfloat16):
    level = steps_of(rng, dims, split, -0.22, 0.18) if split else 1.0
    array = jax.random.normal(rng, dims, jnp.float32) * spread * level
    return jnp.minimum(jnp.maximum(array, -limit), limit).astype(held_as)


def setup_inputs(seed: int = 0) -> dict:
    keys = jax.random.split(jax.random.key(seed), 6)
    return {
        "footprint": draw_footprint(jax.random.fold_in(keys[5], 71), 0),
        "basis": noise(keys[1], (POSITIONS, FREQS, 2 * ELEM, R), (2 * ELEM) ** -0.5, 0.125, ((0, 32), (1, 8))),
        "weights": jnp.clip(jnp.exp(jax.random.uniform(keys[2], (R,), jnp.float32, math.log(0.1), math.log(10.0))), 0.1, 10.0),
        "conduct": jnp.clip(0.08 + 0.16 * jax.random.uniform(keys[3], (2, NX, NZ), jnp.float32) ** steps_of(keys[3], (2, NX, NZ), ((1, 32), (2, 8)), -0.2, 0.2), 0.08, 0.24),
        "baseline": jnp.clip(0.2 + 1.8 * jax.random.uniform(keys[4], (NX, NZ), jnp.float32) ** steps_of(keys[4], (NX, NZ), ((0, 32), (1, 8)), -0.2, 0.2), 0.2, 2.0),
    }


elem_pitch = 0.125
cell_spacing = 0.7
top_depth = 4.0
eps_value = 1e-06

def green_rows(tile_ids, pos_global, freq_global, elements, positions, freqs):
    cells = jnp.arange(TH * TW)
    grid_row = (tile_ids // TILE_DEV)[:, None] * TH + (cells // TW)[None, :]
    grid_col = (tile_ids % TILE_DEV)[:, None] * TW + (cells % TW)[None, :]
    depth = top_depth + cell_spacing * grid_row.reshape(-1).astype(jnp.float32)
    lateral = cell_spacing * grid_col.reshape(-1).astype(jnp.float32)
    centre = pos_global.astype(jnp.float32) * (cell_spacing * TW * TILE_DEV / positions)
    element = (jnp.arange(elements).astype(jnp.float32) - 0.5 * (elements - 1)) * elem_pitch + centre
    across = lateral[:, None] - element[None, :]
    distance = jnp.sqrt(depth[:, None] * depth[:, None] + across * across)
    wavenum = 2.0 * math.pi * (0.5 + freq_global.astype(jnp.float32) / freqs)
    amplitude = jnp.sqrt(top_depth / distance)
    phase = wavenum * distance
    return jnp.concatenate([amplitude * jnp.cos(phase), amplitude * jnp.sin(phase)], axis=1).astype(jnp.bfloat16)

def relax(values, across_k, along_k):
    centre_x = across_k[1:-1, 1:-1]
    centre_z = along_k[1:-1, 1:-1]
    middle = values[1:-1, 1:-1]
    north = jnp.minimum(centre_x, across_k[:-2, 1:-1]) * (values[:-2, 1:-1] - middle)
    south = jnp.minimum(centre_x, across_k[2:, 1:-1]) * (values[2:, 1:-1] - middle)
    west = jnp.minimum(centre_z, along_k[1:-1, :-2]) * (values[1:-1, :-2] - middle)
    east = jnp.minimum(centre_z, along_k[1:-1, 2:]) * (values[1:-1, 2:] - middle)
    return middle + north + south + west + east

def reference(footprint, basis, weights, conduct, baseline):
    tile_cells = TH * TW

    def one_position(pos_index):
        tile_ids = footprint[pos_index]

        def add_freq(running, freq_index):
            green = green_rows(tile_ids, pos_index, freq_index, ELEM, POSITIONS, FREQS)
            return (running + jnp.dot(green, basis[pos_index, freq_index], preferred_element_type=jnp.float32), None)
        start = jnp.zeros((FOOT * tile_cells, R), jnp.float32)
        total, _ = lax.scan(add_freq, start, jnp.arange(FREQS))
        return total
    coeffs = lax.map(one_position, jnp.arange(POSITIONS))
    compound = jnp.zeros((TILES, tile_cells, R), jnp.float32).at[footprint.reshape(-1)].add(coeffs.reshape(POSITIONS * FOOT, tile_cells, R))
    intensity = jnp.sqrt(lax.optimization_barrier(jnp.sum(compound * compound * weights, axis=-1)) / R + eps_value)
    grid = intensity.reshape(N_POS, TILE_DEV, TH, TW).transpose(0, 2, 1, 3).reshape(N_POS * TH, TILE_DEV * TW)
    grid = grid + baseline
    across_k = jnp.pad(conduct[0], 1)
    along_k = jnp.pad(conduct[1], 1)
    for sweep in range(PASSES):
        grid = relax(jnp.pad(grid, 1), across_k, along_k)
    return grid
```

```python
import functools

import jax
import jax.numpy as jnp
from jax import lax
from jax.experimental import pallas as pl
from jax.experimental.pallas import tpu as pltpu
from jax.sharding import PartitionSpec as P

TH = 4
TW = 8
CELLS = TH * TW
TILE_DEV = 32
PASSES = 3
CAP = 4
EPS = 1e-06
MESH = pl.DeviceIdType.MESH

UNIT = 0.025
CELL = 28
PITCH = 5
TOP = 160
MAGIC = 12582912.0
SIN_POLY = (4.442879567546084, -7.307816684491789, 3.597774178087233, -0.7911993921613406)
COS_POLY = (
    1.4142134962552289,
    -6.978850948563853,
    5.7394603769076955,
    -1.8835579059892091,
    0.31068802753070307,
)
CHUNK = 256


def green_block(cross, depth_sq, turns):
    square = cross * cross + depth_sq
    dist = square * lax.rsqrt(square)
    amp = lax.rsqrt(dist) * ((TOP) ** 0.5)
    out = []
    for rate in turns:
        phase = dist * rate
        whole = (phase + MAGIC) - MAGIC
        part = phase - whole
        z = part * part
        s = ((SIN_POLY[3] * z + SIN_POLY[2]) * z + SIN_POLY[1]) * z + SIN_POLY[0]
        c = (((COS_POLY[4] * z + COS_POLY[3]) * z + COS_POLY[2]) * z + COS_POLY[1]) * z + COS_POLY[0]
        s = s * part
        q = amp * s
        out.append(((amp - q * s).astype(jnp.bfloat16), (q * c).astype(jnp.bfloat16)))
    return out


def make_unit(lat_ref, dep_ref, basis_v, green_s, rates, elements):
    rows = lat_ref.shape[1]
    chunks = elements // CHUNK

    def unit(col, p):
        total = None
        for kc in range(chunks):
            buf = green_s.at[kc % green_s.shape[0]]
            for lt in range(CHUNK // 128):
                start = PITCH * (kc * CHUNK + lt * 128)
                shift = (2 * CELL * col + (PITCH * (elements - 1) - 2 * start)).astype(jnp.float32) * 0.5
                for rg in range(rows // 16):
                    span = pl.ds(rg * 16, 16)
                    values = green_block(lat_ref[p, span, :] + shift, dep_ref[p, span, :], rates)
                    for f, (cosine, sine) in enumerate(values):
                        base = f * 2 * CHUNK + lt * 128
                        buf[span, pl.ds(base, 128)] = cosine
                        buf[span, pl.ds(base + CHUNK, 128)] = sine
            part = jnp.dot(buf[...], basis_v[p, kc], preferred_element_type=jnp.float32)
            total = part if total is None else total + part
        return total

    return unit


def split3(x):
    hi = x.astype(jnp.bfloat16)
    rest = x - hi.astype(jnp.float32)
    mid = rest.astype(jnp.bfloat16)
    low = (rest - mid.astype(jnp.float32)).astype(jnp.bfloat16)
    return hi, mid, low


def kernel(
    n_pos,
    n_freq,
    slot_ref,
    lat_ref,
    dep_ref,
    inc_ref,
    weight_ref,
    halo_ref,
    basis_ref,
    out_ref,
    basis_v,
    green_s,
    send_b,
    recv_b,
    final_b,
    packed,
    arrived,
    value_b,
    value_r,
    halo_r,
    basis_sem,
    ring_send,
    ring_recv,
    own_sem,
    a2a_send,
    a2a_recv,
    val_send,
    val_recv,
    halo_send,
    halo_recv,
):
    pos = lax.axis_index("pos")
    freq = lax.axis_index("freq")
    freq_local = basis_ref.shape[1]
    elements = basis_ref.shape[2] // 2
    freqs = freq_local * n_freq
    rows = lat_ref.shape[1]
    half = n_freq // 2
    messages = 4 * half - 2
    chunks = elements // CHUNK

    def other(dp, df):
        return (lax.rem(pos + dp + n_pos, n_pos), lax.rem(freq + df + n_freq, n_freq))

    barrier = pltpu.get_barrier_semaphore()
    near = [(dp, df) for dp in (-1, 0, 1) for df in range(n_freq) if (dp, df) != (0, 0)]
    sideways = [(dp, df) for dp, df in near if df != 0]
    for dp, df in sideways:
        pl.semaphore_signal(barrier, inc=1, device_id=other(dp, df), device_id_type=MESH)

    @pl.loop(1, n_pos)
    def _(step):
        pl.semaphore_signal(barrier, inc=1, device_id=other(step, 0), device_id_type=MESH)

    def basis_copies(p):
        copies = []
        for kc in range(chunks):
            for f in range(freq_local):
                for part in range(2):
                    copies.append(
                        pltpu.make_async_copy(
                            basis_ref.at[p, f, pl.ds(part * elements + kc * CHUNK, CHUNK), :],
                            basis_v.at[p, kc, pl.ds((2 * f + part) * CHUNK, CHUNK), :],
                            basis_sem.at[p, (kc * freq_local + f) * 2 + part],
                        )
                    )
        return copies

    first = basis_copies(0)
    second = basis_copies(1)
    for copy in first + second:
        copy.start()

    rates = [
        (freqs // 2 + freq * freq_local + f).astype(jnp.float32) * (UNIT / freqs)
        for f in range(freq_local)
    ]
    unit = make_unit(lat_ref, dep_ref, basis_v, green_s, rates, elements)

    def plan(u):
        way = 1 - 2 * lax.rem(u, 2)
        dist = half - (u + 2) // 4
        p = lax.rem((u + 1) // 2, 2)
        return way, lax.rem(freq + way * dist + n_freq, n_freq), p

    def ring_copy(u):
        way = 1 - 2 * lax.rem(u, 2)
        return pltpu.make_async_remote_copy(
            src_ref=send_b.at[u],
            dst_ref=recv_b.at[u],
            send_sem=ring_send.at[u],
            recv_sem=ring_recv.at[u],
            device_id=other(0, way),
            device_id_type=MESH,
        )

    for copy in first:
        copy.wait()
    for copy in second:
        copy.wait()

    @pl.loop(0, 2)
    def _(u):
        way, shard, p = plan(u)
        send_b[u] = unit(shard, p)

    pl.semaphore_wait(barrier, len(sideways) + n_pos - 1)

    ring_copy(0).start()
    ring_copy(1).start()

    halo_peers = [(dp, df) for dp in (-1, 0, 1) for df in (-1, 0, 1) if (dp, df) != (0, 0)]

    def halo_copy(i, dp, df):
        return pltpu.make_async_remote_copy(
            src_ref=halo_ref,
            dst_ref=halo_r.at[(1 - dp) * 3 + (1 - df)],
            send_sem=halo_send.at[i],
            recv_sem=halo_recv.at[(1 - dp) * 3 + (1 - df)],
            device_id=other(dp, df),
            device_id_type=MESH,
        )

    for i, (dp, df) in enumerate(halo_peers):
        halo_copy(i, dp, df).start()

    @pl.loop(2, messages + 2)
    def _(u):
        way, shard, p = plan(u)
        send_b[u] = unit(shard, p)

        @pl.when((u >= 4) & (u < messages))
        def _():
            ring_copy(u - 4).wait_recv()
            send_b[u] += recv_b[u - 4]

        @pl.when(u < messages)
        def _():
            ring_copy(u).start()

    for own, (right, left) in (
        (messages, (messages - 4, messages - 1)),
        (messages + 1, (messages - 2, messages - 3)),
    ):
        ring_copy(right).wait_recv()
        ring_copy(left).wait_recv()
        p = ((own + 1) // 2) % 2
        done = send_b[own] + recv_b[right] + recv_b[left]
        for e in range(rows // TH):
            final_b[p * (rows // TH) + e] = done[e * TH : (e + 1) * TH, :]

    for slot in range(n_pos * CAP):
        packed[slot] = final_b[slot_ref[slot]]

    def owner_copy(step):
        target = lax.rem(pos + step, n_pos)
        return pltpu.make_async_remote_copy(
            src_ref=packed.at[pl.ds(target * CAP, CAP)],
            dst_ref=arrived.at[pl.ds(pos * CAP, CAP)],
            send_sem=a2a_send.at[step],
            recv_sem=a2a_recv.at[step],
            device_id=(target, freq),
            device_id_type=MESH,
        )

    @pl.loop(1, n_pos)
    def _(step):
        owner_copy(step).start()

    mine = pl.ds(pos * CAP, CAP)
    own_copy = pltpu.make_async_copy(packed.at[mine], arrived.at[mine], own_sem)
    own_copy.start()

    cols = TILE_DEV * TW // n_freq
    for i, (dp, df) in enumerate(halo_peers):
        halo_copy(i, dp, df).wait_recv()
    lane16 = lax.broadcasted_iota(jnp.int32, (16, 128), 1)
    row16 = lax.broadcasted_iota(jnp.int32, (16, 128), 0)
    strips = []
    for dp in (-1, 0, 1):
        left = halo_r[(dp + 1) * 3]
        centre = halo_ref[...] if dp == 0 else halo_r[(dp + 1) * 3 + 1]
        right = halo_r[(dp + 1) * 3 + 2]
        strip = jnp.where(
            lane16 < PASSES,
            pltpu.roll(left, 128 - cols + PASSES, 1),
            jnp.where(
                lane16 < cols + PASSES,
                pltpu.roll(centre, PASSES, 1),
                pltpu.roll(right, cols + PASSES, 1),
            ),
        )
        strips.append(strip)
    grid_row = row16 + TH * (pos - 1)
    grid_col = lane16 + (cols * freq - PASSES)
    inside = (grid_row >= 0) & (grid_row < TH * n_pos) & (grid_col >= 0) & (grid_col < TILE_DEV * TW)
    inside = inside & (row16 < 3 * TH) & (lane16 < cols + 2 * PASSES)

    def widened(a):
        pieces = [strip[a * TH : (a + 1) * TH, :] for strip in strips]
        tall = jnp.concatenate(pieces + [pieces[0]], axis=0)
        return jnp.where(inside, tall, 0.0)

    across_k = widened(0)
    along_k = widened(1)
    ground = widened(2)
    south_k = jnp.minimum(across_k, pltpu.roll(across_k, 15, 0))
    north_k = jnp.minimum(across_k, pltpu.roll(across_k, 1, 0))
    east_k = jnp.minimum(along_k, pltpu.roll(along_k, 127, 1))
    west_k = jnp.minimum(along_k, pltpu.roll(along_k, 1, 1))

    slots = n_pos * CAP * TH
    place = (lax.broadcasted_iota(jnp.int32, (TH * TILE_DEV, slots), 0) == inc_ref[0:1, :]).astype(
        jnp.float32
    ).astype(jnp.bfloat16)

    @pl.loop(1, n_pos)
    def _(step):
        owner_copy(step).wait_recv()

    own_copy.wait()

    compound = None
    for piece in split3(arrived[...].reshape(slots, arrived.shape[2])):
        part = jnp.dot(place, piece, preferred_element_type=jnp.float32)
        compound = part if compound is None else compound + part
    rank = compound.shape[1]
    scaled = compound * compound * weight_ref[0:1, :]
    energy = lax.dot_general(
        jnp.ones((8, rank), jnp.float32),
        scaled,
        (((1,), (1,)), ((), ())),
        precision=lax.Precision.HIGHEST,
        preferred_element_type=jnp.float32,
    )
    value_b[...] = jnp.sqrt(energy / rank + EPS)

    def value_copy(i, dp, df):
        return pltpu.make_async_remote_copy(
            src_ref=value_b,
            dst_ref=value_r.at[(1 - dp) * n_freq + freq],
            send_sem=val_send.at[i],
            recv_sem=val_recv.at[i],
            device_id=other(dp, df),
            device_id_type=MESH,
        )

    for i, (dp, df) in enumerate(near):
        value_copy(i, dp, df).start()

    value_r[n_freq + freq] = value_b[...]

    from_r = lax.broadcasted_iota(jnp.int32, (128, TH * 128), 0)
    to_n = lax.broadcasted_iota(jnp.int32, (128, TH * 128), 1)
    to_col = to_n % 128 + (cols * freq - PASSES) + TW
    chosen = (from_r // TILE_DEV == to_n // 128) & (from_r % TILE_DEV == to_col // TW - 1)
    spread = chosen.astype(jnp.float32).astype(jnp.bfloat16)
    sub24 = lax.broadcasted_iota(jnp.int32, (3 * TW, TH * 128), 0)
    col24 = lax.broadcasted_iota(jnp.int32, (3 * TW, TH * 128), 1)
    keep = (col24 % 128 + (cols * freq - PASSES) + TW) % TW == sub24 % TW
    sub8 = lax.broadcasted_iota(jnp.int32, (TW, 128), 0)

    for i, (dp, df) in enumerate(near):
        value_copy(i, dp, df).wait_recv()

    groups = []
    for o in range(3):
        group = value_r[o * n_freq]
        for col in range(1, n_freq):
            group = jnp.where(sub8 == col, value_r[o * n_freq + col], group)
        groups.append(group)
    stacked = jnp.concatenate(groups, axis=0)
    wide = None
    for piece in split3(stacked):
        part = jnp.dot(piece, spread, preferred_element_type=jnp.float32)
        wide = part if wide is None else wide + part
    wide = jnp.where(keep, wide, 0.0)
    field = jnp.zeros((16, 128), jnp.float32)
    for o in range(3):
        summed = jnp.sum(wide[o * TW : (o + 1) * TW, :], axis=0, keepdims=True)
        for r in range(TH):
            field = jnp.where(row16 == o * TH + r, summed[:, r * 128 : (r + 1) * 128], field)
    u = jnp.where(inside, field + ground, 0.0)
    for sweep in range(PASSES):
        north = north_k * (pltpu.roll(u, 1, 0) - u)
        south = south_k * (pltpu.roll(u, 15, 0) - u)
        west = west_k * (pltpu.roll(u, 1, 1) - u)
        east = east_k * (pltpu.roll(u, 127, 1) - u)
        u = u + north + south + west + east
    u = pltpu.roll(u, 128 - PASSES, 1)
    out_ref[...] = u[TH : 2 * TH, :cols]

    @pl.loop(0, messages)
    def _(u):
        ring_copy(u).wait_send()

    @pl.loop(1, n_pos)
    def _(step):
        owner_copy(step).wait_send()

    for i, (dp, df) in enumerate(halo_peers):
        halo_copy(i, dp, df).wait_send()
    for i, (dp, df) in enumerate(near):
        value_copy(i, dp, df).wait_send()


def body(footprint, basis, weights, conduct, baseline):
    pos_local, freq_local, doubled, rank = basis.shape
    elements = doubled // 2
    foot = footprint.shape[1]
    n_pos = lax.axis_size("pos")
    n_freq = lax.axis_size("freq")
    positions = pos_local * n_pos
    my_pos = lax.axis_index("pos")
    rows = foot * TH
    entries = pos_local * foot
    blocks = footprint.reshape(n_pos, entries)
    my_ids = lax.dynamic_slice_in_dim(footprint, my_pos * pos_local, pos_local, 0)

    depth = TOP + CELL * ((my_ids // TILE_DEV)[:, :, None] * TH + jnp.arange(TH)[None, None, :])
    centre = (my_pos * pos_local + jnp.arange(pos_local)) * (CELL * TW * TILE_DEV // positions)
    lateral = CELL * TW * (my_ids % TILE_DEV) - centre[:, None]
    lateral = jnp.broadcast_to(lateral[:, :, None], depth.shape).reshape(pos_local, rows, 1)
    lat = (lateral - PITCH * jnp.arange(128)[None, None, :]).astype(jnp.float32)
    depth = depth.reshape(pos_local, rows, 1).astype(jnp.float32)
    dep = jnp.broadcast_to(depth * depth, lat.shape)

    flat = my_ids.reshape(entries)
    owner = flat // TILE_DEV
    earlier = jnp.arange(entries)[None, :] < jnp.arange(entries)[:, None]
    order = jnp.sum(((owner[:, None] == owner[None, :]) & earlier).astype(jnp.int32), axis=1)
    slot_of = owner * CAP + order
    slots = jnp.arange(n_pos * CAP)
    slot = jnp.sum(
        jnp.where(slots[:, None] == slot_of[None, :], jnp.arange(entries)[None, :], 0), axis=1
    ).astype(jnp.int32)
    mine = blocks // TILE_DEV == my_pos
    rank_in = jnp.dot(
        mine.astype(jnp.bfloat16),
        earlier.T.astype(jnp.bfloat16),
        preferred_element_type=jnp.float32,
    ).astype(jnp.int32)
    hit = mine[:, None, :] & (rank_in[:, None, :] == jnp.arange(CAP)[None, :, None])
    tile = jnp.max(jnp.where(hit, (blocks % TILE_DEV)[:, None, :], -1), axis=2)
    inc = jnp.where(
        tile[:, :, None] >= 0, tile[:, :, None] + TILE_DEV * jnp.arange(TH)[None, None, :], -1
    ).reshape(1, n_pos * CAP * TH)

    cols = baseline.shape[1]
    halo = jnp.concatenate([conduct.reshape(2 * TH, cols), baseline], axis=0)
    halo = jnp.pad(halo, ((0, 4), (0, 128 - cols)))

    messages = 2 * n_freq - 2
    near = 3 * n_freq - 1
    vmem = pl.BlockSpec(memory_space=pltpu.VMEM)
    return pl.pallas_call(
        functools.partial(kernel, n_pos, n_freq),
        out_shape=jax.ShapeDtypeStruct(baseline.shape, jnp.float32),
        in_specs=[pl.BlockSpec(memory_space=pltpu.SMEM)]
        + [vmem] * 5
        + [pl.BlockSpec(memory_space=pltpu.MemorySpace.HBM)],
        out_specs=vmem,
        scratch_shapes=[
            pltpu.VMEM((pos_local, elements // CHUNK, 2 * freq_local * CHUNK, rank), jnp.bfloat16),
            pltpu.VMEM((elements // CHUNK, rows, 2 * freq_local * CHUNK), jnp.bfloat16),
            pltpu.VMEM((messages + 2, rows, rank), jnp.float32),
            pltpu.VMEM((messages, rows, rank), jnp.float32),
            pltpu.VMEM((entries, TH, rank), jnp.float32),
            pltpu.VMEM((n_pos * CAP, TH, rank), jnp.float32),
            pltpu.VMEM((n_pos * CAP, TH, rank), jnp.float32),
            pltpu.VMEM((8, 128), jnp.float32),
            pltpu.VMEM((3 * n_freq, 8, 128), jnp.float32),
            pltpu.VMEM((9, 16, 128), jnp.float32),
            pltpu.SemaphoreType.DMA((pos_local, elements // CHUNK * freq_local * 2)),
            pltpu.SemaphoreType.DMA((messages,)),
            pltpu.SemaphoreType.DMA((messages,)),
            pltpu.SemaphoreType.DMA,
            pltpu.SemaphoreType.DMA((n_pos,)),
            pltpu.SemaphoreType.DMA((n_pos,)),
            pltpu.SemaphoreType.DMA((near,)),
            pltpu.SemaphoreType.DMA((near,)),
            pltpu.SemaphoreType.DMA((8,)),
            pltpu.SemaphoreType.DMA((9,)),
        ],
        compiler_params=pltpu.CompilerParams(
            collective_id=0, has_side_effects=True, vmem_limit_bytes=48 * 1024 * 1024
        ),
    )(slot, lat, dep, inc, weights.reshape(1, rank), halo, basis)


def solution(mesh):
    return jax.shard_map(
        body,
        mesh=mesh,
        in_specs=(P(), P("pos", "freq", None, None), P(), P(None, "pos", "freq"), P("pos", "freq")),
        out_specs=P("pos", "freq"),
        check_vma=False,
    )
```

```python
import functools

import jax
import jax.numpy as jnp
from jax import lax
from jax.experimental import pallas as pl
from jax.experimental.pallas import tpu as pltpu
from jax.sharding import PartitionSpec as P

TH = 4
TW = 8
CELLS = TH * TW
TILE_DEV = 32
PASSES = 3
CAP = 4
EPS = 1e-06
MESH = pl.DeviceIdType.MESH

UNIT = 0.025
CELL = 28
PITCH = 5
TOP = 160
SIN_POLY = (-4.547240826688576, 9.23637803174852, -5.615372827081364)
SCALE_SQ = 0.6259964781564749
DOUBLE = (2.0 + 1e-6) / SCALE_SQ
LANES = 128


def green_block(cross, depth_sq, turns):
    square = cross * cross + depth_sq
    dist = square * lax.rsqrt(square)
    root = lax.rsqrt(dist)
    amp = root * (TOP**0.5)
    scaled_amp = root * (TOP**0.5 * SCALE_SQ)
    out = []
    for rate in turns:
        phase = dist * rate
        x = jnp.round(phase) - phase
        z = x * x
        s = x * (((z + SIN_POLY[0]) * z + SIN_POLY[1]) * z + SIN_POLY[2])
        w = DOUBLE - s * s
        u = w * scaled_amp
        out.append(((u - amp).astype(jnp.bfloat16), (u * s * lax.rsqrt(w)).astype(jnp.bfloat16)))
    return out


def make_unit(lat_ref, dep_ref, basis_v, green_s, rates, elements):
    rows = lat_ref.shape[1]

    def unit(col, p):
        total = None
        for tile in range(elements // LANES):
            start = tile * LANES
            shift = (2 * CELL * col + (PITCH * (elements - 1) - 2 * PITCH * start)).astype(jnp.float32) * 0.5
            for rg in range(rows // 16):
                span = pl.ds(rg * 16, 16)
                values = green_block(lat_ref[p, span, :] + shift, dep_ref[p, span, :], rates)
                for f, (cosine, sine) in enumerate(values):
                    green_s[tile, f, span, 0:LANES] = cosine
                    green_s[tile, f, span, LANES : 2 * LANES] = sine
            for f in range(len(rates)):
                right = jnp.concatenate(
                    [
                        basis_v[p, f, start : start + LANES, :],
                        basis_v[p, f, elements + start : elements + start + LANES, :],
                    ],
                    axis=0,
                )
                part = jnp.dot(green_s[tile, f], right, preferred_element_type=jnp.float32)
                total = part if total is None else total + part
        return total

    return unit


def split3(x):
    hi = x.astype(jnp.bfloat16)
    rest = x - hi.astype(jnp.float32)
    mid = rest.astype(jnp.bfloat16)
    low = (rest - mid.astype(jnp.float32)).astype(jnp.bfloat16)
    return hi, mid, low


def kernel(
    n_pos,
    n_freq,
    foot_ref,
    weight_ref,
    conduct_ref,
    base_ref,
    basis_ref,
    out_ref,
    foot_v,
    weight_v,
    conduct_v,
    base_v,
    lat_v,
    dep_v,
    basis_v,
    green_s,
    send_b,
    recv_b,
    final_b,
    packed,
    arrived,
    value_b,
    value_r,
    halo_b,
    halo_r,
    slot_v,
    slot_s,
    in_sem,
    basis_sem,
    ring_send,
    ring_recv,
    own_sem,
    a2a_send,
    a2a_recv,
    val_send,
    val_recv,
    halo_send,
    halo_recv,
):
    pos = lax.axis_index("pos")
    freq = lax.axis_index("freq")
    pos_local, freq_local, doubled, rank = basis_ref.shape
    elements = doubled // 2
    freqs = freq_local * n_freq
    foot = foot_v.shape[0]
    rows = foot * TH
    entries = pos_local * foot
    half = n_freq // 2
    messages = 4 * half - 2
    iota = lax.broadcasted_iota

    loads = [
        pltpu.make_async_copy(src, dst, in_sem.at[i])
        for i, (src, dst) in enumerate(
            ((foot_ref, foot_v), (conduct_ref, conduct_v), (base_ref, base_v), (weight_ref, weight_v))
        )
    ]
    basis_loads = [
        pltpu.make_async_copy(basis_ref.at[p], basis_v.at[p], basis_sem.at[p]) for p in range(pos_local)
    ]
    loads[0].start()
    for copy in basis_loads:
        copy.start()
    for copy in loads[1:]:
        copy.start()

    def other(dp, df):
        return (lax.rem(pos + dp + n_pos, n_pos), lax.rem(freq + df + n_freq, n_freq))

    barrier = pltpu.get_barrier_semaphore()
    near = [(dp, df) for dp in (-1, 0, 1) for df in range(n_freq) if (dp, df) != (0, 0)]
    sideways = [(dp, df) for dp, df in near if df != 0]

    @pl.loop(1, n_pos)
    def _(step):
        pl.semaphore_signal(barrier, inc=1, device_id=other(step, 0), device_id_type=MESH)

    for dp, df in sideways:
        pl.semaphore_signal(barrier, inc=1, device_id=other(dp, df), device_id_type=MESH)

    loads[0].wait()
    positions = pos_local * n_pos
    expand = iota(jnp.int32, (rows, foot), 0) // TH == iota(jnp.int32, (rows, foot), 1)
    expand = jnp.where(expand, 1.0, 0.0).astype(jnp.bfloat16)
    foot_all = foot_v[...]
    owner_of = jnp.dot(
        expand,
        (foot_all // TILE_DEV).astype(jnp.float32).astype(jnp.bfloat16),
        preferred_element_type=jnp.float32,
    )
    local_of = jnp.dot(
        expand,
        (foot_all % TILE_DEV).astype(jnp.float32).astype(jnp.bfloat16),
        preferred_element_type=jnp.float32,
    )
    corner = iota(jnp.int32, (rows, 1), 0) % TH
    which = iota(jnp.int32, (rows, positions), 1)
    for p in range(pos_local):
        position = pos * pos_local + p
        owner = jnp.sum(jnp.where(which == position, owner_of, 0.0), axis=1, keepdims=True)
        local = jnp.sum(jnp.where(which == position, local_of, 0.0), axis=1, keepdims=True)
        depth = (TOP + CELL * (owner.astype(jnp.int32) * TH + corner)).astype(jnp.float32)
        centre = position * (CELL * TW * TILE_DEV // positions)
        lateral = CELL * TW * local.astype(jnp.int32) - centre
        lat_v[p] = (lateral - PITCH * iota(jnp.int32, (rows, LANES), 1)).astype(jnp.float32)
        dep_v[p] = jnp.broadcast_to(depth * depth, (rows, LANES))

    rates = [
        (freqs // 2 + freq * freq_local + f).astype(jnp.float32) * (UNIT / freqs)
        for f in range(freq_local)
    ]
    unit = make_unit(lat_v, dep_v, basis_v, green_s, rates, elements)

    def plan(u):
        way = 1 - 2 * lax.rem(u, 2)
        dist = half - (u + 2) // 4
        p = lax.rem((u + 1) // 2, 2)
        return way, lax.rem(freq + way * dist + n_freq, n_freq), p

    def compute(u):
        way, shard, p = plan(u)
        done = unit(shard, p)
        for h in range(2):
            send_b[u, h] = done[:, h * LANES : (h + 1) * LANES]

    def ring_copy(u):
        return pltpu.make_async_remote_copy(
            src_ref=send_b.at[u],
            dst_ref=recv_b.at[u],
            send_sem=ring_send.at[u, 0],
            recv_sem=ring_recv.at[u, 0],
            device_id=other(0, 1 - 2 * lax.rem(u, 2)),
            device_id_type=MESH,
        )

    def ring_half(u, h):
        return pltpu.make_async_remote_copy(
            src_ref=send_b.at[u, h],
            dst_ref=recv_b.at[u, h],
            send_sem=ring_send.at[u, h],
            recv_sem=ring_recv.at[u, h],
            device_id=other(0, 1 - 2 * lax.rem(u, 2)),
            device_id_type=MESH,
        )

    @pl.loop(0, 2)
    def _(u):
        @pl.when(u == 0)
        def _():
            basis_loads[0].wait()

        @pl.when(u == 1)
        def _():
            basis_loads[1].wait()

        compute(u)

    for copy in loads[1:]:
        copy.wait()
    cols = base_v.shape[1]
    halo_b[...] = jnp.zeros(halo_b.shape, jnp.float32)
    halo_b[0:TH, 0:cols] = conduct_v[0]
    halo_b[TH : 2 * TH, 0:cols] = conduct_v[1]
    halo_b[2 * TH : 3 * TH, 0:cols] = base_v[...]

    pl.semaphore_wait(barrier, len(sideways) + n_pos - 1)

    ring_copy(0).start()
    ring_copy(1).start()

    halo_peers = [(dp, df) for dp in (-1, 0, 1) for df in (-1, 0, 1) if (dp, df) != (0, 0)]

    def halo_copy(i, dp, df):
        return pltpu.make_async_remote_copy(
            src_ref=halo_b,
            dst_ref=halo_r.at[(1 - dp) * 3 + (1 - df)],
            send_sem=halo_send.at[i],
            recv_sem=halo_recv.at[(1 - dp) * 3 + (1 - df)],
            device_id=other(dp, df),
            device_id_type=MESH,
        )

    @pl.loop(2, messages + 2)
    def _(u):
        compute(u)

        @pl.when((u >= 4) & (u < messages))
        def _():
            ring_copy(u - 4).wait_recv()
            send_b[u] += recv_b[u - 4]

        @pl.when(u < messages - 4)
        def _():
            ring_copy(u).start()

        @pl.when((u >= messages - 4) & (u < messages))
        def _():
            ring_half(u, 0).start()

        @pl.when(u == messages - 1)
        def _():
            for back in range(4):
                ring_half(messages - 4 + back, 1).start()

        @pl.when(u == 2)
        def _():
            for i, (dp, df) in enumerate(halo_peers):
                halo_copy(i, dp, df).start()

    foot_f = foot_all.astype(jnp.float32)
    which = iota(jnp.int32, (foot, positions), 1)
    flat_col = jnp.concatenate(
        [
            jnp.sum(jnp.where(which == pos * pos_local + p, foot_f, 0.0), axis=1, keepdims=True)
            for p in range(pos_local)
        ],
        axis=0,
    )
    to_self = iota(jnp.int32, (entries, entries), 0) == iota(jnp.int32, (entries, entries), 1)
    flat_row = jnp.sum(jnp.where(to_self, flat_col, 0.0), axis=0, keepdims=True)
    owner_row = flat_row.astype(jnp.int32) // TILE_DEV
    owner_col = flat_col.astype(jnp.int32) // TILE_DEV
    earlier = iota(jnp.int32, (entries, entries), 1) < iota(jnp.int32, (entries, entries), 0)
    order = jnp.sum(
        jnp.where((owner_row == owner_col) & earlier, 1.0, 0.0), axis=1, keepdims=True
    ).astype(jnp.int32)
    slot_of = owner_col * CAP + order
    all_slots = n_pos * CAP
    here = slot_of == iota(jnp.int32, (entries, all_slots), 1)
    entry = iota(jnp.int32, (entries, all_slots), 0).astype(jnp.float32)
    slot_v[...] = jnp.sum(jnp.where(here, entry, 0.0), axis=0, keepdims=True).astype(jnp.int32)
    slot_load = pltpu.make_async_copy(slot_v, slot_s, own_sem.at[2])
    slot_load.start()

    spans = n_pos * CAP * TH
    mine = foot_all // TILE_DEV == pos
    mine_b = jnp.where(mine, 1.0, 0.0).astype(jnp.bfloat16)
    lower = iota(jnp.int32, (foot, foot), 1) < iota(jnp.int32, (foot, foot), 0)
    from_p = iota(jnp.int32, (positions, positions), 0)
    to_p = iota(jnp.int32, (positions, positions), 1)
    later = (from_p // pos_local == to_p // pos_local) & (from_p < to_p)
    moved = jnp.dot(
        mine_b, jnp.where(later, 1.0, 0.0).astype(jnp.bfloat16), preferred_element_type=jnp.float32
    )
    ahead = jnp.dot(
        jnp.where(lower, 1.0, 0.0).astype(jnp.bfloat16), mine_b, preferred_element_type=jnp.float32
    ) + jnp.sum(moved, axis=0, keepdims=True)
    local = (foot_all % TILE_DEV + 1).astype(jnp.float32)
    found = jnp.concatenate(
        [
            jnp.sum(jnp.where(mine & (ahead == s), local, 0.0), axis=0, keepdims=True)
            for s in range(CAP)
        ],
        axis=0,
    )
    block_of = iota(jnp.int32, (positions, spans), 0) // pos_local
    block_to = iota(jnp.int32, (positions, spans), 1) // (TH * CAP)
    table = jnp.dot(
        found.astype(jnp.bfloat16),
        jnp.where(block_of == block_to, 1.0, 0.0).astype(jnp.bfloat16),
        preferred_element_type=jnp.float32,
    )
    turn = iota(jnp.int32, (CAP, spans), 1) // TH % CAP == iota(jnp.int32, (CAP, spans), 0)
    tile_in = jnp.sum(jnp.where(turn, table, 0.0), axis=0, keepdims=True).astype(jnp.int32)
    corner_in = iota(jnp.int32, (1, spans), 1) % TH
    target_row = jnp.where(tile_in > 0, tile_in - 1 + TILE_DEV * corner_in, -1)
    place = jnp.where(iota(jnp.int32, (TH * TILE_DEV, spans), 0) == target_row, 1.0, 0.0)
    place = place.astype(jnp.bfloat16)

    for i, (dp, df) in enumerate(halo_peers):
        halo_copy(i, dp, df).wait_recv()
    lane16 = iota(jnp.int32, (16, LANES), 1)
    row16 = iota(jnp.int32, (16, LANES), 0)
    strips = []
    for dp in (-1, 0, 1):
        left = halo_r[(dp + 1) * 3]
        centre = halo_b[...] if dp == 0 else halo_r[(dp + 1) * 3 + 1]
        right = halo_r[(dp + 1) * 3 + 2]
        strip = jnp.where(
            lane16 < PASSES,
            pltpu.roll(left, LANES - cols + PASSES, 1),
            jnp.where(
                lane16 < cols + PASSES,
                pltpu.roll(centre, PASSES, 1),
                pltpu.roll(right, cols + PASSES, 1),
            ),
        )
        strips.append(strip)
    grid_row = row16 + TH * (pos - 1)
    grid_col = lane16 + (cols * freq - PASSES)
    inside = (grid_row >= 0) & (grid_row < TH * n_pos) & (grid_col >= 0) & (grid_col < TILE_DEV * TW)
    inside = inside & (row16 < 3 * TH) & (lane16 < cols + 2 * PASSES)

    def widened(a):
        pieces = [strip[a * TH : (a + 1) * TH, :] for strip in strips]
        tall = jnp.concatenate(pieces + [pieces[0]], axis=0)
        return jnp.where(inside, tall, 0.0)

    across_k = widened(0)
    along_k = widened(1)
    ground = widened(2)
    south_k = jnp.minimum(across_k, pltpu.roll(across_k, 15, 0))
    north_k = jnp.minimum(across_k, pltpu.roll(across_k, 1, 0))
    east_k = jnp.minimum(along_k, pltpu.roll(along_k, LANES - 1, 1))
    west_k = jnp.minimum(along_k, pltpu.roll(along_k, 1, 1))

    slot_load.wait()

    def owner_copy(step, h):
        target = lax.rem(pos + step, n_pos)
        return pltpu.make_async_remote_copy(
            src_ref=packed.at[h, pl.ds(target * CAP, CAP)],
            dst_ref=arrived.at[h, pl.ds(pos * CAP, CAP)],
            send_sem=a2a_send.at[h, step],
            recv_sem=a2a_recv.at[h, step],
            device_id=(target, freq),
            device_id_type=MESH,
        )

    own_block = pl.ds(pos * CAP, CAP)
    own_copies = []
    for h in range(2):
        for own, (right, left) in (
            (messages, (messages - 4, messages - 1)),
            (messages + 1, (messages - 2, messages - 3)),
        ):
            ring_half(right, h).wait_recv()
            ring_half(left, h).wait_recv()
            p = ((own + 1) // 2) % 2
            done = send_b[own, h] + recv_b[right, h] + recv_b[left, h]
            for e in range(foot):
                final_b[h, p * foot + e] = done[e * TH : (e + 1) * TH, :]
        for slot in range(all_slots):
            packed[h, slot] = final_b[h, jnp.clip(slot_s[0, slot], 0, entries - 1)]

        @pl.loop(1, n_pos)
        def _(step):
            owner_copy(step, h).start()

        own_copy = pltpu.make_async_copy(
            packed.at[h, own_block], arrived.at[h, own_block], own_sem.at[h]
        )
        own_copy.start()
        own_copies.append(own_copy)

    compounds = []
    for h in range(2):

        @pl.loop(1, n_pos)
        def _(step):
            owner_copy(step, h).wait_recv()

        own_copies[h].wait()
        compound = None
        for piece in split3(arrived[h].reshape(spans, LANES)):
            part = jnp.dot(place, piece, preferred_element_type=jnp.float32)
            compound = part if compound is None else compound + part
        compounds.append(compound)
    compound = jnp.concatenate(compounds, axis=1)
    scaled = compound * compound * weight_v[...]
    energy = lax.dot_general(
        jnp.ones((8, rank), jnp.float32),
        scaled,
        (((1,), (1,)), ((), ())),
        precision=lax.Precision.HIGHEST,
        preferred_element_type=jnp.float32,
    )
    value_b[...] = jnp.sqrt(energy / rank + EPS)

    def value_copy(i, dp, df):
        return pltpu.make_async_remote_copy(
            src_ref=value_b,
            dst_ref=value_r.at[(1 - dp) * n_freq + freq],
            send_sem=val_send.at[i],
            recv_sem=val_recv.at[i],
            device_id=other(dp, df),
            device_id_type=MESH,
        )

    for i, (dp, df) in enumerate(near):
        value_copy(i, dp, df).start()

    value_r[n_freq + freq] = value_b[...]

    from_r = iota(jnp.int32, (LANES, TH * LANES), 0)
    to_n = iota(jnp.int32, (LANES, TH * LANES), 1)
    to_col = to_n % LANES + (cols * freq - PASSES) + TW
    chosen = (from_r // TILE_DEV == to_n // LANES) & (from_r % TILE_DEV == to_col // TW - 1)
    spread = jnp.where(chosen, 1.0, 0.0).astype(jnp.bfloat16)
    sub24 = iota(jnp.int32, (3 * TW, TH * LANES), 0)
    col24 = iota(jnp.int32, (3 * TW, TH * LANES), 1)
    keep = (col24 % LANES + (cols * freq - PASSES) + TW) % TW == sub24 % TW
    sub8 = iota(jnp.int32, (TW, LANES), 0)

    for i, (dp, df) in enumerate(near):
        value_copy(i, dp, df).wait_recv()

    groups = []
    for o in range(3):
        group = value_r[o * n_freq]
        for col in range(1, n_freq):
            group = jnp.where(sub8 == col, value_r[o * n_freq + col], group)
        groups.append(group)
    stacked = jnp.concatenate(groups, axis=0)
    wide = None
    for piece in split3(stacked):
        part = jnp.dot(piece, spread, preferred_element_type=jnp.float32)
        wide = part if wide is None else wide + part
    wide = jnp.where(keep, wide, 0.0)
    field = jnp.zeros((16, LANES), jnp.float32)
    for o in range(3):
        summed = jnp.sum(wide[o * TW : (o + 1) * TW, :], axis=0, keepdims=True)
        for r in range(TH):
            field = jnp.where(row16 == o * TH + r, summed[:, r * LANES : (r + 1) * LANES], field)
    u = jnp.where(inside, field + ground, 0.0)
    for sweep in range(PASSES):
        north = north_k * (pltpu.roll(u, 1, 0) - u)
        south = south_k * (pltpu.roll(u, 15, 0) - u)
        west = west_k * (pltpu.roll(u, 1, 1) - u)
        east = east_k * (pltpu.roll(u, LANES - 1, 1) - u)
        u = u + north + south + west + east
    u = pltpu.roll(u, LANES - PASSES, 1)
    out_ref[...] = u[TH : 2 * TH, :cols]

    @pl.loop(0, messages - 4)
    def _(u):
        ring_copy(u).wait_send()

    for h in range(2):

        @pl.loop(messages - 4, messages)
        def _(u):
            ring_half(u, h).wait_send()

        @pl.loop(1, n_pos)
        def _(step):
            owner_copy(step, h).wait_send()

    for i, (dp, df) in enumerate(halo_peers):
        halo_copy(i, dp, df).wait_send()
    for i, (dp, df) in enumerate(near):
        value_copy(i, dp, df).wait_send()


def body(footprint, basis, weights, conduct, baseline):
    pos_local, freq_local, doubled, rank = basis.shape
    foot = footprint.shape[1]
    n_pos = lax.axis_size("pos")
    n_freq = lax.axis_size("freq")
    rows = foot * TH
    entries = pos_local * foot
    slots = n_pos * CAP
    messages = 2 * n_freq - 2
    near = 3 * n_freq - 1
    hbm = pl.BlockSpec(memory_space=pltpu.MemorySpace.HBM)
    f32, bf16 = jnp.float32, jnp.bfloat16
    return pl.pallas_call(
        functools.partial(kernel, n_pos, n_freq),
        out_shape=jax.ShapeDtypeStruct(baseline.shape, f32),
        in_specs=[hbm] * 5,
        out_specs=pl.BlockSpec(memory_space=pltpu.VMEM),
        scratch_shapes=[
            pltpu.VMEM(footprint.shape[::-1], jnp.int32),
            pltpu.VMEM((1, rank), f32),
            pltpu.VMEM(conduct.shape, f32),
            pltpu.VMEM(baseline.shape, f32),
            pltpu.VMEM((pos_local, rows, LANES), f32),
            pltpu.VMEM((pos_local, rows, LANES), f32),
            pltpu.VMEM(basis.shape, bf16),
            pltpu.VMEM((doubled // 2 // LANES, freq_local, rows, 2 * LANES), bf16),
            pltpu.VMEM((messages + 2, 2, rows, LANES), f32),
            pltpu.VMEM((messages, 2, rows, LANES), f32),
            pltpu.VMEM((2, entries, TH, LANES), f32),
            pltpu.VMEM((2, slots, TH, LANES), f32),
            pltpu.VMEM((2, slots, TH, LANES), f32),
            pltpu.VMEM((8, LANES), f32),
            pltpu.VMEM((3 * n_freq, 8, LANES), f32),
            pltpu.VMEM((16, LANES), f32),
            pltpu.VMEM((9, 16, LANES), f32),
            pltpu.VMEM((1, slots), jnp.int32),
            pltpu.SMEM((1, slots), jnp.int32),
            pltpu.SemaphoreType.DMA((4,)),
            pltpu.SemaphoreType.DMA((pos_local,)),
            pltpu.SemaphoreType.DMA((messages, 2)),
            pltpu.SemaphoreType.DMA((messages, 2)),
            pltpu.SemaphoreType.DMA((3,)),
            pltpu.SemaphoreType.DMA((2, n_pos)),
            pltpu.SemaphoreType.DMA((2, n_pos)),
            pltpu.SemaphoreType.DMA((near,)),
            pltpu.SemaphoreType.DMA((near,)),
            pltpu.SemaphoreType.DMA((8,)),
            pltpu.SemaphoreType.DMA((9,)),
        ],
        compiler_params=pltpu.CompilerParams(
            collective_id=0, has_side_effects=True, vmem_limit_bytes=62 * 1024 * 1024
        ),
    )(footprint.T, weights.reshape(1, rank), conduct, baseline, basis)


def solution(mesh):
    return jax.shard_map(
        body,
        mesh=mesh,
        in_specs=(P(), P("pos", "freq", None, None), P(), P(None, "pos", "freq"), P("pos", "freq")),
        out_specs=P("pos", "freq"),
        check_vma=False,
    )
```

```python
import functools

import jax
import jax.numpy as jnp
from jax import lax
from jax.experimental import pallas as pl
from jax.experimental.pallas import tpu as pltpu
from jax.sharding import PartitionSpec as P

TH = 4
TW = 8
CELLS = TH * TW
TILE_DEV = 32
PASSES = 3
CAP = 4
EPS = 1e-06
MESH = pl.DeviceIdType.MESH

UNIT = 0.025
CELL = 28
PITCH = 5
TOP = 160
SIN_POLY = (-4.547240826688576, 9.23637803174852, -5.615372827081364)
SCALE_SQ = 0.6259964781564749
DOUBLE = (2.0 + 1e-6) / SCALE_SQ
LANES = 128


def green_block(cross, depth_sq, turns):
    square = cross * cross + depth_sq
    dist = square * lax.rsqrt(square)
    root = lax.rsqrt(dist)
    amp = root * (TOP**0.5)
    scaled_amp = root * (TOP**0.5 * SCALE_SQ)
    out = []
    for rate in turns:
        phase = dist * rate
        x = jnp.round(phase) - phase
        z = x * x
        s = x * (((z + SIN_POLY[0]) * z + SIN_POLY[1]) * z + SIN_POLY[2])
        w = DOUBLE - s * s
        u = w * scaled_amp
        out.append(((u - amp).astype(jnp.bfloat16), (u * s * lax.rsqrt(w)).astype(jnp.bfloat16)))
    return out


def make_unit(lat_ref, dep_ref, basis_v, green_s, rates, elements):
    rows = lat_ref.shape[1]

    def unit(col, p):
        total = None
        for tile in range(elements // LANES):
            start = tile * LANES
            shift = (2 * CELL * col + (PITCH * (elements - 1) - 2 * PITCH * start)).astype(jnp.float32) * 0.5
            for rg in range(rows // 16):
                span = pl.ds(rg * 16, 16)
                values = green_block(lat_ref[p, span, :] + shift, dep_ref[p, span, :], rates)
                for f, (cosine, sine) in enumerate(values):
                    green_s[tile, f, span, 0:LANES] = cosine
                    green_s[tile, f, span, LANES : 2 * LANES] = sine
            for f in range(len(rates)):
                right = jnp.concatenate(
                    [
                        basis_v[p, f, start : start + LANES, :],
                        basis_v[p, f, elements + start : elements + start + LANES, :],
                    ],
                    axis=0,
                )
                part = jnp.dot(green_s[tile, f], right, preferred_element_type=jnp.float32)
                total = part if total is None else total + part
        return total

    return unit


def split3(x):
    hi = x.astype(jnp.bfloat16)
    rest = x - hi.astype(jnp.float32)
    mid = rest.astype(jnp.bfloat16)
    low = (rest - mid.astype(jnp.float32)).astype(jnp.bfloat16)
    return hi, mid, low


PARTS = 4


def digits_of(n_pos):
    return {32: (4, 4, 2), 8: (2, 2, 2)}[n_pos]


def displaced(pos, n_pos, k):
    target = 0
    below = n_pos
    for size in digits_of(n_pos):
        below = below // size
        digit = lax.rem(pos // below, size)
        turn = lax.rem(k // below, size)
        if size == 4:
            move = jnp.where(turn == 0, 2, jnp.where(turn == 1, 1, jnp.where(turn == 2, 3, 0)))
        else:
            move = size - 1 - turn
        target = target * size + lax.rem(digit + move, size)
    return target


def kernel(
    n_pos,
    n_freq,
    foot_ref,
    weight_ref,
    conduct_ref,
    base_ref,
    basis_ref,
    out_ref,
    lat_v,
    dep_v,
    basis_v,
    green_s,
    send_b,
    recv_b,
    packed,
    arrived,
    value_b,
    value_r,
    halo_b,
    halo_r,
    basis_sem,
    ring_send,
    ring_recv,
    own_sem,
    a2a_send,
    a2a_recv,
    val_send,
    val_recv,
    halo_send,
    halo_recv,
):
    pos = lax.axis_index("pos")
    freq = lax.axis_index("freq")
    pos_local, freq_local, doubled, rank = basis_ref.shape
    elements = doubled // 2
    freqs = freq_local * n_freq
    foot = foot_ref.shape[0]
    rows = foot * TH
    pair = rows // 2
    entries = pos_local * foot
    positions = pos_local * n_pos
    half = n_freq // 2
    messages = 4 * half - 2
    iota = lax.broadcasted_iota
    f32, bf16, i32 = jnp.float32, jnp.bfloat16, jnp.int32

    basis_loads = [
        [
            pltpu.make_async_copy(basis_ref.at[p, f], basis_v.at[p, f], basis_sem.at[p, f])
            for f in range(freq_local)
        ]
        for p in range(pos_local)
    ]
    for p in range(pos_local):
        for copy in basis_loads[p]:
            copy.start()

    def other(dp, df):
        return (lax.rem(pos + dp + n_pos, n_pos), lax.rem(freq + df + n_freq, n_freq))

    barrier = pltpu.get_barrier_semaphore()
    near = [(dp, df) for dp in (-1, 0, 1) for df in range(n_freq) if (dp, df) != (0, 0)]
    near.sort(key=lambda d: -min(d[1], n_freq - d[1]) - abs(d[0]) * 0.5)
    sideways = [(dp, df) for dp, df in near if df != 0]
    for dp, df in sideways:
        pl.semaphore_signal(barrier, inc=1, device_id=other(dp, df), device_id_type=MESH)

    @pl.loop(0, n_pos - 1)
    def _(k):
        pl.semaphore_signal(
            barrier, inc=1, device_id=(displaced(pos, n_pos, k), freq), device_id_type=MESH
        )

    expand = iota(i32, (rows, foot), 0) % foot == iota(i32, (rows, foot), 1)
    expand = jnp.where(expand, 1.0, 0.0).astype(bf16)
    foot_all = foot_ref[...]
    foot_owner = (foot_all // TILE_DEV).astype(f32)
    foot_local = (foot_all % TILE_DEV).astype(f32)
    owner_of = jnp.dot(expand, foot_owner.astype(bf16), preferred_element_type=f32)
    local_of = jnp.dot(expand, foot_local.astype(bf16), preferred_element_type=f32)
    corner = iota(i32, (rows, 1), 0) // foot
    which = iota(i32, (rows, positions), 1)

    def locate(p):
        position = pos * pos_local + p
        owner = jnp.sum(jnp.where(which == position, owner_of, 0.0), axis=1, keepdims=True)
        local = jnp.sum(jnp.where(which == position, local_of, 0.0), axis=1, keepdims=True)
        depth = (TOP + CELL * (owner.astype(i32) * TH + corner)).astype(f32)
        centre = position * (CELL * TW * TILE_DEV // positions)
        lateral = CELL * TW * local.astype(i32) - centre
        lat_v[p] = (lateral - PITCH * iota(i32, (rows, LANES), 1)).astype(f32)
        dep_v[p] = jnp.broadcast_to(depth * depth, (rows, LANES))

    locate(0)

    rates = [
        (freqs // 2 + freq * freq_local + f).astype(f32) * (UNIT / freqs) for f in range(freq_local)
    ]
    unit = make_unit(lat_v, dep_v, basis_v, green_s, rates, elements)

    def compute(u):
        way = 1 - 2 * lax.rem(u, 2)
        dist = half - (u + 2) // 4
        p = lax.rem((u + 1) // 2, 2)
        done = unit(lax.rem(freq + way * dist + n_freq, n_freq), p)
        for h in range(2):
            send_b[u, h] = done[:, h * LANES : (h + 1) * LANES]

    def ring_copy(u):
        return pltpu.make_async_remote_copy(
            src_ref=send_b.at[u],
            dst_ref=recv_b.at[u],
            send_sem=ring_send.at[u, 0],
            recv_sem=ring_recv.at[u, 0],
            device_id=other(0, 1 - 2 * lax.rem(u, 2)),
            device_id_type=MESH,
        )

    def ring_part(u, c):
        span = pl.ds((c % 2) * pair, pair)
        return pltpu.make_async_remote_copy(
            src_ref=send_b.at[u, c // 2, span, :],
            dst_ref=recv_b.at[u, c // 2, span, :],
            send_sem=ring_send.at[u, c],
            recv_sem=ring_recv.at[u, c],
            device_id=other(0, 1 - 2 * lax.rem(u, 2)),
            device_id_type=MESH,
        )

    for copy in basis_loads[0]:
        copy.wait()
    compute(jnp.int32(0))
    pl.semaphore_wait(barrier, len(sideways) + n_pos - 1)
    ring_copy(0).start()
    for p in range(1, pos_local):
        locate(p)

    cols = base_ref.shape[1]
    halo_b[...] = jnp.zeros(halo_b.shape, f32)
    halo_b[0:TH, 0:cols] = conduct_ref[0]
    halo_b[TH : 2 * TH, 0:cols] = conduct_ref[1]
    halo_b[2 * TH : 3 * TH, 0:cols] = base_ref[...]
    halo_peers = [(dp, df) for dp in (-1, 0, 1) for df in (-1, 0, 1) if (dp, df) != (0, 0)]

    def halo_copy(i, dp, df):
        return pltpu.make_async_remote_copy(
            src_ref=halo_b,
            dst_ref=halo_r.at[(1 - dp) * 3 + (1 - df)],
            send_sem=halo_send.at[i],
            recv_sem=halo_recv.at[(1 - dp) * 3 + (1 - df)],
            device_id=other(dp, df),
            device_id_type=MESH,
        )

    @pl.loop(1, messages + 2)
    def _(u):
        @pl.when(u == 1)
        def _():
            for p in range(1, pos_local):
                for copy in basis_loads[p]:
                    copy.wait()

        compute(u)

        @pl.when((u >= 4) & (u < messages))
        def _():
            ring_copy(u - 4).wait_recv()
            send_b[u] += recv_b[u - 4]

        @pl.when(u < messages - 4)
        def _():
            ring_copy(u).start()

        @pl.when((u >= messages - 4) & (u < messages))
        def _():
            ring_part(u, 0).start()
            ring_part(u, 1).start()

        @pl.when((u >= messages - 2) & (u < messages))
        def _():
            for c in range(2, PARTS):
                ring_part(u - 2, c).start()
                ring_part(u, c).start()

        @pl.when(u == 5)
        def _():
            for i, (dp, df) in enumerate(halo_peers):
                halo_copy(i, dp, df).start()

    outs = n_pos * CAP * 2
    width = pos_local * 2 * foot
    picks = iota(i32, (foot, positions), 1)
    owner_col = jnp.concatenate(
        [
            jnp.sum(jnp.where(picks == pos * pos_local + p, foot_owner, 0.0), axis=1, keepdims=True)
            for p in range(pos_local)
        ],
        axis=0,
    )
    lane = iota(i32, (entries, width), 1)
    entry_of_lane = lane // (2 * foot) * foot + lane % foot
    entry = iota(i32, (entries, width), 0)
    owner_row = jnp.sum(jnp.where(entry == entry_of_lane, owner_col, 0.0), axis=0, keepdims=True)
    same = (owner_col == owner_row) & (entry < entry_of_lane)
    order_row = jnp.sum(jnp.where(same, 1.0, 0.0), axis=0, keepdims=True)
    slot_row = owner_row * CAP + order_row
    to_row = iota(i32, (outs, width), 0)
    from_lane = iota(i32, (outs, width), 1)
    slot_out = (to_row // (2 * CAP) * CAP + to_row % CAP).astype(f32)
    gather = (slot_out == slot_row) & (to_row // CAP % 2 == from_lane // foot % 2)
    gather = jnp.where(gather, 1.0, 0.0).astype(bf16)
    gather = jnp.concatenate([gather] * 3, axis=1)

    mine = foot_owner == pos.astype(f32)
    mine_b = jnp.where(mine, 1.0, 0.0).astype(bf16)
    lower = iota(i32, (foot, foot), 1) < iota(i32, (foot, foot), 0)
    from_p = iota(i32, (positions, positions), 0)
    to_p = iota(i32, (positions, positions), 1)
    later = (from_p // pos_local == to_p // pos_local) & (from_p < to_p)
    moved = jnp.dot(mine_b, jnp.where(later, 1.0, 0.0).astype(bf16), preferred_element_type=f32)
    ahead = jnp.dot(
        jnp.where(lower, 1.0, 0.0).astype(bf16), mine_b, preferred_element_type=f32
    ) + jnp.sum(moved, axis=0, keepdims=True)
    found = jnp.concatenate(
        [
            jnp.sum(jnp.where(mine & (ahead == s), foot_local + 1.0, 0.0), axis=0, keepdims=True)
            for s in range(CAP)
        ],
        axis=0,
    )
    block_of = iota(i32, (positions, outs), 0) // pos_local
    block_to = iota(i32, (positions, outs), 1) // (2 * CAP)
    table = jnp.dot(
        found.astype(bf16),
        jnp.where(block_of == block_to, 1.0, 0.0).astype(bf16),
        preferred_element_type=f32,
    )
    turn = iota(i32, (CAP, outs), 1) % CAP == iota(i32, (CAP, outs), 0)
    tile_in = jnp.sum(jnp.where(turn, table, 0.0), axis=0, keepdims=True)
    row_in = iota(i32, (1, outs), 1) // CAP % 2
    target_row = jnp.where(tile_in > 0.0, tile_in - 1.0 + (TILE_DEV * row_in).astype(f32), -1.0)
    place = iota(i32, (2 * TILE_DEV, outs), 0).astype(f32) == target_row
    place = jnp.where(place, 1.0, 0.0).astype(bf16)
    place = jnp.concatenate([place] * 3, axis=1)

    for i, (dp, df) in enumerate(halo_peers):
        halo_copy(i, dp, df).wait_recv()
    lane16 = iota(i32, (16, LANES), 1)
    row16 = iota(i32, (16, LANES), 0)
    strips = []
    for dp in (-1, 0, 1):
        left = halo_r[(dp + 1) * 3]
        centre = halo_b[...] if dp == 0 else halo_r[(dp + 1) * 3 + 1]
        right = halo_r[(dp + 1) * 3 + 2]
        strip = jnp.where(
            lane16 < PASSES,
            pltpu.roll(left, LANES - cols + PASSES, 1),
            jnp.where(
                lane16 < cols + PASSES,
                pltpu.roll(centre, PASSES, 1),
                pltpu.roll(right, cols + PASSES, 1),
            ),
        )
        strips.append(strip)
    grid_row = row16 + TH * (pos - 1)
    grid_col = lane16 + (cols * freq - PASSES)
    inside = (grid_row >= 0) & (grid_row < TH * n_pos) & (grid_col >= 0) & (grid_col < TILE_DEV * TW)
    inside = inside & (row16 < 3 * TH) & (lane16 < cols + 2 * PASSES)

    def widened(a):
        pieces = [strip[a * TH : (a + 1) * TH, :] for strip in strips]
        tall = jnp.concatenate(pieces + [pieces[0]], axis=0)
        return jnp.where(inside, tall, 0.0)

    across_k = widened(0)
    along_k = widened(1)
    ground = widened(2)
    south_k = jnp.minimum(across_k, pltpu.roll(across_k, 15, 0))
    north_k = jnp.minimum(across_k, pltpu.roll(across_k, 1, 0))
    east_k = jnp.minimum(along_k, pltpu.roll(along_k, LANES - 1, 1))
    west_k = jnp.minimum(along_k, pltpu.roll(along_k, 1, 1))

    block = 2 * CAP

    def owner_copy(k, c):
        target = displaced(pos, n_pos, k)
        return pltpu.make_async_remote_copy(
            src_ref=packed.at[c, pl.ds(pl.multiple_of(target * block, block), block), :],
            dst_ref=arrived.at[c, pl.ds(pl.multiple_of(pos * block, block), block), :],
            send_sem=a2a_send.at[c, k],
            recv_sem=a2a_recv.at[c, k],
            device_id=(target, freq),
            device_id_type=MESH,
        )

    own_block = pl.ds(pl.multiple_of(pos * block, block), block)
    own_copies = []
    for c in range(PARTS):
        span = pl.ds((c % 2) * pair, pair)
        sums = []
        for own, right, left in (
            (messages + 1, messages - 2, messages - 3),
            (messages, messages - 4, messages - 1),
        ):
            ring_part(right, c).wait_recv()
            ring_part(left, c).wait_recv()
            sums.append(send_b[own, c // 2, span, :] + recv_b[right, c // 2, span, :] + recv_b[left, c // 2, span, :])
        stacked = jnp.concatenate(split3(jnp.concatenate(sums, axis=0)), axis=0)
        packed[c] = jnp.dot(gather, stacked, preferred_element_type=f32)

        @pl.loop(0, n_pos - 1)
        def _(k):
            owner_copy(k, c).start()

        own_copy = pltpu.make_async_copy(
            packed.at[c, own_block, :], arrived.at[c, own_block, :], own_sem.at[c]
        )
        own_copy.start()
        own_copies.append(own_copy)

    energies = [None, None]
    for c in range(PARTS):

        @pl.loop(0, n_pos - 1)
        def _(k):
            owner_copy(k, c).wait_recv()

        own_copies[c].wait()
        stacked = jnp.concatenate(split3(arrived[c]), axis=0)
        compound = jnp.dot(place, stacked, preferred_element_type=f32)
        scaled = compound * compound * weight_ref[0:1, (c // 2) * LANES : (c // 2 + 1) * LANES]
        energies[c % 2] = scaled if energies[c % 2] is None else energies[c % 2] + scaled
    value = jnp.zeros((1, LANES), f32)
    for pair_at, energy in enumerate(energies):
        energy = jnp.sum(energy, axis=1, keepdims=True)
        on = iota(i32, (2 * TILE_DEV, LANES), 1) == iota(i32, (2 * TILE_DEV, LANES), 0) + pair_at * 2 * TILE_DEV
        value = value + jnp.sum(jnp.where(on, energy, 0.0), axis=0, keepdims=True)
    value_b[...] = jnp.sqrt(value / rank + EPS)

    def value_copy(i, dp, df):
        return pltpu.make_async_remote_copy(
            src_ref=value_b,
            dst_ref=value_r.at[(1 - dp) * n_freq + freq],
            send_sem=val_send.at[i],
            recv_sem=val_recv.at[i],
            device_id=other(dp, df),
            device_id_type=MESH,
        )

    for i, (dp, df) in enumerate(near):
        value_copy(i, dp, df).start()

    value_r[n_freq + freq] = value_b[...]

    @pl.loop(0, messages - 4)
    def _(u):
        ring_copy(u).wait_send()

    for c in range(PARTS):

        @pl.loop(messages - 4, messages)
        def _(u):
            ring_part(u, c).wait_send()

        @pl.loop(0, n_pos - 1)
        def _(k):
            owner_copy(k, c).wait_send()

    for i, (dp, df) in enumerate(halo_peers):
        halo_copy(i, dp, df).wait_send()

    from_r = iota(i32, (LANES, TH * LANES), 0)
    to_n = iota(i32, (LANES, TH * LANES), 1)
    to_col = to_n % LANES + (cols * freq - PASSES) + TW
    chosen = (from_r // TILE_DEV == to_n // LANES) & (from_r % TILE_DEV == to_col // TW - 1)
    spread = jnp.where(chosen, 1.0, 0.0).astype(bf16)
    sub24 = iota(i32, (3 * TW, TH * LANES), 0)
    col24 = iota(i32, (3 * TW, TH * LANES), 1)
    keep = (col24 % LANES + (cols * freq - PASSES) + TW) % TW == sub24 % TW
    sub8 = iota(i32, (TW, LANES), 0)

    for i, (dp, df) in enumerate(near):
        value_copy(i, dp, df).wait_recv()

    groups = []
    for o in range(3):
        group = jnp.broadcast_to(value_r[o * n_freq], (TW, LANES))
        for col in range(1, n_freq):
            group = jnp.where(sub8 == col, value_r[o * n_freq + col], group)
        groups.append(group)
    wide = None
    for piece in split3(jnp.concatenate(groups, axis=0)):
        part = jnp.dot(piece, spread, preferred_element_type=f32)
        wide = part if wide is None else wide + part
    wide = jnp.where(keep, wide, 0.0)
    field = jnp.zeros((16, LANES), f32)
    for o in range(3):
        summed = jnp.sum(wide[o * TW : (o + 1) * TW, :], axis=0, keepdims=True)
        for r in range(TH):
            field = jnp.where(row16 == o * TH + r, summed[:, r * LANES : (r + 1) * LANES], field)
    u = jnp.where(inside, field + ground, 0.0)
    for sweep in range(PASSES):
        north = north_k * (pltpu.roll(u, 1, 0) - u)
        south = south_k * (pltpu.roll(u, 15, 0) - u)
        west = west_k * (pltpu.roll(u, 1, 1) - u)
        east = east_k * (pltpu.roll(u, LANES - 1, 1) - u)
        u = u + north + south + west + east
    u = pltpu.roll(u, LANES - PASSES, 1)
    out_ref[...] = u[TH : 2 * TH, :cols]

    for i, (dp, df) in enumerate(near):
        value_copy(i, dp, df).wait_send()


def body(footprint, basis, weights, conduct, baseline):
    pos_local, freq_local, doubled, rank = basis.shape
    foot = footprint.shape[1]
    n_pos = lax.axis_size("pos")
    n_freq = lax.axis_size("freq")
    rows = foot * TH
    outs = n_pos * CAP * 2
    messages = 2 * n_freq - 2
    near = 3 * n_freq - 1
    vmem = pl.BlockSpec(memory_space=pltpu.VMEM)
    hbm = pl.BlockSpec(memory_space=pltpu.MemorySpace.HBM)
    f32, bf16 = jnp.float32, jnp.bfloat16
    return pl.pallas_call(
        functools.partial(kernel, n_pos, n_freq),
        out_shape=jax.ShapeDtypeStruct(baseline.shape, f32),
        in_specs=[vmem] * 4 + [hbm],
        out_specs=vmem,
        scratch_shapes=[
            pltpu.VMEM((pos_local, rows, LANES), f32),
            pltpu.VMEM((pos_local, rows, LANES), f32),
            pltpu.VMEM(basis.shape, bf16),
            pltpu.VMEM((doubled // 2 // LANES, freq_local, rows, 2 * LANES), bf16),
            pltpu.VMEM((messages + 2, 2, rows, LANES), f32),
            pltpu.VMEM((messages, 2, rows, LANES), f32),
            pltpu.VMEM((PARTS, outs, LANES), f32),
            pltpu.VMEM((PARTS, outs, LANES), f32),
            pltpu.VMEM((1, LANES), f32),
            pltpu.VMEM((3 * n_freq, 1, LANES), f32),
            pltpu.VMEM((16, LANES), f32),
            pltpu.VMEM((9, 16, LANES), f32),
            pltpu.SemaphoreType.DMA((pos_local, freq_local)),
            pltpu.SemaphoreType.DMA((messages, PARTS)),
            pltpu.SemaphoreType.DMA((messages, PARTS)),
            pltpu.SemaphoreType.DMA((PARTS,)),
            pltpu.SemaphoreType.DMA((PARTS, n_pos)),
            pltpu.SemaphoreType.DMA((PARTS, n_pos)),
            pltpu.SemaphoreType.DMA((near,)),
            pltpu.SemaphoreType.DMA((near,)),
            pltpu.SemaphoreType.DMA((8,)),
            pltpu.SemaphoreType.DMA((9,)),
        ],
        compiler_params=pltpu.CompilerParams(
            collective_id=0, has_side_effects=True, vmem_limit_bytes=50 * 1024 * 1024
        ),
    )(footprint.T, weights.reshape(1, rank), conduct, baseline, basis)


def solution(mesh):
    return jax.shard_map(
        body,
        mesh=mesh,
        in_specs=(P(), P("pos", "freq", None, None), P(), P(None, "pos", "freq"), P("pos", "freq")),
        out_specs=P("pos", "freq"),
        check_vma=False,
    )
```

```python
import functools
import itertools

import jax
import jax.numpy as jnp
from jax import lax
from jax.experimental import pallas as pl
from jax.experimental.pallas import tpu as pltpu
from jax.sharding import PartitionSpec as P

TH = 4
TW = 8
CELLS = TH * TW
TILE_DEV = 32
PASSES = 3
CAP = 4
EPS = 1e-06
MESH = pl.DeviceIdType.MESH

UNIT = 0.025
CELL = 28
PITCH = 5
TOP = 160
SIN_POLY = (-4.547240826688576, 9.23637803174852, -5.615372827081364)
SCALE_SQ = 0.6259964781564749
DOUBLE = (2.0 + 1e-6) / SCALE_SQ
LANES = 128


def green_block(cross, depth_sq, turns):
    square = cross * cross + depth_sq
    dist = square * lax.rsqrt(square)
    root = lax.rsqrt(dist)
    amp = root * (TOP**0.5)
    scaled_amp = root * (TOP**0.5 * SCALE_SQ)
    out = []
    for rate in turns:
        phase = dist * rate
        x = jnp.round(phase) - phase
        z = x * x
        s = x * (((z + SIN_POLY[0]) * z + SIN_POLY[1]) * z + SIN_POLY[2])
        w = DOUBLE - s * s
        u = w * scaled_amp
        out.append(((u - amp).astype(jnp.bfloat16), (u * s * lax.rsqrt(w)).astype(jnp.bfloat16)))
    return out


def make_unit(lat_ref, dep_ref, basis_v, green_s, rates, elements):
    rows = lat_ref.shape[1]

    def unit(col, p):
        total = None
        for tile in range(elements // LANES):
            start = tile * LANES
            shift = (2 * CELL * col + (PITCH * (elements - 1) - 2 * PITCH * start)).astype(jnp.float32) * 0.5
            for rg in range(rows // 16):
                span = pl.ds(rg * 16, 16)
                values = green_block(lat_ref[p, span, :] + shift, dep_ref[p, span, :], rates)
                for f, (cosine, sine) in enumerate(values):
                    green_s[tile, f, span, 0:LANES] = cosine
                    green_s[tile, f, span, LANES : 2 * LANES] = sine
            for f in range(len(rates)):
                right = jnp.concatenate(
                    [
                        basis_v[p, f, start : start + LANES, :],
                        basis_v[p, f, elements + start : elements + start + LANES, :],
                    ],
                    axis=0,
                )
                part = jnp.dot(green_s[tile, f], right, preferred_element_type=jnp.float32)
                total = part if total is None else total + part
        return total

    return unit


def split3(x):
    hi = x.astype(jnp.bfloat16)
    rest = x - hi.astype(jnp.float32)
    mid = rest.astype(jnp.bfloat16)
    low = (rest - mid.astype(jnp.float32)).astype(jnp.bfloat16)
    return hi, mid, low


PARTS = 4


def digits_of(n_pos):
    return {32: (4, 4, 2), 8: (2, 2, 2)}[n_pos]


def walks_of(pos, n_pos):
    sizes = digits_of(n_pos)
    tables = []
    below = n_pos
    for size in sizes:
        below = below // size
        digit = pos // below % size
        tables.append([(digit + move) % size * below for move in range(size)])
    moves = list(itertools.product(*[range(size) for size in sizes]))[1:]
    moves.sort(key=lambda m: -sum(min(d, z - d) for d, z in zip(m, sizes)))
    return [sum(table[d] for table, d in zip(tables, m)) for m in moves]


def kernel(
    n_pos,
    n_freq,
    foot_in,
    weight_in,
    conduct_in,
    base_in,
    basis_ref,
    out_ref,
    foot_ref,
    weight_ref,
    conduct_ref,
    base_ref,
    in_sem,
    lat_v,
    dep_v,
    basis_v,
    green_s,
    send_b,
    recv_b,
    packed,
    arrived,
    value_b,
    value_r,
    halo_b,
    halo_r,
    basis_sem,
    ring_send,
    ring_recv,
    a2a_send,
    a2a_recv,
    val_send,
    val_recv,
    halo_send,
    halo_recv,
):
    pos = lax.axis_index("pos")
    freq = lax.axis_index("freq")
    pos_local, freq_local, doubled, rank = basis_ref.shape
    elements = doubled // 2
    freqs = freq_local * n_freq
    foot = foot_ref.shape[0]
    rows = foot * TH
    pair = rows // 2
    entries = pos_local * foot
    positions = pos_local * n_pos
    half = n_freq // 2
    messages = 4 * half - 2
    iota = lax.broadcasted_iota
    f32, bf16, i32 = jnp.float32, jnp.bfloat16, jnp.int32

    basis_loads = [
        [
            pltpu.make_async_copy(basis_ref.at[p, f], basis_v.at[p, f], basis_sem.at[p, f])
            for f in range(freq_local)
        ]
        for p in range(pos_local)
    ]
    foot_load, *small_loads = [
        pltpu.make_async_copy(src, dst, in_sem.at[i])
        for i, (src, dst) in enumerate(
            (
                (foot_in, foot_ref),
                (conduct_in, conduct_ref),
                (base_in, base_ref),
                (weight_in, weight_ref),
            )
        )
    ]
    foot_load.start()
    for p in range(pos_local):
        for copy in basis_loads[p]:
            copy.start()
    for copy in small_loads:
        copy.start()

    rows_at = {dp: (pos + dp + n_pos) % n_pos if dp else pos for dp in (-1, 0, 1)}
    cols_at = [(freq + df) % n_freq for df in range(n_freq)]

    def other(dp, df):
        return (rows_at[dp], cols_at[df % n_freq] if isinstance(df, int) else (freq + df + n_freq) % n_freq)

    def wait_all(ref, sem):
        pltpu.make_async_copy(ref, ref, sem).wait()

    barrier = pltpu.get_barrier_semaphore()
    near = [(dp, df) for dp in (-1, 0, 1) for df in range(n_freq) if (dp, df) != (0, 0)]
    near.sort(key=lambda d: -min(d[1], n_freq - d[1]) - abs(d[0]) * 0.5)
    sideways = [(dp, df) for dp, df in near if df != 0]
    for dp, df in sideways:
        pl.semaphore_signal(barrier, inc=1, device_id=other(dp, df), device_id_type=MESH)

    walks = walks_of(pos, n_pos)
    for target in walks:
        pl.semaphore_signal(barrier, inc=1, device_id=(target, freq), device_id_type=MESH)

    expand = iota(i32, (rows, foot), 0) % foot == iota(i32, (rows, foot), 1)
    expand = jnp.where(expand, 1.0, 0.0).astype(bf16)
    foot_load.wait()
    foot_all = foot_ref[...]
    foot_owner = (foot_all // TILE_DEV).astype(f32)
    foot_local = (foot_all % TILE_DEV).astype(f32)
    owner_of = jnp.dot(expand, foot_owner.astype(bf16), preferred_element_type=f32)
    local_of = jnp.dot(expand, foot_local.astype(bf16), preferred_element_type=f32)
    corner = iota(i32, (rows, 1), 0) // foot
    which = iota(i32, (rows, positions), 1)

    def locate(p):
        position = pos * pos_local + p
        owner = jnp.sum(jnp.where(which == position, owner_of, 0.0), axis=1, keepdims=True)
        local = jnp.sum(jnp.where(which == position, local_of, 0.0), axis=1, keepdims=True)
        depth = (TOP + CELL * (owner.astype(i32) * TH + corner)).astype(f32)
        centre = position * (CELL * TW * TILE_DEV // positions)
        lateral = CELL * TW * local.astype(i32) - centre
        lat_v[p] = (lateral - PITCH * iota(i32, (rows, LANES), 1)).astype(f32)
        dep_v[p] = jnp.broadcast_to(depth * depth, (rows, LANES))

    locate(0)

    rates = [
        (freqs // 2 + freq * freq_local + f).astype(f32) * (UNIT / freqs) for f in range(freq_local)
    ]
    unit = make_unit(lat_v, dep_v, basis_v, green_s, rates, elements)

    def compute(u):
        way = 1 - 2 * lax.rem(u, 2)
        dist = half - (u + 2) // 4
        p = lax.rem((u + 1) // 2, 2)
        done = unit(lax.rem(freq + way * dist + n_freq, n_freq), p)
        for h in range(2):
            send_b[u, h] = done[:, h * LANES : (h + 1) * LANES]

    def ring_copy(u):
        return pltpu.make_async_remote_copy(
            src_ref=send_b.at[u],
            dst_ref=recv_b.at[u],
            send_sem=ring_send,
            recv_sem=ring_recv.at[u, 0],
            device_id=other(0, 1 - 2 * lax.rem(u, 2)),
            device_id_type=MESH,
        )

    def ring_part(u, c):
        span = pl.ds((c % 2) * pair, pair)
        return pltpu.make_async_remote_copy(
            src_ref=send_b.at[u, c // 2, span, :],
            dst_ref=recv_b.at[u, c // 2, span, :],
            send_sem=ring_send,
            recv_sem=ring_recv.at[u, c],
            device_id=other(0, 1 - 2 * lax.rem(u, 2)),
            device_id_type=MESH,
        )

    for copy in basis_loads[0]:
        copy.wait()
    compute(jnp.int32(0))
    pl.semaphore_wait(barrier, len(sideways) + n_pos - 1)
    ring_copy(0).start()
    for p in range(1, pos_local):
        locate(p)

    for copy in small_loads:
        copy.wait()
    cols = base_ref.shape[1]
    halo_b[...] = jnp.zeros(halo_b.shape, f32)
    halo_b[0:TH, 0:cols] = conduct_ref[0]
    halo_b[TH : 2 * TH, 0:cols] = conduct_ref[1]
    halo_b[2 * TH : 3 * TH, 0:cols] = base_ref[...]
    halo_peers = [(dp, df) for dp in (-1, 0, 1) for df in (-1, 0, 1) if (dp, df) != (0, 0)]

    def halo_copy(i, dp, df):
        return pltpu.make_async_remote_copy(
            src_ref=halo_b,
            dst_ref=halo_r.at[(1 - dp) * 3 + (1 - df)],
            send_sem=halo_send,
            recv_sem=halo_recv,
            device_id=other(dp, df),
            device_id_type=MESH,
        )

    @pl.loop(1, messages + 2)
    def _(u):
        @pl.when(u == 1)
        def _():
            for p in range(1, pos_local):
                for copy in basis_loads[p]:
                    copy.wait()

        compute(u)

        @pl.when((u >= 4) & (u < messages))
        def _():
            ring_copy(u - 4).wait_recv()
            send_b[u] += recv_b[u - 4]

        @pl.when(u < messages - 4)
        def _():
            ring_copy(u).start()

        @pl.when((u >= messages - 4) & (u < messages))
        def _():
            ring_part(u, 0).start()
            ring_part(u, 1).start()

        @pl.when((u >= messages - 2) & (u < messages))
        def _():
            for c in range(2, PARTS):
                ring_part(u - 2, c).start()
                ring_part(u, c).start()

        @pl.when(u == 5)
        def _():
            for i, (dp, df) in enumerate(halo_peers):
                halo_copy(i, dp, df).start()

    outs = n_pos * CAP * 2
    width = pos_local * 2 * foot
    picks = iota(i32, (foot, positions), 1)
    owner_col = jnp.concatenate(
        [
            jnp.sum(jnp.where(picks == pos * pos_local + p, foot_owner, 0.0), axis=1, keepdims=True)
            for p in range(pos_local)
        ],
        axis=0,
    )
    lane = iota(i32, (entries, width), 1)
    entry_of_lane = lane // (2 * foot) * foot + lane % foot
    entry = iota(i32, (entries, width), 0)
    owner_row = jnp.sum(jnp.where(entry == entry_of_lane, owner_col, 0.0), axis=0, keepdims=True)
    same = (owner_col == owner_row) & (entry < entry_of_lane)
    order_row = jnp.sum(jnp.where(same, 1.0, 0.0), axis=0, keepdims=True)
    slot_row = owner_row * CAP + order_row
    to_row = iota(i32, (outs, width), 0)
    from_lane = iota(i32, (outs, width), 1)
    slot_out = (to_row // (2 * CAP) * CAP + to_row % CAP).astype(f32)
    gather = (slot_out == slot_row) & (to_row // CAP % 2 == from_lane // foot % 2)
    gather = jnp.where(gather, 1.0, 0.0).astype(bf16)
    gather = jnp.concatenate([gather] * 3, axis=1)

    mine = foot_owner == pos.astype(f32)
    mine_b = jnp.where(mine, 1.0, 0.0).astype(bf16)
    lower = iota(i32, (foot, foot), 1) < iota(i32, (foot, foot), 0)
    from_p = iota(i32, (positions, positions), 0)
    to_p = iota(i32, (positions, positions), 1)
    later = (from_p // pos_local == to_p // pos_local) & (from_p < to_p)
    moved = jnp.dot(mine_b, jnp.where(later, 1.0, 0.0).astype(bf16), preferred_element_type=f32)
    ahead = jnp.dot(
        jnp.where(lower, 1.0, 0.0).astype(bf16), mine_b, preferred_element_type=f32
    ) + jnp.sum(moved, axis=0, keepdims=True)
    found = jnp.concatenate(
        [
            jnp.sum(jnp.where(mine & (ahead == s), foot_local + 1.0, 0.0), axis=0, keepdims=True)
            for s in range(CAP)
        ],
        axis=0,
    )
    block_of = iota(i32, (positions, outs), 0) // pos_local
    block_to = iota(i32, (positions, outs), 1) // (2 * CAP)
    table = jnp.dot(
        found.astype(bf16),
        jnp.where(block_of == block_to, 1.0, 0.0).astype(bf16),
        preferred_element_type=f32,
    )
    turn = iota(i32, (CAP, outs), 1) % CAP == iota(i32, (CAP, outs), 0)
    tile_in = jnp.sum(jnp.where(turn, table, 0.0), axis=0, keepdims=True)
    row_in = iota(i32, (1, outs), 1) // CAP % 2
    target_row = jnp.where(tile_in > 0.0, tile_in - 1.0 + (TILE_DEV * row_in).astype(f32), -1.0)
    place = iota(i32, (2 * TILE_DEV, outs), 0).astype(f32) == target_row
    place = jnp.where(place, 1.0, 0.0).astype(bf16)
    place = jnp.concatenate([place] * 3, axis=1)

    wait_all(halo_r.at[pl.ds(0, 8)], halo_recv)
    lane16 = iota(i32, (16, LANES), 1)
    row16 = iota(i32, (16, LANES), 0)
    strips = []
    for dp in (-1, 0, 1):
        left = halo_r[(dp + 1) * 3]
        centre = halo_b[...] if dp == 0 else halo_r[(dp + 1) * 3 + 1]
        right = halo_r[(dp + 1) * 3 + 2]
        strip = jnp.where(
            lane16 < PASSES,
            pltpu.roll(left, LANES - cols + PASSES, 1),
            jnp.where(
                lane16 < cols + PASSES,
                pltpu.roll(centre, PASSES, 1),
                pltpu.roll(right, cols + PASSES, 1),
            ),
        )
        strips.append(strip)
    grid_row = row16 + TH * (pos - 1)
    grid_col = lane16 + (cols * freq - PASSES)
    inside = (grid_row >= 0) & (grid_row < TH * n_pos) & (grid_col >= 0) & (grid_col < TILE_DEV * TW)
    inside = inside & (row16 < 3 * TH) & (lane16 < cols + 2 * PASSES)

    def widened(a):
        pieces = [strip[a * TH : (a + 1) * TH, :] for strip in strips]
        tall = jnp.concatenate(pieces + [pieces[0]], axis=0)
        return jnp.where(inside, tall, 0.0)

    across_k = widened(0)
    along_k = widened(1)
    ground = widened(2)
    south_k = jnp.minimum(across_k, pltpu.roll(across_k, 15, 0))
    north_k = jnp.minimum(across_k, pltpu.roll(across_k, 1, 0))
    east_k = jnp.minimum(along_k, pltpu.roll(along_k, LANES - 1, 1))
    west_k = jnp.minimum(along_k, pltpu.roll(along_k, 1, 1))

    block = 2 * CAP
    own_block = pl.ds(pl.multiple_of(pos * block, block), block)

    def owner_copy(target, c):
        return pltpu.make_async_remote_copy(
            src_ref=packed.at[c, pl.ds(pl.multiple_of(target * block, block), block), :],
            dst_ref=arrived.at[c, own_block, :],
            send_sem=a2a_send,
            recv_sem=a2a_recv.at[c],
            device_id=(target, freq),
            device_id_type=MESH,
        )

    for c in range(PARTS):
        span = pl.ds((c % 2) * pair, pair)
        sums = []
        for own, right, left in (
            (messages + 1, messages - 2, messages - 3),
            (messages, messages - 4, messages - 1),
        ):
            ring_part(right, c).wait_recv()
            ring_part(left, c).wait_recv()
            sums.append(send_b[own, c // 2, span, :] + recv_b[right, c // 2, span, :] + recv_b[left, c // 2, span, :])
        stacked = jnp.concatenate(split3(jnp.concatenate(sums, axis=0)), axis=0)
        packed[c] = jnp.dot(gather, stacked, preferred_element_type=f32)

        for target in walks:
            owner_copy(target, c).start()
        pltpu.make_async_copy(
            packed.at[c, own_block, :], arrived.at[c, own_block, :], a2a_recv.at[c]
        ).start()

    energies = [None, None]
    for c in range(PARTS):
        wait_all(arrived.at[c], a2a_recv.at[c])
        stacked = jnp.concatenate(split3(arrived[c]), axis=0)
        compound = jnp.dot(place, stacked, preferred_element_type=f32)
        scaled = compound * compound * weight_ref[0:1, (c // 2) * LANES : (c // 2 + 1) * LANES]
        energies[c % 2] = scaled if energies[c % 2] is None else energies[c % 2] + scaled
    value = jnp.zeros((1, LANES), f32)
    for pair_at, energy in enumerate(energies):
        energy = jnp.sum(energy, axis=1, keepdims=True)
        on = iota(i32, (2 * TILE_DEV, LANES), 1) == iota(i32, (2 * TILE_DEV, LANES), 0) + pair_at * 2 * TILE_DEV
        value = value + jnp.sum(jnp.where(on, energy, 0.0), axis=0, keepdims=True)
    value_b[...] = jnp.sqrt(value / rank + EPS)

    def value_copy(i, dp, df):
        return pltpu.make_async_remote_copy(
            src_ref=value_b,
            dst_ref=value_r.at[(1 - dp) * n_freq + freq],
            send_sem=val_send,
            recv_sem=val_recv,
            device_id=other(dp, df),
            device_id_type=MESH,
        )

    for i, (dp, df) in enumerate(near):
        value_copy(i, dp, df).start()

    value_r[n_freq + freq] = value_b[...]

    wait_all(send_b.at[pl.ds(0, messages)], ring_send)
    wait_all(packed.at[:, pl.ds(0, (n_pos - 1) * block), :], a2a_send)
    wait_all(halo_r.at[pl.ds(0, 8)], halo_send)

    from_r = iota(i32, (LANES, TH * LANES), 0)
    to_n = iota(i32, (LANES, TH * LANES), 1)
    to_col = to_n % LANES + (cols * freq - PASSES) + TW
    chosen = (from_r // TILE_DEV == to_n // LANES) & (from_r % TILE_DEV == to_col // TW - 1)
    spread = jnp.where(chosen, 1.0, 0.0).astype(bf16)
    sub24 = iota(i32, (3 * TW, TH * LANES), 0)
    col24 = iota(i32, (3 * TW, TH * LANES), 1)
    keep = (col24 % LANES + (cols * freq - PASSES) + TW) % TW == sub24 % TW
    sub8 = iota(i32, (TW, LANES), 0)

    wait_all(value_r.at[pl.ds(0, len(near))], val_recv)

    groups = []
    for o in range(3):
        group = jnp.broadcast_to(value_r[o * n_freq], (TW, LANES))
        for col in range(1, n_freq):
            group = jnp.where(sub8 == col, value_r[o * n_freq + col], group)
        groups.append(group)
    wide = None
    for piece in split3(jnp.concatenate(groups, axis=0)):
        part = jnp.dot(piece, spread, preferred_element_type=f32)
        wide = part if wide is None else wide + part
    wide = jnp.where(keep, wide, 0.0)
    field = jnp.zeros((16, LANES), f32)
    for o in range(3):
        summed = jnp.sum(wide[o * TW : (o + 1) * TW, :], axis=0, keepdims=True)
        for r in range(TH):
            field = jnp.where(row16 == o * TH + r, summed[:, r * LANES : (r + 1) * LANES], field)
    u = jnp.where(inside, field + ground, 0.0)
    for sweep in range(PASSES):
        north = north_k * (pltpu.roll(u, 1, 0) - u)
        south = south_k * (pltpu.roll(u, 15, 0) - u)
        west = west_k * (pltpu.roll(u, 1, 1) - u)
        east = east_k * (pltpu.roll(u, LANES - 1, 1) - u)
        u = u + north + south + west + east
    u = pltpu.roll(u, LANES - PASSES, 1)
    out_ref[...] = u[TH : 2 * TH, :cols]

    wait_all(value_r.at[pl.ds(0, len(near))], val_send)


def body(footprint, basis, weights, conduct, baseline):
    pos_local, freq_local, doubled, rank = basis.shape
    foot = footprint.shape[1]
    n_pos = lax.axis_size("pos")
    n_freq = lax.axis_size("freq")
    rows = foot * TH
    outs = n_pos * CAP * 2
    messages = 2 * n_freq - 2
    vmem = pl.BlockSpec(memory_space=pltpu.VMEM)
    hbm = pl.BlockSpec(memory_space=pltpu.MemorySpace.HBM)
    f32, bf16 = jnp.float32, jnp.bfloat16
    return pl.pallas_call(
        functools.partial(kernel, n_pos, n_freq),
        out_shape=jax.ShapeDtypeStruct(baseline.shape, f32),
        in_specs=[hbm] * 5,
        out_specs=vmem,
        scratch_shapes=[
            pltpu.VMEM(footprint.shape[::-1], jnp.int32),
            pltpu.VMEM((1, rank), f32),
            pltpu.VMEM(conduct.shape, f32),
            pltpu.VMEM(baseline.shape, f32),
            pltpu.SemaphoreType.DMA((4,)),
            pltpu.VMEM((pos_local, rows, LANES), f32),
            pltpu.VMEM((pos_local, rows, LANES), f32),
            pltpu.VMEM(basis.shape, bf16),
            pltpu.VMEM((doubled // 2 // LANES, freq_local, rows, 2 * LANES), bf16),
            pltpu.VMEM((messages + 2, 2, rows, LANES), f32),
            pltpu.VMEM((messages, 2, rows, LANES), f32),
            pltpu.VMEM((PARTS, outs, LANES), f32),
            pltpu.VMEM((PARTS, outs, LANES), f32),
            pltpu.VMEM((1, LANES), f32),
            pltpu.VMEM((3 * n_freq, 1, LANES), f32),
            pltpu.VMEM((16, LANES), f32),
            pltpu.VMEM((9, 16, LANES), f32),
            pltpu.SemaphoreType.DMA((pos_local, freq_local)),
            pltpu.SemaphoreType.DMA,
            pltpu.SemaphoreType.DMA((messages, PARTS)),
            pltpu.SemaphoreType.DMA,
            pltpu.SemaphoreType.DMA((PARTS,)),
            pltpu.SemaphoreType.DMA,
            pltpu.SemaphoreType.DMA,
            pltpu.SemaphoreType.DMA,
            pltpu.SemaphoreType.DMA,
        ],
        compiler_params=pltpu.CompilerParams(
            collective_id=0, has_side_effects=True, vmem_limit_bytes=50 * 1024 * 1024
        ),
    )(*[pltpu.with_memory_space_constraint(x, pltpu.MemorySpace.HBM) for x in (footprint.T, weights.reshape(1, rank), conduct, baseline, basis)])


def solution(mesh):
    return jax.shard_map(
        body,
        mesh=mesh,
        in_specs=(P(), P("pos", "freq", None, None), P(), P(None, "pos", "freq"), P("pos", "freq")),
        out_specs=P("pos", "freq"),
        check_vma=False,
    )
```

```python
import functools
import itertools

import jax
import jax.numpy as jnp
from jax import lax
from jax.experimental import pallas as pl
from jax.experimental.pallas import tpu as pltpu
from jax.sharding import PartitionSpec as P

TH = 4
TW = 8
CELLS = TH * TW
TILE_DEV = 32
PASSES = 3
CAP = 4
EPS = 1e-06
MESH = pl.DeviceIdType.MESH

UNIT = 0.025
CELL = 28
PITCH = 5
TOP = 160
SIN_POLY = (-4.547240826688576, 9.23637803174852, -5.615372827081364)
SCALE_SQ = 0.6259964781564749
DOUBLE = (2.0 + 1e-6) / SCALE_SQ
LANES = 128


def green_block(cross, depth_sq, turns):
    square = cross * cross + depth_sq
    dist = square * lax.rsqrt(square)
    root = lax.rsqrt(dist)
    amp = root * (TOP**0.5)
    scaled_amp = root * (TOP**0.5 * SCALE_SQ)
    out = []
    for rate in turns:
        phase = dist * rate
        x = jnp.round(phase) - phase
        z = x * x
        s = x * (((z + SIN_POLY[0]) * z + SIN_POLY[1]) * z + SIN_POLY[2])
        w = DOUBLE - s * s
        u = w * scaled_amp
        out.append(((u - amp).astype(jnp.bfloat16), (u * s * lax.rsqrt(w)).astype(jnp.bfloat16)))
    return out


def make_unit(lat_ref, dep_ref, basis_v, green_s, rates, elements):
    rows = lat_ref.shape[1]

    def unit(col, p, base=0, height=rows):
        total = None
        for tile in range(elements // LANES):
            start = tile * LANES
            shift = (2 * CELL * col + (PITCH * (elements - 1) - 2 * PITCH * start)).astype(jnp.float32) * 0.5
            for rg in range(base // 16, (base + height) // 16):
                span = pl.ds(rg * 16, 16)
                values = green_block(lat_ref[p, span, :] + shift, dep_ref[p, span, :], rates)
                for f, (cosine, sine) in enumerate(values):
                    green_s[tile, f, span, 0:LANES] = cosine
                    green_s[tile, f, span, LANES : 2 * LANES] = sine
            for f in range(len(rates)):
                right = jnp.concatenate(
                    [
                        basis_v[p, f, start : start + LANES, :],
                        basis_v[p, f, elements + start : elements + start + LANES, :],
                    ],
                    axis=0,
                )
                part = jnp.dot(
                    green_s[tile, f, base : base + height, :], right, preferred_element_type=jnp.float32
                )
                total = part if total is None else total + part
        return total

    return unit


def split3(x):
    hi = x.astype(jnp.bfloat16)
    rest = x - hi.astype(jnp.float32)
    mid = rest.astype(jnp.bfloat16)
    low = (rest - mid.astype(jnp.float32)).astype(jnp.bfloat16)
    return hi, mid, low


PARTS = 4


def digits_of(n_pos):
    return {32: (4, 4, 2), 8: (2, 2, 2)}[n_pos]


def walks_of(pos, n_pos):
    sizes = digits_of(n_pos)
    tables = []
    below = n_pos
    for size in sizes:
        below = below // size
        digit = pos // below % size
        tables.append([(digit + move) % size * below for move in range(size)])
    moves = list(itertools.product(*[range(size) for size in sizes]))[1:]
    moves.sort(key=lambda m: -sum(min(d, z - d) for d, z in zip(m, sizes)))
    return [sum(table[d] for table, d in zip(tables, m)) for m in moves]


def kernel(
    n_pos,
    n_freq,
    foot_in,
    weight_in,
    conduct_in,
    base_in,
    basis_ref,
    out_ref,
    foot_ref,
    weight_ref,
    conduct_ref,
    base_ref,
    in_sem,
    lat_v,
    dep_v,
    basis_v,
    green_s,
    send_b,
    recv_b,
    packed,
    arrived,
    value_b,
    value_r,
    halo_b,
    halo_r,
    basis_sem,
    ring_send,
    ring_recv,
    a2a_send,
    a2a_recv,
    val_send,
    val_recv,
    halo_send,
    halo_recv,
):
    pos = lax.axis_index("pos")
    freq = lax.axis_index("freq")
    pos_local, freq_local, doubled, rank = basis_ref.shape
    elements = doubled // 2
    freqs = freq_local * n_freq
    foot = foot_ref.shape[0]
    rows = foot * TH
    pair = rows // 2
    entries = pos_local * foot
    positions = pos_local * n_pos
    half = n_freq // 2
    messages = 4 * half - 2
    iota = lax.broadcasted_iota
    f32, bf16, i32 = jnp.float32, jnp.bfloat16, jnp.int32

    basis_loads = [
        [
            pltpu.make_async_copy(basis_ref.at[p, f], basis_v.at[p, f], basis_sem.at[p, f])
            for f in range(freq_local)
        ]
        for p in range(pos_local)
    ]
    foot_load, *small_loads = [
        pltpu.make_async_copy(src, dst, in_sem.at[i])
        for i, (src, dst) in enumerate(
            (
                (foot_in, foot_ref),
                (conduct_in, conduct_ref),
                (base_in, base_ref),
                (weight_in, weight_ref),
            )
        )
    ]
    foot_load.start()
    for p in range(pos_local):
        for copy in basis_loads[p]:
            copy.start()
    for copy in small_loads:
        copy.start()

    rows_at = {dp: (pos + dp + n_pos) % n_pos if dp else pos for dp in (-1, 0, 1)}
    cols_at = [(freq + df) % n_freq for df in range(n_freq)]

    def other(dp, df):
        return (rows_at[dp], cols_at[df % n_freq] if isinstance(df, int) else (freq + df + n_freq) % n_freq)

    def wait_all(ref, sem):
        pltpu.make_async_copy(ref, ref, sem).wait()

    barrier = pltpu.get_barrier_semaphore()
    near = [(dp, df) for dp in (-1, 0, 1) for df in range(n_freq) if (dp, df) != (0, 0)]
    near.sort(key=lambda d: -min(d[1], n_freq - d[1]) - abs(d[0]) * 0.5)
    sideways = [(dp, df) for dp, df in near if df != 0]
    for dp, df in sideways:
        pl.semaphore_signal(barrier, inc=1, device_id=other(dp, df), device_id_type=MESH)

    walks = walks_of(pos, n_pos)
    for target in walks:
        pl.semaphore_signal(barrier, inc=1, device_id=(target, freq), device_id_type=MESH)

    expand = iota(i32, (rows, foot), 0) % foot == iota(i32, (rows, foot), 1)
    expand = jnp.where(expand, 1.0, 0.0).astype(bf16)
    foot_load.wait()
    foot_all = foot_ref[...]
    foot_owner = (foot_all // TILE_DEV).astype(f32)
    foot_local = (foot_all % TILE_DEV).astype(f32)
    owner_of = jnp.dot(expand, foot_owner.astype(bf16), preferred_element_type=f32)
    local_of = jnp.dot(expand, foot_local.astype(bf16), preferred_element_type=f32)
    corner = iota(i32, (rows, 1), 0) // foot
    which = iota(i32, (rows, positions), 1)

    def locate(p):
        position = pos * pos_local + p
        owner = jnp.sum(jnp.where(which == position, owner_of, 0.0), axis=1, keepdims=True)
        local = jnp.sum(jnp.where(which == position, local_of, 0.0), axis=1, keepdims=True)
        depth = (TOP + CELL * (owner.astype(i32) * TH + corner)).astype(f32)
        centre = position * (CELL * TW * TILE_DEV // positions)
        lateral = CELL * TW * local.astype(i32) - centre
        lat_v[p] = (lateral - PITCH * iota(i32, (rows, LANES), 1)).astype(f32)
        dep_v[p] = jnp.broadcast_to(depth * depth, (rows, LANES))

    locate(0)

    rates = [
        (freqs // 2 + freq * freq_local + f).astype(f32) * (UNIT / freqs) for f in range(freq_local)
    ]
    unit = make_unit(lat_v, dep_v, basis_v, green_s, rates, elements)

    def compute(u, base=0, height=rows):
        way = 1 - 2 * (u % 2)
        dist = half - (u + 2) // 4
        p = (u + 1) // 2 % 2
        done = unit((freq + way * dist + n_freq) % n_freq, p, base, height)
        for h in range(2):
            send_b[u, h, base : base + height, :] = done[:, h * LANES : (h + 1) * LANES]

    def ring_copy(u):
        return pltpu.make_async_remote_copy(
            src_ref=send_b.at[u],
            dst_ref=recv_b.at[u],
            send_sem=ring_send,
            recv_sem=ring_recv.at[u, 0],
            device_id=other(0, 1 - 2 * lax.rem(u, 2)),
            device_id_type=MESH,
        )

    def ring_part(u, c):
        span = pl.ds((c % 2) * pair, pair)
        return pltpu.make_async_remote_copy(
            src_ref=send_b.at[u, c // 2, span, :],
            dst_ref=recv_b.at[u, c // 2, span, :],
            send_sem=ring_send,
            recv_sem=ring_recv.at[u, c],
            device_id=other(0, 1 - 2 * lax.rem(u, 2)),
            device_id_type=MESH,
        )

    def ring_early(u, base):
        span = pl.ds(base, pair)
        return pltpu.make_async_remote_copy(
            src_ref=send_b.at[u, :, span, :],
            dst_ref=recv_b.at[u, :, span, :],
            send_sem=ring_send,
            recv_sem=ring_recv.at[u, 0],
            device_id=other(0, 1 - 2 * u),
            device_id_type=MESH,
        )

    for copy in basis_loads[0]:
        copy.wait()
    compute(0, 0, pair)
    pl.semaphore_wait(barrier, len(sideways) + n_pos - 1)
    ring_early(0, 0).start()
    for p in range(1, pos_local):
        locate(p)
        for copy in basis_loads[p]:
            copy.wait()
    for u, base in ((1, 0), (0, pair), (1, pair)):
        compute(u, base, pair)
        ring_early(u, base).start()

    for copy in small_loads:
        copy.wait()
    cols = base_ref.shape[1]
    halo_b[...] = jnp.zeros(halo_b.shape, f32)
    halo_b[0:TH, 0:cols] = conduct_ref[0]
    halo_b[TH : 2 * TH, 0:cols] = conduct_ref[1]
    halo_b[2 * TH : 3 * TH, 0:cols] = base_ref[...]
    halo_peers = [(dp, df) for dp in (-1, 0, 1) for df in (-1, 0, 1) if (dp, df) != (0, 0)]

    def halo_copy(i, dp, df):
        return pltpu.make_async_remote_copy(
            src_ref=halo_b,
            dst_ref=halo_r.at[(1 - dp) * 3 + (1 - df)],
            send_sem=halo_send,
            recv_sem=halo_recv,
            device_id=other(dp, df),
            device_id_type=MESH,
        )

    @pl.loop(2, messages + 2)
    def _(u):
        compute(u)

        @pl.when((u >= 4) & (u < messages))
        def _():
            ring_copy(u - 4).wait_recv()
            send_b[u] += recv_b[u - 4]

        @pl.when(u < messages - 4)
        def _():
            ring_copy(u).start()

        @pl.when((u >= messages - 4) & (u < messages))
        def _():
            ring_part(u, 0).start()
            ring_part(u, 1).start()

        @pl.when((u >= messages - 2) & (u < messages))
        def _():
            for c in range(2, PARTS):
                ring_part(u - 2, c).start()
                ring_part(u, c).start()

        @pl.when(u == 5)
        def _():
            for i, (dp, df) in enumerate(halo_peers):
                halo_copy(i, dp, df).start()

    outs = n_pos * CAP * 2
    width = pos_local * 2 * foot
    picks = iota(i32, (foot, positions), 1)
    owner_col = jnp.concatenate(
        [
            jnp.sum(jnp.where(picks == pos * pos_local + p, foot_owner, 0.0), axis=1, keepdims=True)
            for p in range(pos_local)
        ],
        axis=0,
    )
    lane = iota(i32, (entries, width), 1)
    entry_of_lane = lane // (2 * foot) * foot + lane % foot
    entry = iota(i32, (entries, width), 0)
    owner_row = jnp.sum(jnp.where(entry == entry_of_lane, owner_col, 0.0), axis=0, keepdims=True)
    same = (owner_col == owner_row) & (entry < entry_of_lane)
    order_row = jnp.sum(jnp.where(same, 1.0, 0.0), axis=0, keepdims=True)
    slot_row = owner_row * CAP + order_row
    to_row = iota(i32, (outs, width), 0)
    from_lane = iota(i32, (outs, width), 1)
    slot_out = (to_row // (2 * CAP) * CAP + to_row % CAP).astype(f32)
    gather = (slot_out == slot_row) & (to_row // CAP % 2 == from_lane // foot % 2)
    gather = jnp.where(gather, 1.0, 0.0).astype(bf16)
    gather = jnp.concatenate([gather] * 3, axis=1)

    mine = foot_owner == pos.astype(f32)
    mine_b = jnp.where(mine, 1.0, 0.0).astype(bf16)
    lower = iota(i32, (foot, foot), 1) < iota(i32, (foot, foot), 0)
    from_p = iota(i32, (positions, positions), 0)
    to_p = iota(i32, (positions, positions), 1)
    later = (from_p // pos_local == to_p // pos_local) & (from_p < to_p)
    moved = jnp.dot(mine_b, jnp.where(later, 1.0, 0.0).astype(bf16), preferred_element_type=f32)
    ahead = jnp.dot(
        jnp.where(lower, 1.0, 0.0).astype(bf16), mine_b, preferred_element_type=f32
    ) + jnp.sum(moved, axis=0, keepdims=True)
    found = jnp.concatenate(
        [
            jnp.sum(jnp.where(mine & (ahead == s), foot_local + 1.0, 0.0), axis=0, keepdims=True)
            for s in range(CAP)
        ],
        axis=0,
    )
    block_of = iota(i32, (positions, outs), 0) // pos_local
    block_to = iota(i32, (positions, outs), 1) // (2 * CAP)
    table = jnp.dot(
        found.astype(bf16),
        jnp.where(block_of == block_to, 1.0, 0.0).astype(bf16),
        preferred_element_type=f32,
    )
    turn = iota(i32, (CAP, outs), 1) % CAP == iota(i32, (CAP, outs), 0)
    tile_in = jnp.sum(jnp.where(turn, table, 0.0), axis=0, keepdims=True)
    row_in = iota(i32, (1, outs), 1) // CAP % 2
    target_row = jnp.where(tile_in > 0.0, tile_in - 1.0 + (TILE_DEV * row_in).astype(f32), -1.0)
    place = iota(i32, (2 * TILE_DEV, outs), 0).astype(f32) == target_row
    place = jnp.where(place, 1.0, 0.0).astype(bf16)
    place = jnp.concatenate([place] * 3, axis=1)

    wait_all(halo_r.at[pl.ds(0, 8)], halo_recv)
    lane16 = iota(i32, (16, LANES), 1)
    row16 = iota(i32, (16, LANES), 0)
    strips = []
    for dp in (-1, 0, 1):
        left = halo_r[(dp + 1) * 3]
        centre = halo_b[...] if dp == 0 else halo_r[(dp + 1) * 3 + 1]
        right = halo_r[(dp + 1) * 3 + 2]
        strip = jnp.where(
            lane16 < PASSES,
            pltpu.roll(left, LANES - cols + PASSES, 1),
            jnp.where(
                lane16 < cols + PASSES,
                pltpu.roll(centre, PASSES, 1),
                pltpu.roll(right, cols + PASSES, 1),
            ),
        )
        strips.append(strip)
    grid_row = row16 + TH * (pos - 1)
    grid_col = lane16 + (cols * freq - PASSES)
    inside = (grid_row >= 0) & (grid_row < TH * n_pos) & (grid_col >= 0) & (grid_col < TILE_DEV * TW)
    inside = inside & (row16 < 3 * TH) & (lane16 < cols + 2 * PASSES)

    def widened(a):
        pieces = [strip[a * TH : (a + 1) * TH, :] for strip in strips]
        tall = jnp.concatenate(pieces + [pieces[0]], axis=0)
        return jnp.where(inside, tall, 0.0)

    across_k = widened(0)
    along_k = widened(1)
    ground = widened(2)
    south_k = jnp.minimum(across_k, pltpu.roll(across_k, 15, 0))
    north_k = jnp.minimum(across_k, pltpu.roll(across_k, 1, 0))
    east_k = jnp.minimum(along_k, pltpu.roll(along_k, LANES - 1, 1))
    west_k = jnp.minimum(along_k, pltpu.roll(along_k, 1, 1))

    block = 2 * CAP
    own_block = pl.ds(pl.multiple_of(pos * block, block), block)

    def owner_copy(target, c):
        return pltpu.make_async_remote_copy(
            src_ref=packed.at[c, pl.ds(pl.multiple_of(target * block, block), block), :],
            dst_ref=arrived.at[c, own_block, :],
            send_sem=a2a_send,
            recv_sem=a2a_recv.at[c],
            device_id=(target, freq),
            device_id_type=MESH,
        )

    for c in range(PARTS):
        span = pl.ds((c % 2) * pair, pair)
        sums = []
        for own, right, left in (
            (messages + 1, messages - 2, messages - 3),
            (messages, messages - 4, messages - 1),
        ):
            ring_part(right, c).wait_recv()
            ring_part(left, c).wait_recv()
            sums.append(send_b[own, c // 2, span, :] + recv_b[right, c // 2, span, :] + recv_b[left, c // 2, span, :])
        stacked = jnp.concatenate(split3(jnp.concatenate(sums, axis=0)), axis=0)
        packed[c] = jnp.dot(gather, stacked, preferred_element_type=f32)

        for target in walks:
            owner_copy(target, c).start()
        pltpu.make_async_copy(
            packed.at[c, own_block, :], arrived.at[c, own_block, :], a2a_recv.at[c]
        ).start()

    energies = [None, None]
    for c in range(PARTS):
        wait_all(arrived.at[c], a2a_recv.at[c])
        stacked = jnp.concatenate(split3(arrived[c]), axis=0)
        compound = jnp.dot(place, stacked, preferred_element_type=f32)
        scaled = compound * compound * weight_ref[0:1, (c // 2) * LANES : (c // 2 + 1) * LANES]
        energies[c % 2] = scaled if energies[c % 2] is None else energies[c % 2] + scaled
    value = jnp.zeros((1, LANES), f32)
    for pair_at, energy in enumerate(energies):
        energy = jnp.sum(energy, axis=1, keepdims=True)
        on = iota(i32, (2 * TILE_DEV, LANES), 1) == iota(i32, (2 * TILE_DEV, LANES), 0) + pair_at * 2 * TILE_DEV
        value = value + jnp.sum(jnp.where(on, energy, 0.0), axis=0, keepdims=True)
    value_b[...] = jnp.sqrt(value / rank + EPS)

    def value_copy(i, dp, df):
        return pltpu.make_async_remote_copy(
            src_ref=value_b,
            dst_ref=value_r.at[(1 - dp) * n_freq + freq],
            send_sem=val_send,
            recv_sem=val_recv,
            device_id=other(dp, df),
            device_id_type=MESH,
        )

    for i, (dp, df) in enumerate(near):
        value_copy(i, dp, df).start()

    value_r[n_freq + freq] = value_b[...]

    wait_all(send_b.at[pl.ds(0, messages)], ring_send)
    wait_all(packed.at[:, pl.ds(0, (n_pos - 1) * block), :], a2a_send)
    wait_all(halo_r.at[pl.ds(0, 8)], halo_send)

    from_r = iota(i32, (LANES, TH * LANES), 0)
    to_n = iota(i32, (LANES, TH * LANES), 1)
    to_col = to_n % LANES + (cols * freq - PASSES) + TW
    chosen = (from_r // TILE_DEV == to_n // LANES) & (from_r % TILE_DEV == to_col // TW - 1)
    spread = jnp.where(chosen, 1.0, 0.0).astype(bf16)
    sub24 = iota(i32, (3 * TW, TH * LANES), 0)
    col24 = iota(i32, (3 * TW, TH * LANES), 1)
    keep = (col24 % LANES + (cols * freq - PASSES) + TW) % TW == sub24 % TW
    sub8 = iota(i32, (TW, LANES), 0)

    wait_all(value_r.at[pl.ds(0, len(near))], val_recv)

    groups = []
    for o in range(3):
        group = jnp.broadcast_to(value_r[o * n_freq], (TW, LANES))
        for col in range(1, n_freq):
            group = jnp.where(sub8 == col, value_r[o * n_freq + col], group)
        groups.append(group)
    wide = None
    for piece in split3(jnp.concatenate(groups, axis=0)):
        part = jnp.dot(piece, spread, preferred_element_type=f32)
        wide = part if wide is None else wide + part
    wide = jnp.where(keep, wide, 0.0)
    field = jnp.zeros((16, LANES), f32)
    for o in range(3):
        summed = jnp.sum(wide[o * TW : (o + 1) * TW, :], axis=0, keepdims=True)
        for r in range(TH):
            field = jnp.where(row16 == o * TH + r, summed[:, r * LANES : (r + 1) * LANES], field)
    u = jnp.where(inside, field + ground, 0.0)
    for sweep in range(PASSES):
        north = north_k * (pltpu.roll(u, 1, 0) - u)
        south = south_k * (pltpu.roll(u, 15, 0) - u)
        west = west_k * (pltpu.roll(u, 1, 1) - u)
        east = east_k * (pltpu.roll(u, LANES - 1, 1) - u)
        u = u + north + south + west + east
    u = pltpu.roll(u, LANES - PASSES, 1)
    out_ref[...] = u[TH : 2 * TH, :cols]

    wait_all(value_r.at[pl.ds(0, len(near))], val_send)


def body(footprint, basis, weights, conduct, baseline):
    pos_local, freq_local, doubled, rank = basis.shape
    foot = footprint.shape[1]
    n_pos = lax.axis_size("pos")
    n_freq = lax.axis_size("freq")
    rows = foot * TH
    outs = n_pos * CAP * 2
    messages = 2 * n_freq - 2
    vmem = pl.BlockSpec(memory_space=pltpu.VMEM)
    hbm = pl.BlockSpec(memory_space=pltpu.MemorySpace.HBM)
    f32, bf16 = jnp.float32, jnp.bfloat16
    return pl.pallas_call(
        functools.partial(kernel, n_pos, n_freq),
        out_shape=jax.ShapeDtypeStruct(baseline.shape, f32),
        in_specs=[hbm] * 5,
        out_specs=vmem,
        scratch_shapes=[
            pltpu.VMEM(footprint.shape[::-1], jnp.int32),
            pltpu.VMEM((1, rank), f32),
            pltpu.VMEM(conduct.shape, f32),
            pltpu.VMEM(baseline.shape, f32),
            pltpu.SemaphoreType.DMA((4,)),
            pltpu.VMEM((pos_local, rows, LANES), f32),
            pltpu.VMEM((pos_local, rows, LANES), f32),
            pltpu.VMEM(basis.shape, bf16),
            pltpu.VMEM((doubled // 2 // LANES, freq_local, rows, 2 * LANES), bf16),
            pltpu.VMEM((messages + 2, 2, rows, LANES), f32),
            pltpu.VMEM((messages, 2, rows, LANES), f32),
            pltpu.VMEM((PARTS, outs, LANES), f32),
            pltpu.VMEM((PARTS, outs, LANES), f32),
            pltpu.VMEM((1, LANES), f32),
            pltpu.VMEM((3 * n_freq, 1, LANES), f32),
            pltpu.VMEM((16, LANES), f32),
            pltpu.VMEM((9, 16, LANES), f32),
            pltpu.SemaphoreType.DMA((pos_local, freq_local)),
            pltpu.SemaphoreType.DMA,
            pltpu.SemaphoreType.DMA((messages, PARTS)),
            pltpu.SemaphoreType.DMA,
            pltpu.SemaphoreType.DMA((PARTS,)),
            pltpu.SemaphoreType.DMA,
            pltpu.SemaphoreType.DMA,
            pltpu.SemaphoreType.DMA,
            pltpu.SemaphoreType.DMA,
        ],
        compiler_params=pltpu.CompilerParams(
            collective_id=0, has_side_effects=True, vmem_limit_bytes=50 * 1024 * 1024
        ),
    )(*[pltpu.with_memory_space_constraint(x, pltpu.MemorySpace.HBM) for x in (footprint.T, weights.reshape(1, rank), conduct, baseline, basis)])


def solution(mesh):
    return jax.shard_map(
        body,
        mesh=mesh,
        in_specs=(P(), P("pos", "freq", None, None), P(), P(None, "pos", "freq"), P("pos", "freq")),
        out_specs=P("pos", "freq"),
        check_vma=False,
    )
```

```python
import functools
import itertools

import jax
import jax.numpy as jnp
from jax import lax
from jax.experimental import pallas as pl
from jax.experimental.pallas import tpu as pltpu
from jax.sharding import PartitionSpec as P

TH = 4
TW = 8
CELLS = TH * TW
TILE_DEV = 32
PASSES = 3
CAP = 4
EPS = 1e-06
MESH = pl.DeviceIdType.MESH

UNIT = 0.025
CELL = 28
PITCH = 5
TOP = 160
SIN_POLY = (-4.547240826688576, 9.23637803174852, -5.615372827081364)
SCALE_SQ = 0.6259964781564749
DOUBLE = (2.0 + 1e-6) / SCALE_SQ
LANES = 128


def green_block(cross, depth_sq, turns):
    square = cross * cross + depth_sq
    dist = square * lax.rsqrt(square)
    root = lax.rsqrt(dist)
    amp = root * (TOP**0.5)
    scaled_amp = root * (TOP**0.5 * SCALE_SQ)
    out = []
    for rate in turns:
        phase = dist * rate
        x = jnp.round(phase) - phase
        z = x * x
        s = x * (((z + SIN_POLY[0]) * z + SIN_POLY[1]) * z + SIN_POLY[2])
        w = DOUBLE - s * s
        u = w * scaled_amp
        out.append(((u - amp).astype(jnp.bfloat16), (u * s * lax.rsqrt(w)).astype(jnp.bfloat16)))
    return out


def make_unit(lat_ref, dep_ref, basis_v, green_s, rates, elements):
    rows = lat_ref.shape[1]

    def unit(col, p, base=0, height=rows):
        total = None
        for tile in range(elements // LANES):
            start = tile * LANES
            shift = (2 * CELL * col + (PITCH * (elements - 1) - 2 * PITCH * start)).astype(jnp.float32) * 0.5
            for rg in range(base // 16, (base + height) // 16):
                span = pl.ds(rg * 16, 16)
                values = green_block(lat_ref[p, span, :] + shift, dep_ref[p, span, :], rates)
                for f, (cosine, sine) in enumerate(values):
                    green_s[tile, f, span, 0:LANES] = cosine
                    green_s[tile, f, span, LANES : 2 * LANES] = sine
            for f in range(len(rates)):
                right = jnp.concatenate(
                    [
                        basis_v[p, f, start : start + LANES, :],
                        basis_v[p, f, elements + start : elements + start + LANES, :],
                    ],
                    axis=0,
                )
                part = jnp.dot(
                    green_s[tile, f, base : base + height, :], right, preferred_element_type=jnp.float32
                )
                total = part if total is None else total + part
        return total

    return unit


def split3(x):
    hi = x.astype(jnp.bfloat16)
    rest = x - hi.astype(jnp.float32)
    mid = rest.astype(jnp.bfloat16)
    low = (rest - mid.astype(jnp.float32)).astype(jnp.bfloat16)
    return hi, mid, low


PARTS = 4


def digits_of(n_pos):
    return {32: (4, 4, 2), 8: (2, 2, 2)}[n_pos]


def walks_of(pos, n_pos):
    sizes = digits_of(n_pos)
    tables = []
    below = n_pos
    for size in sizes:
        below = below // size
        digit = pos // below % size
        tables.append([(digit + move) % size * below for move in range(size)])
    moves = list(itertools.product(*[range(size) for size in sizes]))[1:]
    moves.sort(key=lambda m: -sum(min(d, z - d) for d, z in zip(m, sizes)))
    lines = []
    for i, size in enumerate(sizes):
        rest = sum(table[0] for j, table in enumerate(tables) if j != i)
        lines.append([rest + tables[i][d] for d in range(1, size)])
    return [sum(table[d] for table, d in zip(tables, m)) for m in moves], lines


def kernel(
    n_pos,
    n_freq,
    foot_in,
    weight_in,
    conduct_in,
    base_in,
    basis_ref,
    out_ref,
    foot_ref,
    weight_ref,
    conduct_ref,
    base_ref,
    in_sem,
    lat_v,
    dep_v,
    basis_v,
    green_s,
    send_b,
    recv_b,
    packed,
    arrived,
    value_b,
    value_r,
    halo_b,
    halo_r,
    basis_sem,
    ring_send,
    ring_recv,
    a2a_send,
    a2a_recv,
    val_send,
    val_recv,
    halo_send,
    halo_recv,
    rounds,
):
    pos = lax.axis_index("pos")
    freq = lax.axis_index("freq")
    pos_local, freq_local, doubled, rank = basis_ref.shape
    elements = doubled // 2
    freqs = freq_local * n_freq
    foot = foot_ref.shape[0]
    rows = foot * TH
    pair = rows // 2
    entries = pos_local * foot
    positions = pos_local * n_pos
    half = n_freq // 2
    messages = 4 * half - 2
    iota = lax.broadcasted_iota
    f32, bf16, i32 = jnp.float32, jnp.bfloat16, jnp.int32

    basis_loads = [
        [
            pltpu.make_async_copy(basis_ref.at[p, f], basis_v.at[p, f], basis_sem.at[p, f])
            for f in range(freq_local)
        ]
        for p in range(pos_local)
    ]
    rows_at = {dp: (pos + dp + n_pos) % n_pos if dp else pos for dp in (-1, 0, 1)}
    cols_at = [(freq + df) % n_freq for df in range(n_freq)]

    def other(dp, df):
        return (rows_at[dp], cols_at[df % n_freq] if isinstance(df, int) else (freq + df + n_freq) % n_freq)

    barrier = pltpu.get_barrier_semaphore()
    walks, lines = walks_of(pos, n_pos)
    greeted = [other(0, 1), other(0, -1)] + [(target, freq) for line in lines for target in line]
    for peer in greeted:
        pl.semaphore_signal(barrier, inc=1, device_id=peer, device_id_type=MESH)

    stages = [[other(0, 1), other(0, -1)]] * (n_freq // 2 - 1)
    stages += [[(target, freq) for target in line] for line in lines[1:]]

    def round_signal(i):
        for peer in stages[i]:
            pl.semaphore_signal(rounds.at[i], inc=1, device_id=peer, device_id_type=MESH)

    def round_wait(i):
        pl.semaphore_wait(rounds.at[i], len(stages[i]))

    foot_load, *small_loads = [
        pltpu.make_async_copy(src, dst, in_sem.at[i])
        for i, (src, dst) in enumerate(
            (
                (foot_in, foot_ref),
                (conduct_in, conduct_ref),
                (base_in, base_ref),
                (weight_in, weight_ref),
            )
        )
    ]
    foot_load.start()
    for p in range(pos_local):
        for copy in basis_loads[p]:
            copy.start()
    for copy in small_loads:
        copy.start()

    def wait_all(ref, sem):
        pltpu.make_async_copy(ref, ref, sem).wait()

    near = [(dp, df) for dp in (-1, 0, 1) for df in range(n_freq) if (dp, df) != (0, 0)]
    near.sort(key=lambda d: -min(d[1], n_freq - d[1]) - abs(d[0]) * 0.5)

    expand = iota(i32, (rows, foot), 0) % foot == iota(i32, (rows, foot), 1)
    expand = jnp.where(expand, 1.0, 0.0).astype(bf16)
    foot_load.wait()
    foot_all = foot_ref[...]
    foot_owner = (foot_all // TILE_DEV).astype(f32)
    foot_local = (foot_all % TILE_DEV).astype(f32)
    owner_of = jnp.dot(expand, foot_owner.astype(bf16), preferred_element_type=f32)
    local_of = jnp.dot(expand, foot_local.astype(bf16), preferred_element_type=f32)
    corner = iota(i32, (rows, 1), 0) // foot
    which = iota(i32, (rows, positions), 1)

    def locate(p):
        position = pos * pos_local + p
        owner = jnp.sum(jnp.where(which == position, owner_of, 0.0), axis=1, keepdims=True)
        local = jnp.sum(jnp.where(which == position, local_of, 0.0), axis=1, keepdims=True)
        depth = (TOP + CELL * (owner.astype(i32) * TH + corner)).astype(f32)
        centre = position * (CELL * TW * TILE_DEV // positions)
        lateral = CELL * TW * local.astype(i32) - centre
        lat_v[p] = (lateral - PITCH * iota(i32, (rows, LANES), 1)).astype(f32)
        dep_v[p] = jnp.broadcast_to(depth * depth, (rows, LANES))

    locate(0)

    rates = [
        (freqs // 2 + freq * freq_local + f).astype(f32) * (UNIT / freqs) for f in range(freq_local)
    ]
    unit = make_unit(lat_v, dep_v, basis_v, green_s, rates, elements)

    def compute(u, base=0, height=rows):
        way = 1 - 2 * (u % 2)
        dist = half - (u + 2) // 4
        p = (u + 1) // 2 % 2
        done = unit((freq + way * dist + n_freq) % n_freq, p, base, height)
        for h in range(2):
            send_b[u, h, base : base + height, :] = done[:, h * LANES : (h + 1) * LANES]

    def ring_copy(u):
        return pltpu.make_async_remote_copy(
            src_ref=send_b.at[u],
            dst_ref=recv_b.at[u],
            send_sem=ring_send,
            recv_sem=ring_recv.at[u, 0],
            device_id=other(0, 1 - 2 * lax.rem(u, 2)),
            device_id_type=MESH,
        )

    def ring_part(u, c):
        span = pl.ds((c % 2) * pair, pair)
        return pltpu.make_async_remote_copy(
            src_ref=send_b.at[u, c // 2, span, :],
            dst_ref=recv_b.at[u, c // 2, span, :],
            send_sem=ring_send,
            recv_sem=ring_recv.at[u, c],
            device_id=other(0, 1 - 2 * lax.rem(u, 2)),
            device_id_type=MESH,
        )

    def ring_early(u, base):
        span = pl.ds(base, pair)
        return pltpu.make_async_remote_copy(
            src_ref=send_b.at[u, :, span, :],
            dst_ref=recv_b.at[u, :, span, :],
            send_sem=ring_send,
            recv_sem=ring_recv.at[u, 0],
            device_id=other(0, 1 - 2 * u),
            device_id_type=MESH,
        )

    for copy in basis_loads[0]:
        copy.wait()
    compute(0, 0, pair)
    pl.semaphore_wait(barrier, len(greeted))
    ring_early(0, 0).start()
    for p in range(1, pos_local):
        locate(p)
        for copy in basis_loads[p]:
            copy.wait()
    for u, base in ((1, 0), (0, pair), (1, pair)):
        compute(u, base, pair)
        ring_early(u, base).start()

    for copy in small_loads:
        copy.wait()
    cols = base_ref.shape[1]
    halo_b[...] = jnp.zeros(halo_b.shape, f32)
    halo_b[0:TH, 0:cols] = conduct_ref[0]
    halo_b[TH : 2 * TH, 0:cols] = conduct_ref[1]
    halo_b[2 * TH : 3 * TH, 0:cols] = base_ref[...]
    halo_peers = [(dp, df) for dp in (-1, 0, 1) for df in (-1, 0, 1) if (dp, df) != (0, 0)]

    def halo_copy(i, dp, df):
        return pltpu.make_async_remote_copy(
            src_ref=halo_b,
            dst_ref=halo_r.at[(1 - dp) * 3 + (1 - df)],
            send_sem=halo_send,
            recv_sem=halo_recv,
            device_id=other(dp, df),
            device_id_type=MESH,
        )

    @pl.loop(2, messages + 2)
    def _(u):
        compute(u)

        @pl.when((u >= 4) & (u < messages))
        def _():
            ring_copy(u - 4).wait_recv()
            send_b[u] += recv_b[u - 4]

        @pl.when(u < messages - 4)
        def _():
            ring_copy(u).start()

        @pl.when((u >= messages - 4) & (u < messages))
        def _():
            ring_part(u, 0).start()
            ring_part(u, 1).start()

        @pl.when((u >= messages - 2) & (u < messages))
        def _():
            for c in range(2, PARTS):
                ring_part(u - 2, c).start()
                ring_part(u, c).start()

        for i in range(len(stages)):

            @pl.when(u == 4 + i)
            def _():
                if i > 0:
                    round_wait(i - 1)
                round_signal(i)

        @pl.when(u == 4 + len(stages))
        def _():
            round_wait(len(stages) - 1)
            for i, (dp, df) in enumerate(halo_peers):
                halo_copy(i, dp, df).start()

    outs = n_pos * CAP * 2
    width = pos_local * 2 * foot
    picks = iota(i32, (foot, positions), 1)
    owner_col = jnp.concatenate(
        [
            jnp.sum(jnp.where(picks == pos * pos_local + p, foot_owner, 0.0), axis=1, keepdims=True)
            for p in range(pos_local)
        ],
        axis=0,
    )
    lane = iota(i32, (entries, width), 1)
    entry_of_lane = lane // (2 * foot) * foot + lane % foot
    entry = iota(i32, (entries, width), 0)
    owner_row = jnp.sum(jnp.where(entry == entry_of_lane, owner_col, 0.0), axis=0, keepdims=True)
    same = (owner_col == owner_row) & (entry < entry_of_lane)
    order_row = jnp.sum(jnp.where(same, 1.0, 0.0), axis=0, keepdims=True)
    slot_row = owner_row * CAP + order_row
    to_row = iota(i32, (outs, width), 0)
    from_lane = iota(i32, (outs, width), 1)
    slot_out = (to_row // (2 * CAP) * CAP + to_row % CAP).astype(f32)
    gather = (slot_out == slot_row) & (to_row // CAP % 2 == from_lane // foot % 2)
    gather = jnp.where(gather, 1.0, 0.0).astype(bf16)
    gather = jnp.concatenate([gather] * 3, axis=1)

    mine = foot_owner == pos.astype(f32)
    mine_b = jnp.where(mine, 1.0, 0.0).astype(bf16)
    lower = iota(i32, (foot, foot), 1) < iota(i32, (foot, foot), 0)
    from_p = iota(i32, (positions, positions), 0)
    to_p = iota(i32, (positions, positions), 1)
    later = (from_p // pos_local == to_p // pos_local) & (from_p < to_p)
    moved = jnp.dot(mine_b, jnp.where(later, 1.0, 0.0).astype(bf16), preferred_element_type=f32)
    ahead = jnp.dot(
        jnp.where(lower, 1.0, 0.0).astype(bf16), mine_b, preferred_element_type=f32
    ) + jnp.sum(moved, axis=0, keepdims=True)
    found = jnp.concatenate(
        [
            jnp.sum(jnp.where(mine & (ahead == s), foot_local + 1.0, 0.0), axis=0, keepdims=True)
            for s in range(CAP)
        ],
        axis=0,
    )
    block_of = iota(i32, (positions, outs), 0) // pos_local
    block_to = iota(i32, (positions, outs), 1) // (2 * CAP)
    table = jnp.dot(
        found.astype(bf16),
        jnp.where(block_of == block_to, 1.0, 0.0).astype(bf16),
        preferred_element_type=f32,
    )
    turn = iota(i32, (CAP, outs), 1) % CAP == iota(i32, (CAP, outs), 0)
    tile_in = jnp.sum(jnp.where(turn, table, 0.0), axis=0, keepdims=True)
    row_in = iota(i32, (1, outs), 1) // CAP % 2
    target_row = jnp.where(tile_in > 0.0, tile_in - 1.0 + (TILE_DEV * row_in).astype(f32), -1.0)
    place = iota(i32, (2 * TILE_DEV, outs), 0).astype(f32) == target_row
    place = jnp.where(place, 1.0, 0.0).astype(bf16)
    place = jnp.concatenate([place] * 3, axis=1)

    wait_all(halo_r.at[pl.ds(0, 8)], halo_recv)
    lane16 = iota(i32, (16, LANES), 1)
    row16 = iota(i32, (16, LANES), 0)
    strips = []
    for dp in (-1, 0, 1):
        left = halo_r[(dp + 1) * 3]
        centre = halo_b[...] if dp == 0 else halo_r[(dp + 1) * 3 + 1]
        right = halo_r[(dp + 1) * 3 + 2]
        strip = jnp.where(
            lane16 < PASSES,
            pltpu.roll(left, LANES - cols + PASSES, 1),
            jnp.where(
                lane16 < cols + PASSES,
                pltpu.roll(centre, PASSES, 1),
                pltpu.roll(right, cols + PASSES, 1),
            ),
        )
        strips.append(strip)
    grid_row = row16 + TH * (pos - 1)
    grid_col = lane16 + (cols * freq - PASSES)
    inside = (grid_row >= 0) & (grid_row < TH * n_pos) & (grid_col >= 0) & (grid_col < TILE_DEV * TW)
    inside = inside & (row16 < 3 * TH) & (lane16 < cols + 2 * PASSES)

    def widened(a):
        pieces = [strip[a * TH : (a + 1) * TH, :] for strip in strips]
        tall = jnp.concatenate(pieces + [pieces[0]], axis=0)
        return jnp.where(inside, tall, 0.0)

    across_k = widened(0)
    along_k = widened(1)
    ground = widened(2)
    south_k = jnp.minimum(across_k, pltpu.roll(across_k, 15, 0))
    north_k = jnp.minimum(across_k, pltpu.roll(across_k, 1, 0))
    east_k = jnp.minimum(along_k, pltpu.roll(along_k, LANES - 1, 1))
    west_k = jnp.minimum(along_k, pltpu.roll(along_k, 1, 1))

    block = 2 * CAP
    own_block = pl.ds(pl.multiple_of(pos * block, block), block)

    def owner_copy(target, c):
        return pltpu.make_async_remote_copy(
            src_ref=packed.at[c, pl.ds(pl.multiple_of(target * block, block), block), :],
            dst_ref=arrived.at[c, own_block, :],
            send_sem=a2a_send,
            recv_sem=a2a_recv.at[c],
            device_id=(target, freq),
            device_id_type=MESH,
        )

    for c in range(PARTS):
        span = pl.ds((c % 2) * pair, pair)
        sums = []
        for own, right, left in (
            (messages + 1, messages - 2, messages - 3),
            (messages, messages - 4, messages - 1),
        ):
            ring_part(right, c).wait_recv()
            ring_part(left, c).wait_recv()
            sums.append(send_b[own, c // 2, span, :] + recv_b[right, c // 2, span, :] + recv_b[left, c // 2, span, :])
        stacked = jnp.concatenate(split3(jnp.concatenate(sums, axis=0)), axis=0)
        packed[c] = jnp.dot(gather, stacked, preferred_element_type=f32)

        for target in walks:
            owner_copy(target, c).start()
        pltpu.make_async_copy(
            packed.at[c, own_block, :], arrived.at[c, own_block, :], a2a_recv.at[c]
        ).start()

    energies = [None, None]
    for c in range(PARTS):
        wait_all(arrived.at[c], a2a_recv.at[c])
        stacked = jnp.concatenate(split3(arrived[c]), axis=0)
        compound = jnp.dot(place, stacked, preferred_element_type=f32)
        scaled = compound * compound * weight_ref[0:1, (c // 2) * LANES : (c // 2 + 1) * LANES]
        energies[c % 2] = scaled if energies[c % 2] is None else energies[c % 2] + scaled
    value = jnp.zeros((1, LANES), f32)
    for pair_at, energy in enumerate(energies):
        energy = jnp.sum(energy, axis=1, keepdims=True)
        on = iota(i32, (2 * TILE_DEV, LANES), 1) == iota(i32, (2 * TILE_DEV, LANES), 0) + pair_at * 2 * TILE_DEV
        value = value + jnp.sum(jnp.where(on, energy, 0.0), axis=0, keepdims=True)
    value_b[...] = jnp.sqrt(value / rank + EPS)

    def value_copy(i, dp, df):
        return pltpu.make_async_remote_copy(
            src_ref=value_b,
            dst_ref=value_r.at[(1 - dp) * n_freq + freq],
            send_sem=val_send,
            recv_sem=val_recv,
            device_id=other(dp, df),
            device_id_type=MESH,
        )

    for i, (dp, df) in enumerate(near):
        value_copy(i, dp, df).start()

    value_r[n_freq + freq] = value_b[...]

    wait_all(send_b.at[pl.ds(0, messages)], ring_send)
    wait_all(packed.at[:, pl.ds(0, (n_pos - 1) * block), :], a2a_send)
    wait_all(halo_r.at[pl.ds(0, 8)], halo_send)

    from_r = iota(i32, (LANES, TH * LANES), 0)
    to_n = iota(i32, (LANES, TH * LANES), 1)
    to_col = to_n % LANES + (cols * freq - PASSES) + TW
    chosen = (from_r // TILE_DEV == to_n // LANES) & (from_r % TILE_DEV == to_col // TW - 1)
    spread = jnp.where(chosen, 1.0, 0.0).astype(bf16)
    sub24 = iota(i32, (3 * TW, TH * LANES), 0)
    col24 = iota(i32, (3 * TW, TH * LANES), 1)
    keep = (col24 % LANES + (cols * freq - PASSES) + TW) % TW == sub24 % TW
    sub8 = iota(i32, (TW, LANES), 0)

    wait_all(value_r.at[pl.ds(0, len(near))], val_recv)

    groups = []
    for o in range(3):
        group = jnp.broadcast_to(value_r[o * n_freq], (TW, LANES))
        for col in range(1, n_freq):
            group = jnp.where(sub8 == col, value_r[o * n_freq + col], group)
        groups.append(group)
    wide = None
    for piece in split3(jnp.concatenate(groups, axis=0)):
        part = jnp.dot(piece, spread, preferred_element_type=f32)
        wide = part if wide is None else wide + part
    wide = jnp.where(keep, wide, 0.0)
    field = jnp.zeros((16, LANES), f32)
    for o in range(3):
        summed = jnp.sum(wide[o * TW : (o + 1) * TW, :], axis=0, keepdims=True)
        for r in range(TH):
            field = jnp.where(row16 == o * TH + r, summed[:, r * LANES : (r + 1) * LANES], field)
    u = jnp.where(inside, field + ground, 0.0)
    for sweep in range(PASSES):
        north = north_k * (pltpu.roll(u, 1, 0) - u)
        south = south_k * (pltpu.roll(u, 15, 0) - u)
        west = west_k * (pltpu.roll(u, 1, 1) - u)
        east = east_k * (pltpu.roll(u, LANES - 1, 1) - u)
        u = u + north + south + west + east
    u = pltpu.roll(u, LANES - PASSES, 1)
    out_ref[...] = u[TH : 2 * TH, :cols]

    wait_all(value_r.at[pl.ds(0, len(near))], val_send)


def body(footprint, basis, weights, conduct, baseline):
    pos_local, freq_local, doubled, rank = basis.shape
    foot = footprint.shape[1]
    n_pos = lax.axis_size("pos")
    n_freq = lax.axis_size("freq")
    rows = foot * TH
    outs = n_pos * CAP * 2
    messages = 2 * n_freq - 2
    vmem = pl.BlockSpec(memory_space=pltpu.VMEM)
    hbm = pl.BlockSpec(memory_space=pltpu.MemorySpace.HBM)
    f32, bf16 = jnp.float32, jnp.bfloat16
    return pl.pallas_call(
        functools.partial(kernel, n_pos, n_freq),
        out_shape=jax.ShapeDtypeStruct(baseline.shape, f32),
        in_specs=[hbm] * 5,
        out_specs=vmem,
        scratch_shapes=[
            pltpu.VMEM(footprint.shape[::-1], jnp.int32),
            pltpu.VMEM((1, rank), f32),
            pltpu.VMEM(conduct.shape, f32),
            pltpu.VMEM(baseline.shape, f32),
            pltpu.SemaphoreType.DMA((4,)),
            pltpu.VMEM((pos_local, rows, LANES), f32),
            pltpu.VMEM((pos_local, rows, LANES), f32),
            pltpu.VMEM(basis.shape, bf16),
            pltpu.VMEM((doubled // 2 // LANES, freq_local, rows, 2 * LANES), bf16),
            pltpu.VMEM((messages + 2, 2, rows, LANES), f32),
            pltpu.VMEM((messages, 2, rows, LANES), f32),
            pltpu.VMEM((PARTS, outs, LANES), f32),
            pltpu.VMEM((PARTS, outs, LANES), f32),
            pltpu.VMEM((1, LANES), f32),
            pltpu.VMEM((3 * n_freq, 1, LANES), f32),
            pltpu.VMEM((16, LANES), f32),
            pltpu.VMEM((9, 16, LANES), f32),
            pltpu.SemaphoreType.DMA((pos_local, freq_local)),
            pltpu.SemaphoreType.DMA,
            pltpu.SemaphoreType.DMA((messages, PARTS)),
            pltpu.SemaphoreType.DMA,
            pltpu.SemaphoreType.DMA((PARTS,)),
            pltpu.SemaphoreType.DMA,
            pltpu.SemaphoreType.DMA,
            pltpu.SemaphoreType.DMA,
            pltpu.SemaphoreType.DMA,
            pltpu.SemaphoreType.REGULAR((len(digits_of(n_pos)) + n_freq // 2 - 2,)),
        ],
        compiler_params=pltpu.CompilerParams(
            collective_id=0, has_side_effects=True, vmem_limit_bytes=50 * 1024 * 1024
        ),
    )(*[pltpu.with_memory_space_constraint(x, pltpu.MemorySpace.HBM) for x in (footprint.T, weights.reshape(1, rank), conduct, baseline, basis)])


def solution(mesh):
    return jax.shard_map(
        body,
        mesh=mesh,
        in_specs=(P(), P("pos", "freq", None, None), P(), P(None, "pos", "freq"), P("pos", "freq")),
        out_specs=P("pos", "freq"),
        check_vma=False,
    )
```

```python
import functools
import itertools

import jax
import jax.numpy as jnp
from jax import lax
from jax.experimental import pallas as pl
from jax.experimental.pallas import tpu as pltpu
from jax.sharding import PartitionSpec as P

TH = 4
TW = 8
CELLS = TH * TW
TILE_DEV = 32
PASSES = 3
CAP = 4
EPS = 1e-06
MESH = pl.DeviceIdType.MESH

UNIT = 0.025
CELL = 28
PITCH = 5
TOP = 160
SIN_POLY = (-4.547240826688576, 9.23637803174852, -5.615372827081364)
SCALE_SQ = 0.6259964781564749
DOUBLE = (2.0 + 1e-6) / SCALE_SQ
LANES = 128


def green_block(cross, depth_sq, turns):
    square = cross * cross + depth_sq
    dist = square * lax.rsqrt(square)
    root = lax.rsqrt(dist)
    amp = root * (TOP**0.5)
    scaled_amp = root * (TOP**0.5 * SCALE_SQ)
    out = []
    for rate in turns:
        phase = dist * rate
        x = jnp.round(phase) - phase
        z = x * x
        s = x * (((z + SIN_POLY[0]) * z + SIN_POLY[1]) * z + SIN_POLY[2])
        w = DOUBLE - s * s
        u = w * scaled_amp
        out.append(((u - amp).astype(jnp.bfloat16), (u * s * lax.rsqrt(w)).astype(jnp.bfloat16)))
    return out


def make_unit(lat_ref, dep_ref, basis_v, green_s, rates, elements):
    rows = lat_ref.shape[1]

    def unit(col, p, base=0, height=rows):
        total = None
        for tile in range(elements // LANES):
            start = tile * LANES
            shift = (2 * CELL * col + (PITCH * (elements - 1) - 2 * PITCH * start)).astype(jnp.float32) * 0.5
            for rg in range(base // 16, (base + height) // 16):
                span = pl.ds(rg * 16, 16)
                values = green_block(lat_ref[p, span, :] + shift, dep_ref[p, span, :], rates)
                for f, (cosine, sine) in enumerate(values):
                    green_s[tile, f, span, 0:LANES] = cosine
                    green_s[tile, f, span, LANES : 2 * LANES] = sine
            for f in range(len(rates)):
                right = jnp.concatenate(
                    [
                        basis_v[p, f, start : start + LANES, :],
                        basis_v[p, f, elements + start : elements + start + LANES, :],
                    ],
                    axis=0,
                )
                part = jnp.dot(
                    green_s[tile, f, base : base + height, :], right, preferred_element_type=jnp.float32
                )
                total = part if total is None else total + part
        return total

    return unit


def split3(x):
    hi = x.astype(jnp.bfloat16)
    rest = x - hi.astype(jnp.float32)
    mid = rest.astype(jnp.bfloat16)
    low = (rest - mid.astype(jnp.float32)).astype(jnp.bfloat16)
    return hi, mid, low


PARTS = 4


def digits_of(n_pos):
    return {32: (4, 4, 2), 8: (2, 2, 2)}[n_pos]


def walks_of(pos, n_pos):
    sizes = digits_of(n_pos)
    tables = []
    below = n_pos
    for size in sizes:
        below = below // size
        digit = pos // below % size
        tables.append([(digit + move) % size * below for move in range(size)])
    moves = list(itertools.product(*[range(size) for size in sizes]))[1:]
    moves.sort(key=lambda m: -sum(min(d, z - d) for d, z in zip(m, sizes)))
    lines = []
    for i, size in enumerate(sizes):
        rest = sum(table[0] for j, table in enumerate(tables) if j != i)
        lines.append([rest + tables[i][d] for d in range(1, size)])
    return [sum(table[d] for table, d in zip(tables, m)) for m in moves], lines


def kernel(
    n_pos,
    n_freq,
    foot_in,
    weight_in,
    conduct_in,
    base_in,
    basis_ref,
    out_ref,
    foot_ref,
    weight_ref,
    conduct_ref,
    base_ref,
    in_sem,
    lat_v,
    dep_v,
    basis_v,
    green_s,
    send_b,
    recv_b,
    packed,
    arrived,
    value_b,
    value_r,
    halo_b,
    halo_r,
    basis_sem,
    ring_send,
    ring_recv,
    a2a_send,
    a2a_recv,
    val_send,
    val_recv,
    halo_send,
    halo_recv,
    rounds,
):
    pos = lax.axis_index("pos")
    freq = lax.axis_index("freq")
    pos_local, freq_local, doubled, rank = basis_ref.shape
    elements = doubled // 2
    freqs = freq_local * n_freq
    foot = foot_ref.shape[0]
    rows = foot * TH
    pair = rows // 2
    entries = pos_local * foot
    positions = pos_local * n_pos
    half = n_freq // 2
    messages = 4 * half - 2
    iota = lax.broadcasted_iota
    f32, bf16, i32 = jnp.float32, jnp.bfloat16, jnp.int32

    basis_loads = [
        [
            pltpu.make_async_copy(basis_ref.at[p, f], basis_v.at[p, f], basis_sem.at[p, f])
            for f in range(freq_local)
        ]
        for p in range(pos_local)
    ]
    rows_at = {dp: (pos + dp + n_pos) % n_pos if dp else pos for dp in (-1, 0, 1)}
    cols_at = [(freq + df) % n_freq for df in range(n_freq)]

    def other(dp, df):
        return (rows_at[dp], cols_at[df % n_freq] if isinstance(df, int) else (freq + df + n_freq) % n_freq)

    barrier = pltpu.get_barrier_semaphore()
    walks, lines = walks_of(pos, n_pos)
    greeted = [other(0, 1), other(0, -1)] + [(target, freq) for line in lines for target in line]
    for peer in greeted:
        pl.semaphore_signal(barrier, inc=1, device_id=peer, device_id_type=MESH)

    stages = [[other(0, 1), other(0, -1)]] * (n_freq // 2 - 1)
    stages += [[(target, freq) for target in line] for line in lines[1:]]

    def round_signal(i):
        for peer in stages[i]:
            pl.semaphore_signal(rounds.at[i], inc=1, device_id=peer, device_id_type=MESH)

    def round_wait(i):
        pl.semaphore_wait(rounds.at[i], len(stages[i]))

    foot_load, *small_loads = [
        pltpu.make_async_copy(src, dst, in_sem.at[i])
        for i, (src, dst) in enumerate(
            (
                (foot_in, foot_ref),
                (conduct_in, conduct_ref),
                (base_in, base_ref),
                (weight_in, weight_ref),
            )
        )
    ]
    foot_load.start()
    for p in range(pos_local):
        for copy in basis_loads[p]:
            copy.start()
    for copy in small_loads:
        copy.start()

    def wait_all(ref, sem):
        pltpu.make_async_copy(ref, ref, sem).wait()

    near = [(dp, df) for dp in (-1, 0, 1) for df in range(n_freq) if (dp, df) != (0, 0)]
    near.sort(key=lambda d: -min(d[1], n_freq - d[1]) - abs(d[0]) * 0.5)

    expand = iota(i32, (rows, foot), 0) % foot == iota(i32, (rows, foot), 1)
    expand = jnp.where(expand, 1.0, 0.0).astype(bf16)
    foot_load.wait()
    foot_all = foot_ref[...]
    foot_owner = (foot_all // TILE_DEV).astype(f32)
    foot_local = (foot_all % TILE_DEV).astype(f32)
    owner_of = jnp.dot(expand, foot_owner.astype(bf16), preferred_element_type=f32)
    local_of = jnp.dot(expand, foot_local.astype(bf16), preferred_element_type=f32)
    corner = iota(i32, (rows, 1), 0) // foot
    which = iota(i32, (rows, positions), 1)

    def locate(p):
        position = pos * pos_local + p
        owner = jnp.sum(jnp.where(which == position, owner_of, 0.0), axis=1, keepdims=True)
        local = jnp.sum(jnp.where(which == position, local_of, 0.0), axis=1, keepdims=True)
        depth = (TOP + CELL * (owner.astype(i32) * TH + corner)).astype(f32)
        centre = position * (CELL * TW * TILE_DEV // positions)
        lateral = CELL * TW * local.astype(i32) - centre
        lat_v[p] = (lateral - PITCH * iota(i32, (rows, LANES), 1)).astype(f32)
        dep_v[p] = jnp.broadcast_to(depth * depth, (rows, LANES))

    locate(0)

    rates = [
        (freqs // 2 + freq * freq_local + f).astype(f32) * (UNIT / freqs) for f in range(freq_local)
    ]
    unit = make_unit(lat_v, dep_v, basis_v, green_s, rates, elements)

    def compute(u, base=0, height=rows):
        way = 1 - 2 * (u % 2)
        dist = half - (u + 2) // 4
        p = (u + 1) // 2 % 2
        done = unit((freq + way * dist + n_freq) % n_freq, p, base, height)
        for h in range(2):
            send_b[u, h, base : base + height, :] = done[:, h * LANES : (h + 1) * LANES]

    def ring_copy(u):
        return pltpu.make_async_remote_copy(
            src_ref=send_b.at[u],
            dst_ref=recv_b.at[u],
            send_sem=ring_send,
            recv_sem=ring_recv.at[u, 0],
            device_id=other(0, 1 - 2 * lax.rem(u, 2)),
            device_id_type=MESH,
        )

    def ring_part(u, c):
        span = pl.ds((c % 2) * pair, pair)
        return pltpu.make_async_remote_copy(
            src_ref=send_b.at[u, c // 2, span, :],
            dst_ref=recv_b.at[u, c // 2, span, :],
            send_sem=ring_send,
            recv_sem=ring_recv.at[u, c],
            device_id=other(0, 1 - 2 * lax.rem(u, 2)),
            device_id_type=MESH,
        )

    def ring_early(u, base):
        span = pl.ds(base, pair)
        return pltpu.make_async_remote_copy(
            src_ref=send_b.at[u, :, span, :],
            dst_ref=recv_b.at[u, :, span, :],
            send_sem=ring_send,
            recv_sem=ring_recv.at[u, 0],
            device_id=other(0, 1 - 2 * u),
            device_id_type=MESH,
        )

    for copy in basis_loads[0]:
        copy.wait()
    compute(0, 0, pair)
    pl.semaphore_wait(barrier, len(greeted))
    ring_early(0, 0).start()
    for p in range(1, pos_local):
        locate(p)
        for copy in basis_loads[p]:
            copy.wait()
    for u, base in ((1, 0), (0, pair), (1, pair)):
        compute(u, base, pair)
        ring_early(u, base).start()

    for copy in small_loads:
        copy.wait()
    cols = base_ref.shape[1]
    halo_b[...] = jnp.zeros(halo_b.shape, f32)
    halo_b[0:TH, 0:cols] = conduct_ref[0]
    halo_b[TH : 2 * TH, 0:cols] = conduct_ref[1]
    halo_b[2 * TH : 3 * TH, 0:cols] = base_ref[...]
    halo_peers = [(dp, df) for dp in (-1, 0, 1) for df in (-1, 0, 1) if (dp, df) != (0, 0)]

    def halo_copy(i, dp, df):
        return pltpu.make_async_remote_copy(
            src_ref=halo_b,
            dst_ref=halo_r.at[(1 - dp) * 3 + (1 - df)],
            send_sem=halo_send,
            recv_sem=halo_recv,
            device_id=other(dp, df),
            device_id_type=MESH,
        )

    @pl.loop(2, messages + 2)
    def _(v):
        late = messages - 2
        u = jnp.where(
            v < late - 4,
            v,
            jnp.where(
                v == late - 4,
                messages,
                jnp.where(v <= late, v - 1, jnp.where(v == late + 1, messages + 1, v - 2)),
            ),
        )
        compute(u)

        @pl.when((u >= 4) & (u < messages))
        def _():
            ring_copy(u - 4).wait_recv()
            send_b[u] += recv_b[u - 4]

        @pl.when(u < messages - 4)
        def _():
            ring_copy(u).start()

        @pl.when((u >= messages - 4) & (u < messages))
        def _():
            ring_part(u, 0).start()
            ring_part(u, 1).start()

        @pl.when((u >= messages - 2) & (u < messages))
        def _():
            for c in range(2, PARTS):
                ring_part(u - 2, c).start()
                ring_part(u, c).start()

        for i in range(len(stages)):

            @pl.when(u == 4 + i)
            def _():
                if i > 0:
                    round_wait(i - 1)
                round_signal(i)

        @pl.when(u == 4 + len(stages))
        def _():
            round_wait(len(stages) - 1)
            for i, (dp, df) in enumerate(halo_peers):
                halo_copy(i, dp, df).start()

    outs = n_pos * CAP * 2
    width = pos_local * 2 * foot
    picks = iota(i32, (foot, positions), 1)
    owner_col = jnp.concatenate(
        [
            jnp.sum(jnp.where(picks == pos * pos_local + p, foot_owner, 0.0), axis=1, keepdims=True)
            for p in range(pos_local)
        ],
        axis=0,
    )
    lane = iota(i32, (entries, width), 1)
    entry_of_lane = lane // (2 * foot) * foot + lane % foot
    entry = iota(i32, (entries, width), 0)
    owner_row = jnp.sum(jnp.where(entry == entry_of_lane, owner_col, 0.0), axis=0, keepdims=True)
    same = (owner_col == owner_row) & (entry < entry_of_lane)
    order_row = jnp.sum(jnp.where(same, 1.0, 0.0), axis=0, keepdims=True)
    slot_row = owner_row * CAP + order_row
    to_row = iota(i32, (outs, width), 0)
    from_lane = iota(i32, (outs, width), 1)
    slot_out = (to_row // (2 * CAP) * CAP + to_row % CAP).astype(f32)
    gather = (slot_out == slot_row) & (to_row // CAP % 2 == from_lane // foot % 2)
    gather = jnp.where(gather, 1.0, 0.0).astype(bf16)
    gather = jnp.concatenate([gather] * 3, axis=1)

    mine = foot_owner == pos.astype(f32)
    mine_b = jnp.where(mine, 1.0, 0.0).astype(bf16)
    lower = iota(i32, (foot, foot), 1) < iota(i32, (foot, foot), 0)
    from_p = iota(i32, (positions, positions), 0)
    to_p = iota(i32, (positions, positions), 1)
    later = (from_p // pos_local == to_p // pos_local) & (from_p < to_p)
    moved = jnp.dot(mine_b, jnp.where(later, 1.0, 0.0).astype(bf16), preferred_element_type=f32)
    ahead = jnp.dot(
        jnp.where(lower, 1.0, 0.0).astype(bf16), mine_b, preferred_element_type=f32
    ) + jnp.sum(moved, axis=0, keepdims=True)
    found = jnp.concatenate(
        [
            jnp.sum(jnp.where(mine & (ahead == s), foot_local + 1.0, 0.0), axis=0, keepdims=True)
            for s in range(CAP)
        ],
        axis=0,
    )
    block_of = iota(i32, (positions, outs), 0) // pos_local
    block_to = iota(i32, (positions, outs), 1) // (2 * CAP)
    table = jnp.dot(
        found.astype(bf16),
        jnp.where(block_of == block_to, 1.0, 0.0).astype(bf16),
        preferred_element_type=f32,
    )
    turn = iota(i32, (CAP, outs), 1) % CAP == iota(i32, (CAP, outs), 0)
    tile_in = jnp.sum(jnp.where(turn, table, 0.0), axis=0, keepdims=True)
    row_in = iota(i32, (1, outs), 1) // CAP % 2
    target_row = jnp.where(tile_in > 0.0, tile_in - 1.0 + (TILE_DEV * row_in).astype(f32), -1.0)
    place = iota(i32, (2 * TILE_DEV, outs), 0).astype(f32) == target_row
    place = jnp.where(place, 1.0, 0.0).astype(bf16)
    place = jnp.concatenate([place] * 3, axis=1)

    wait_all(halo_r.at[pl.ds(0, 8)], halo_recv)
    lane16 = iota(i32, (16, LANES), 1)
    row16 = iota(i32, (16, LANES), 0)
    strips = []
    for dp in (-1, 0, 1):
        left = halo_r[(dp + 1) * 3]
        centre = halo_b[...] if dp == 0 else halo_r[(dp + 1) * 3 + 1]
        right = halo_r[(dp + 1) * 3 + 2]
        strip = jnp.where(
            lane16 < PASSES,
            pltpu.roll(left, LANES - cols + PASSES, 1),
            jnp.where(
                lane16 < cols + PASSES,
                pltpu.roll(centre, PASSES, 1),
                pltpu.roll(right, cols + PASSES, 1),
            ),
        )
        strips.append(strip)
    grid_row = row16 + TH * (pos - 1)
    grid_col = lane16 + (cols * freq - PASSES)
    inside = (grid_row >= 0) & (grid_row < TH * n_pos) & (grid_col >= 0) & (grid_col < TILE_DEV * TW)
    inside = inside & (row16 < 3 * TH) & (lane16 < cols + 2 * PASSES)

    def widened(a):
        pieces = [strip[a * TH : (a + 1) * TH, :] for strip in strips]
        tall = jnp.concatenate(pieces + [pieces[0]], axis=0)
        return jnp.where(inside, tall, 0.0)

    across_k = widened(0)
    along_k = widened(1)
    ground = widened(2)
    south_k = jnp.minimum(across_k, pltpu.roll(across_k, 15, 0))
    north_k = jnp.minimum(across_k, pltpu.roll(across_k, 1, 0))
    east_k = jnp.minimum(along_k, pltpu.roll(along_k, LANES - 1, 1))
    west_k = jnp.minimum(along_k, pltpu.roll(along_k, 1, 1))

    block = 2 * CAP
    own_block = pl.ds(pl.multiple_of(pos * block, block), block)

    def owner_copy(target, c):
        return pltpu.make_async_remote_copy(
            src_ref=packed.at[c, pl.ds(pl.multiple_of(target * block, block), block), :],
            dst_ref=arrived.at[c, own_block, :],
            send_sem=a2a_send,
            recv_sem=a2a_recv.at[c],
            device_id=(target, freq),
            device_id_type=MESH,
        )

    for c in range(PARTS):
        span = pl.ds((c % 2) * pair, pair)
        sums = []
        for own, right, left in (
            (messages + 1, messages - 2, messages - 3),
            (messages, messages - 4, messages - 1),
        ):
            ring_part(right, c).wait_recv()
            ring_part(left, c).wait_recv()
            sums.append(send_b[own, c // 2, span, :] + recv_b[right, c // 2, span, :] + recv_b[left, c // 2, span, :])
        stacked = jnp.concatenate(split3(jnp.concatenate(sums, axis=0)), axis=0)
        packed[c] = jnp.dot(gather, stacked, preferred_element_type=f32)

        for target in walks:
            owner_copy(target, c).start()
        pltpu.make_async_copy(
            packed.at[c, own_block, :], arrived.at[c, own_block, :], a2a_recv.at[c]
        ).start()

    energies = [None, None]
    for c in range(PARTS):
        wait_all(arrived.at[c], a2a_recv.at[c])
        stacked = jnp.concatenate(split3(arrived[c]), axis=0)
        compound = jnp.dot(place, stacked, preferred_element_type=f32)
        scaled = compound * compound * weight_ref[0:1, (c // 2) * LANES : (c // 2 + 1) * LANES]
        energies[c % 2] = scaled if energies[c % 2] is None else energies[c % 2] + scaled
    value = jnp.zeros((1, LANES), f32)
    for pair_at, energy in enumerate(energies):
        energy = jnp.sum(energy, axis=1, keepdims=True)
        on = iota(i32, (2 * TILE_DEV, LANES), 1) == iota(i32, (2 * TILE_DEV, LANES), 0) + pair_at * 2 * TILE_DEV
        value = value + jnp.sum(jnp.where(on, energy, 0.0), axis=0, keepdims=True)
    value_b[...] = jnp.sqrt(value / rank + EPS)

    def value_copy(i, dp, df):
        return pltpu.make_async_remote_copy(
            src_ref=value_b,
            dst_ref=value_r.at[(1 - dp) * n_freq + freq],
            send_sem=val_send,
            recv_sem=val_recv,
            device_id=other(dp, df),
            device_id_type=MESH,
        )

    for i, (dp, df) in enumerate(near):
        value_copy(i, dp, df).start()

    value_r[n_freq + freq] = value_b[...]

    wait_all(send_b.at[pl.ds(0, messages)], ring_send)
    wait_all(packed.at[:, pl.ds(0, (n_pos - 1) * block), :], a2a_send)
    wait_all(halo_r.at[pl.ds(0, 8)], halo_send)

    from_r = iota(i32, (LANES, TH * LANES), 0)
    to_n = iota(i32, (LANES, TH * LANES), 1)
    to_col = to_n % LANES + (cols * freq - PASSES) + TW
    chosen = (from_r // TILE_DEV == to_n // LANES) & (from_r % TILE_DEV == to_col // TW - 1)
    spread = jnp.where(chosen, 1.0, 0.0).astype(bf16)
    sub24 = iota(i32, (3 * TW, TH * LANES), 0)
    col24 = iota(i32, (3 * TW, TH * LANES), 1)
    keep = (col24 % LANES + (cols * freq - PASSES) + TW) % TW == sub24 % TW
    sub8 = iota(i32, (TW, LANES), 0)

    wait_all(value_r.at[pl.ds(0, len(near))], val_recv)

    groups = []
    for o in range(3):
        group = jnp.broadcast_to(value_r[o * n_freq], (TW, LANES))
        for col in range(1, n_freq):
            group = jnp.where(sub8 == col, value_r[o * n_freq + col], group)
        groups.append(group)
    wide = None
    for piece in split3(jnp.concatenate(groups, axis=0)):
        part = jnp.dot(piece, spread, preferred_element_type=f32)
        wide = part if wide is None else wide + part
    wide = jnp.where(keep, wide, 0.0)
    field = jnp.zeros((16, LANES), f32)
    for o in range(3):
        summed = jnp.sum(wide[o * TW : (o + 1) * TW, :], axis=0, keepdims=True)
        for r in range(TH):
            field = jnp.where(row16 == o * TH + r, summed[:, r * LANES : (r + 1) * LANES], field)
    u = jnp.where(inside, field + ground, 0.0)
    for sweep in range(PASSES):
        north = north_k * (pltpu.roll(u, 1, 0) - u)
        south = south_k * (pltpu.roll(u, 15, 0) - u)
        west = west_k * (pltpu.roll(u, 1, 1) - u)
        east = east_k * (pltpu.roll(u, LANES - 1, 1) - u)
        u = u + north + south + west + east
    u = pltpu.roll(u, LANES - PASSES, 1)
    out_ref[...] = u[TH : 2 * TH, :cols]

    wait_all(value_r.at[pl.ds(0, len(near))], val_send)


def body(footprint, basis, weights, conduct, baseline):
    pos_local, freq_local, doubled, rank = basis.shape
    foot = footprint.shape[1]
    n_pos = lax.axis_size("pos")
    n_freq = lax.axis_size("freq")
    rows = foot * TH
    outs = n_pos * CAP * 2
    messages = 2 * n_freq - 2
    vmem = pl.BlockSpec(memory_space=pltpu.VMEM)
    hbm = pl.BlockSpec(memory_space=pltpu.MemorySpace.HBM)
    f32, bf16 = jnp.float32, jnp.bfloat16
    return pl.pallas_call(
        functools.partial(kernel, n_pos, n_freq),
        out_shape=jax.ShapeDtypeStruct(baseline.shape, f32),
        in_specs=[hbm] * 5,
        out_specs=vmem,
        scratch_shapes=[
            pltpu.VMEM(footprint.shape[::-1], jnp.int32),
            pltpu.VMEM((1, rank), f32),
            pltpu.VMEM(conduct.shape, f32),
            pltpu.VMEM(baseline.shape, f32),
            pltpu.SemaphoreType.DMA((4,)),
            pltpu.VMEM((pos_local, rows, LANES), f32),
            pltpu.VMEM((pos_local, rows, LANES), f32),
            pltpu.VMEM(basis.shape, bf16),
            pltpu.VMEM((doubled // 2 // LANES, freq_local, rows, 2 * LANES), bf16),
            pltpu.VMEM((messages + 2, 2, rows, LANES), f32),
            pltpu.VMEM((messages, 2, rows, LANES), f32),
            pltpu.VMEM((PARTS, outs, LANES), f32),
            pltpu.VMEM((PARTS, outs, LANES), f32),
            pltpu.VMEM((1, LANES), f32),
            pltpu.VMEM((3 * n_freq, 1, LANES), f32),
            pltpu.VMEM((16, LANES), f32),
            pltpu.VMEM((9, 16, LANES), f32),
            pltpu.SemaphoreType.DMA((pos_local, freq_local)),
            pltpu.SemaphoreType.DMA,
            pltpu.SemaphoreType.DMA((messages, PARTS)),
            pltpu.SemaphoreType.DMA,
            pltpu.SemaphoreType.DMA((PARTS,)),
            pltpu.SemaphoreType.DMA,
            pltpu.SemaphoreType.DMA,
            pltpu.SemaphoreType.DMA,
            pltpu.SemaphoreType.DMA,
            pltpu.SemaphoreType.REGULAR((len(digits_of(n_pos)) + n_freq // 2 - 2,)),
        ],
        compiler_params=pltpu.CompilerParams(
            collective_id=0, has_side_effects=True, vmem_limit_bytes=50 * 1024 * 1024
        ),
    )(*[pltpu.with_memory_space_constraint(x, pltpu.MemorySpace.HBM) for x in (footprint.T, weights.reshape(1, rank), conduct, baseline, basis)])


def solution(mesh):
    return jax.shard_map(
        body,
        mesh=mesh,
        in_specs=(P(), P("pos", "freq", None, None), P(), P(None, "pos", "freq"), P("pos", "freq")),
        out_specs=P("pos", "freq"),
        check_vma=False,
    )
```

```python
import functools
import itertools

import jax
import jax.numpy as jnp
from jax import lax
from jax.experimental import pallas as pl
from jax.experimental.pallas import tpu as pltpu
from jax.sharding import PartitionSpec as P

TH = 4
TW = 8
CELLS = TH * TW
TILE_DEV = 32
PASSES = 3
CAP = 4
EPS = 1e-06
MESH = pl.DeviceIdType.MESH

UNIT = 0.025
CELL = 28
PITCH = 5
TOP = 160
SIN_POLY = (-4.547240826688576, 9.23637803174852, -5.615372827081364)
SCALE_SQ = 0.6259964781564749
DOUBLE = (2.0 + 1e-6) / SCALE_SQ
LANES = 128


def green_block(cross, depth_sq, turns):
    square = cross * cross + depth_sq
    dist = square * lax.rsqrt(square)
    root = lax.rsqrt(dist)
    amp = root * (TOP**0.5)
    scaled_amp = root * (TOP**0.5 * SCALE_SQ)
    out = []
    for rate in turns:
        phase = dist * rate
        x = jnp.round(phase) - phase
        z = x * x
        s = x * (((z + SIN_POLY[0]) * z + SIN_POLY[1]) * z + SIN_POLY[2])
        w = DOUBLE - s * s
        u = w * scaled_amp
        out.append(((u - amp).astype(jnp.bfloat16), (u * s * lax.rsqrt(w)).astype(jnp.bfloat16)))
    return out


def make_unit(lat_ref, dep_ref, basis_v, green_s, rates, elements):
    rows = lat_ref.shape[1]

    def unit(col, p, base=0, height=rows):
        total = None
        for tile in range(elements // LANES):
            start = tile * LANES
            shift = (2 * CELL * col + (PITCH * (elements - 1) - 2 * PITCH * start)).astype(jnp.float32) * 0.5
            for rg in range(base // 16, (base + height) // 16):
                span = pl.ds(rg * 16, 16)
                values = green_block(lat_ref[p, span, :] + shift, dep_ref[p, span, :], rates)
                for f, (cosine, sine) in enumerate(values):
                    green_s[tile, f, span, 0:LANES] = cosine
                    green_s[tile, f, span, LANES : 2 * LANES] = sine
            for f in range(len(rates)):
                right = jnp.concatenate(
                    [
                        basis_v[p, f, start : start + LANES, :],
                        basis_v[p, f, elements + start : elements + start + LANES, :],
                    ],
                    axis=0,
                )
                part = jnp.dot(
                    green_s[tile, f, base : base + height, :], right, preferred_element_type=jnp.float32
                )
                total = part if total is None else total + part
        return total

    return unit


def split3(x):
    hi = x.astype(jnp.bfloat16)
    rest = x - hi.astype(jnp.float32)
    mid = rest.astype(jnp.bfloat16)
    low = (rest - mid.astype(jnp.float32)).astype(jnp.bfloat16)
    return hi, mid, low


PARTS = 4


def digits_of(n_pos):
    return {32: (4, 4, 2), 8: (2, 2, 2)}[n_pos]


def walks_of(pos, n_pos):
    sizes = digits_of(n_pos)
    tables = []
    below = n_pos
    for size in sizes:
        below = below // size
        digit = pos // below % size
        tables.append([(digit + move) % size * below for move in range(size)])
    moves = list(itertools.product(*[range(size) for size in sizes]))[1:]
    moves.sort(key=lambda m: -sum(min(d, z - d) for d, z in zip(m, sizes)))
    lines = []
    for i, size in enumerate(sizes):
        rest = sum(table[0] for j, table in enumerate(tables) if j != i)
        lines.append([rest + tables[i][d] for d in range(1, size)])
    return [sum(table[d] for table, d in zip(tables, m)) for m in moves], lines


def kernel(
    n_pos,
    n_freq,
    foot_in,
    weight_in,
    conduct_in,
    base_in,
    basis_ref,
    out_ref,
    foot_ref,
    weight_ref,
    conduct_ref,
    base_ref,
    in_sem,
    lat_v,
    dep_v,
    basis_v,
    green_s,
    send_b,
    recv_b,
    packed,
    arrived,
    value_b,
    value_r,
    halo_b,
    halo_r,
    basis_sem,
    ring_send,
    ring_recv,
    a2a_send,
    a2a_recv,
    val_send,
    val_recv,
    halo_send,
    halo_recv,
    rounds,
):
    pos = lax.axis_index("pos")
    freq = lax.axis_index("freq")
    pos_local, freq_local, doubled, rank = basis_ref.shape
    elements = doubled // 2
    freqs = freq_local * n_freq
    foot = foot_ref.shape[0]
    rows = foot * TH
    pair = rows // 2
    entries = pos_local * foot
    positions = pos_local * n_pos
    half = n_freq // 2
    messages = 4 * half - 2
    iota = lax.broadcasted_iota
    f32, bf16, i32 = jnp.float32, jnp.bfloat16, jnp.int32

    basis_loads = [
        [
            pltpu.make_async_copy(basis_ref.at[p, f], basis_v.at[p, f], basis_sem.at[p, f])
            for f in range(freq_local)
        ]
        for p in range(pos_local)
    ]
    rows_at = {dp: (pos + dp + n_pos) % n_pos if dp else pos for dp in (-1, 0, 1)}
    cols_at = [(freq + df) % n_freq for df in range(n_freq)]

    def other(dp, df):
        return (rows_at[dp], cols_at[df % n_freq] if isinstance(df, int) else (freq + df + n_freq) % n_freq)

    barrier = pltpu.get_barrier_semaphore()
    walks, lines = walks_of(pos, n_pos)
    greeted = [other(0, 1), other(0, -1)] + [(target, freq) for line in lines for target in line]
    for peer in greeted:
        pl.semaphore_signal(barrier, inc=1, device_id=peer, device_id_type=MESH)

    stages = [[other(0, 1), other(0, -1)]] * (n_freq // 2 - 1)
    stages += [[(target, freq) for target in line] for line in lines[1:]]

    def round_signal(i):
        for peer in stages[i]:
            pl.semaphore_signal(rounds.at[i], inc=1, device_id=peer, device_id_type=MESH)

    def round_wait(i):
        pl.semaphore_wait(rounds.at[i], len(stages[i]))

    foot_load, *small_loads = [
        pltpu.make_async_copy(src, dst, in_sem.at[i])
        for i, (src, dst) in enumerate(
            (
                (foot_in, foot_ref),
                (conduct_in, conduct_ref),
                (base_in, base_ref),
                (weight_in, weight_ref),
            )
        )
    ]
    foot_load.start()
    for p in range(pos_local):
        for copy in basis_loads[p]:
            copy.start()
    for copy in small_loads:
        copy.start()

    def wait_all(ref, sem):
        pltpu.make_async_copy(ref, ref, sem).wait()

    near = [(dp, df) for dp in (-1, 0, 1) for df in range(n_freq) if (dp, df) != (0, 0)]
    near.sort(key=lambda d: -min(d[1], n_freq - d[1]) - abs(d[0]) * 0.5)

    expand = iota(i32, (rows, foot), 0) % foot == iota(i32, (rows, foot), 1)
    expand = jnp.where(expand, 1.0, 0.0).astype(bf16)
    foot_load.wait()
    foot_all = foot_ref[...]
    foot_owner = (foot_all // TILE_DEV).astype(f32)
    foot_local = (foot_all % TILE_DEV).astype(f32)
    owner_of = jnp.dot(expand, foot_owner.astype(bf16), preferred_element_type=f32)
    local_of = jnp.dot(expand, foot_local.astype(bf16), preferred_element_type=f32)
    corner = iota(i32, (rows, 1), 0) // foot
    which = iota(i32, (rows, positions), 1)

    def locate(p):
        position = pos * pos_local + p
        owner = jnp.sum(jnp.where(which == position, owner_of, 0.0), axis=1, keepdims=True)
        local = jnp.sum(jnp.where(which == position, local_of, 0.0), axis=1, keepdims=True)
        depth = (TOP + CELL * (owner.astype(i32) * TH + corner)).astype(f32)
        centre = position * (CELL * TW * TILE_DEV // positions)
        lateral = CELL * TW * local.astype(i32) - centre
        lat_v[p] = (lateral - PITCH * iota(i32, (rows, LANES), 1)).astype(f32)
        dep_v[p] = jnp.broadcast_to(depth * depth, (rows, LANES))

    locate(0)

    rates = [
        (freqs // 2 + freq * freq_local + f).astype(f32) * (UNIT / freqs) for f in range(freq_local)
    ]
    unit = make_unit(lat_v, dep_v, basis_v, green_s, rates, elements)

    def compute(u, base=0, height=rows):
        way = 1 - 2 * (u % 2)
        dist = half - (u + 2) // 4
        p = (u + 1) // 2 % 2
        done = unit((freq + way * dist + n_freq) % n_freq, p, base, height)
        for h in range(2):
            send_b[u, h, base : base + height, :] = done[:, h * LANES : (h + 1) * LANES]

    def ring_copy(u):
        return pltpu.make_async_remote_copy(
            src_ref=send_b.at[u],
            dst_ref=recv_b.at[u],
            send_sem=ring_send,
            recv_sem=ring_recv.at[u, 0],
            device_id=other(0, 1 - 2 * lax.rem(u, 2)),
            device_id_type=MESH,
        )

    def ring_part(u, c):
        span = pl.ds((c % 2) * pair, pair)
        return pltpu.make_async_remote_copy(
            src_ref=send_b.at[u, c // 2, span, :],
            dst_ref=recv_b.at[u, c // 2, span, :],
            send_sem=ring_send,
            recv_sem=ring_recv.at[u, c],
            device_id=other(0, 1 - 2 * lax.rem(u, 2)),
            device_id_type=MESH,
        )

    def ring_early(u, base):
        span = pl.ds(base, pair)
        return pltpu.make_async_remote_copy(
            src_ref=send_b.at[u, :, span, :],
            dst_ref=recv_b.at[u, :, span, :],
            send_sem=ring_send,
            recv_sem=ring_recv.at[u, 0],
            device_id=other(0, 1 - 2 * u),
            device_id_type=MESH,
        )

    for copy in basis_loads[0]:
        copy.wait()
    compute(0, 0, pair)
    pl.semaphore_wait(barrier, len(greeted))
    ring_early(0, 0).start()
    for p in range(1, pos_local):
        locate(p)
        for copy in basis_loads[p]:
            copy.wait()
    for u, base in ((1, 0), (0, pair), (1, pair)):
        compute(u, base, pair)
        ring_early(u, base).start()

    for copy in small_loads:
        copy.wait()
    cols = base_ref.shape[1]
    halo_b[...] = jnp.zeros(halo_b.shape, f32)
    halo_b[0:TH, 0:cols] = conduct_ref[0]
    halo_b[TH : 2 * TH, 0:cols] = conduct_ref[1]
    halo_b[2 * TH : 3 * TH, 0:cols] = base_ref[...]
    halo_peers = [(dp, df) for dp in (-1, 0, 1) for df in (-1, 0, 1) if (dp, df) != (0, 0)]

    def halo_copy(i, dp, df):
        return pltpu.make_async_remote_copy(
            src_ref=halo_b,
            dst_ref=halo_r.at[(1 - dp) * 3 + (1 - df)],
            send_sem=halo_send,
            recv_sem=halo_recv,
            device_id=other(dp, df),
            device_id_type=MESH,
        )

    @pl.loop(2, messages + 2)
    def _(u):
        compute(u)

        @pl.when((u >= 4) & (u < messages))
        def _():
            ring_copy(u - 4).wait_recv()
            send_b[u] += recv_b[u - 4]

        @pl.when(u < messages - 4)
        def _():
            ring_copy(u).start()

        @pl.when((u >= messages - 4) & (u < messages))
        def _():
            ring_part(u, 0).start()
            ring_part(u, 1).start()

        @pl.when((u >= messages - 2) & (u < messages))
        def _():
            for c in range(2, PARTS):
                ring_part(u - 2, c).start()
                ring_part(u, c).start()

        for i in range(len(stages)):

            @pl.when(u == 4 + i)
            def _():
                if i > 0:
                    round_wait(i - 1)
                round_signal(i)

        @pl.when(u == 4 + len(stages))
        def _():
            round_wait(len(stages) - 1)
            for i, (dp, df) in enumerate(halo_peers):
                halo_copy(i, dp, df).start()

    outs = n_pos * CAP * 2
    width = pos_local * 2 * foot
    picks = iota(i32, (foot, positions), 1)
    owner_col = jnp.concatenate(
        [
            jnp.sum(jnp.where(picks == pos * pos_local + p, foot_owner, 0.0), axis=1, keepdims=True)
            for p in range(pos_local)
        ],
        axis=0,
    )
    lane = iota(i32, (entries, width), 1)
    entry_of_lane = lane // (2 * foot) * foot + lane % foot
    entry = iota(i32, (entries, width), 0)
    owner_row = jnp.sum(jnp.where(entry == entry_of_lane, owner_col, 0.0), axis=0, keepdims=True)
    same = (owner_col == owner_row) & (entry < entry_of_lane)
    order_row = jnp.sum(jnp.where(same, 1.0, 0.0), axis=0, keepdims=True)
    slot_row = owner_row * CAP + order_row
    to_row = iota(i32, (outs, width), 0)
    from_lane = iota(i32, (outs, width), 1)
    slot_out = (to_row // (2 * CAP) * CAP + to_row % CAP).astype(f32)
    gather = (slot_out == slot_row) & (to_row // CAP % 2 == from_lane // foot % 2)
    gather = jnp.where(gather, 1.0, 0.0).astype(bf16)
    gather = jnp.concatenate([gather] * 3, axis=1)

    mine = foot_owner == pos.astype(f32)
    mine_b = jnp.where(mine, 1.0, 0.0).astype(bf16)
    lower = iota(i32, (foot, foot), 1) < iota(i32, (foot, foot), 0)
    from_p = iota(i32, (positions, positions), 0)
    to_p = iota(i32, (positions, positions), 1)
    later = (from_p // pos_local == to_p // pos_local) & (from_p < to_p)
    moved = jnp.dot(mine_b, jnp.where(later, 1.0, 0.0).astype(bf16), preferred_element_type=f32)
    ahead = jnp.dot(
        jnp.where(lower, 1.0, 0.0).astype(bf16), mine_b, preferred_element_type=f32
    ) + jnp.sum(moved, axis=0, keepdims=True)
    found = jnp.concatenate(
        [
            jnp.sum(jnp.where(mine & (ahead == s), foot_local + 1.0, 0.0), axis=0, keepdims=True)
            for s in range(CAP)
        ],
        axis=0,
    )
    block_of = iota(i32, (positions, outs), 0) // pos_local
    block_to = iota(i32, (positions, outs), 1) // (2 * CAP)
    table = jnp.dot(
        found.astype(bf16),
        jnp.where(block_of == block_to, 1.0, 0.0).astype(bf16),
        preferred_element_type=f32,
    )
    turn = iota(i32, (CAP, outs), 1) % CAP == iota(i32, (CAP, outs), 0)
    tile_in = jnp.sum(jnp.where(turn, table, 0.0), axis=0, keepdims=True)
    row_in = iota(i32, (1, outs), 1) // CAP % 2
    target_row = jnp.where(tile_in > 0.0, tile_in - 1.0 + (TILE_DEV * row_in).astype(f32), -1.0)
    place = iota(i32, (2 * TILE_DEV, outs), 0).astype(f32) == target_row
    place = jnp.where(place, 1.0, 0.0).astype(bf16)
    place = jnp.concatenate([place] * 3, axis=1)

    wait_all(halo_r.at[pl.ds(0, 8)], halo_recv)
    lane16 = iota(i32, (16, LANES), 1)
    row16 = iota(i32, (16, LANES), 0)
    strips = []
    for dp in (-1, 0, 1):
        left = halo_r[(dp + 1) * 3]
        centre = halo_b[...] if dp == 0 else halo_r[(dp + 1) * 3 + 1]
        right = halo_r[(dp + 1) * 3 + 2]
        strip = jnp.where(
            lane16 < PASSES,
            pltpu.roll(left, LANES - cols + PASSES, 1),
            jnp.where(
                lane16 < cols + PASSES,
                pltpu.roll(centre, PASSES, 1),
                pltpu.roll(right, cols + PASSES, 1),
            ),
        )
        strips.append(strip)
    grid_row = row16 + TH * (pos - 1)
    grid_col = lane16 + (cols * freq - PASSES)
    inside = (grid_row >= 0) & (grid_row < TH * n_pos) & (grid_col >= 0) & (grid_col < TILE_DEV * TW)
    inside = inside & (row16 < 3 * TH) & (lane16 < cols + 2 * PASSES)

    def widened(a):
        pieces = [strip[a * TH : (a + 1) * TH, :] for strip in strips]
        tall = jnp.concatenate(pieces + [pieces[0]], axis=0)
        return jnp.where(inside, tall, 0.0)

    across_k = widened(0)
    along_k = widened(1)
    ground = widened(2)
    south_k = jnp.minimum(across_k, pltpu.roll(across_k, 15, 0))
    north_k = jnp.minimum(across_k, pltpu.roll(across_k, 1, 0))
    east_k = jnp.minimum(along_k, pltpu.roll(along_k, LANES - 1, 1))
    west_k = jnp.minimum(along_k, pltpu.roll(along_k, 1, 1))

    block = 2 * CAP
    own_block = pl.ds(pl.multiple_of(pos * block, block), block)

    def owner_copy(target, c):
        return pltpu.make_async_remote_copy(
            src_ref=packed.at[c, pl.ds(pl.multiple_of(target * block, block), block), :],
            dst_ref=arrived.at[c, own_block, :],
            send_sem=a2a_send,
            recv_sem=a2a_recv.at[c],
            device_id=(target, freq),
            device_id_type=MESH,
        )

    for c in range(PARTS):
        span = pl.ds((c % 2) * pair, pair)
        sums = []
        for own, right, left in (
            (messages + 1, messages - 2, messages - 3),
            (messages, messages - 4, messages - 1),
        ):
            ring_part(right, c).wait_recv()
            ring_part(left, c).wait_recv()
            sums.append(send_b[own, c // 2, span, :] + recv_b[right, c // 2, span, :] + recv_b[left, c // 2, span, :])
        stacked = jnp.concatenate(split3(jnp.concatenate(sums, axis=0)), axis=0)
        packed[c] = jnp.dot(gather, stacked, preferred_element_type=f32)

        for target in walks:
            owner_copy(target, c).start()
        pltpu.make_async_copy(
            packed.at[c, own_block, :], arrived.at[c, own_block, :], a2a_recv.at[c]
        ).start()

    energies = [None, None]
    for c in range(PARTS):
        wait_all(arrived.at[c], a2a_recv.at[c])
        stacked = jnp.concatenate(split3(arrived[c]), axis=0)
        compound = jnp.dot(place, stacked, preferred_element_type=f32)
        scaled = compound * compound * weight_ref[0:1, (c // 2) * LANES : (c // 2 + 1) * LANES]
        energies[c % 2] = scaled if energies[c % 2] is None else energies[c % 2] + scaled
    value = jnp.zeros((1, LANES), f32)
    for pair_at, energy in enumerate(energies):
        energy = jnp.sum(energy, axis=1, keepdims=True)
        on = iota(i32, (2 * TILE_DEV, LANES), 1) == iota(i32, (2 * TILE_DEV, LANES), 0) + pair_at * 2 * TILE_DEV
        value = value + jnp.sum(jnp.where(on, energy, 0.0), axis=0, keepdims=True)
    value_b[...] = jnp.sqrt(value / rank + EPS)

    def value_copy(i, dp, df):
        return pltpu.make_async_remote_copy(
            src_ref=value_b,
            dst_ref=value_r.at[(1 - dp) * n_freq + freq],
            send_sem=val_send,
            recv_sem=val_recv,
            device_id=other(dp, df),
            device_id_type=MESH,
        )

    for i, (dp, df) in enumerate(near):
        value_copy(i, dp, df).start()

    value_r[n_freq + freq] = value_b[...]

    wait_all(send_b.at[pl.ds(0, messages)], ring_send)
    wait_all(packed.at[:, pl.ds(0, (n_pos - 1) * block), :], a2a_send)
    wait_all(halo_r.at[pl.ds(0, 8)], halo_send)

    from_r = iota(i32, (LANES, TH * LANES), 0)
    to_n = iota(i32, (LANES, TH * LANES), 1)
    to_col = to_n % LANES + (cols * freq - PASSES) + TW
    chosen = (from_r // TILE_DEV == to_n // LANES) & (from_r % TILE_DEV == to_col // TW - 1)
    spread = jnp.where(chosen, 1.0, 0.0).astype(bf16)
    sub24 = iota(i32, (3 * TW, TH * LANES), 0)
    col24 = iota(i32, (3 * TW, TH * LANES), 1)
    keep = (col24 % LANES + (cols * freq - PASSES) + TW) % TW == sub24 % TW
    sub8 = iota(i32, (TW, LANES), 0)

    wait_all(value_r.at[pl.ds(0, len(near))], val_recv)

    groups = []
    for o in range(3):
        group = jnp.broadcast_to(value_r[o * n_freq], (TW, LANES))
        for col in range(1, n_freq):
            group = jnp.where(sub8 == col, value_r[o * n_freq + col], group)
        groups.append(group)
    pieces = jnp.concatenate(split3(jnp.concatenate(groups, axis=0)), axis=1)
    wide = jnp.dot(pieces, jnp.concatenate([spread] * 3, axis=0), preferred_element_type=f32)
    wide = jnp.where(keep, wide, 0.0)
    field = jnp.zeros((16, LANES), f32)
    for o in range(3):
        summed = jnp.sum(wide[o * TW : (o + 1) * TW, :], axis=0, keepdims=True)
        for r in range(TH):
            field = jnp.where(row16 == o * TH + r, summed[:, r * LANES : (r + 1) * LANES], field)
    u = jnp.where(inside, field + ground, 0.0)
    for sweep in range(PASSES):
        north = north_k * (pltpu.roll(u, 1, 0) - u)
        south = south_k * (pltpu.roll(u, 15, 0) - u)
        west = west_k * (pltpu.roll(u, 1, 1) - u)
        east = east_k * (pltpu.roll(u, LANES - 1, 1) - u)
        u = u + north + south + west + east
    u = pltpu.roll(u, LANES - PASSES, 1)
    out_ref[...] = u[TH : 2 * TH, :cols]

    wait_all(value_r.at[pl.ds(0, len(near))], val_send)


def body(footprint, basis, weights, conduct, baseline):
    pos_local, freq_local, doubled, rank = basis.shape
    foot = footprint.shape[1]
    n_pos = lax.axis_size("pos")
    n_freq = lax.axis_size("freq")
    rows = foot * TH
    outs = n_pos * CAP * 2
    messages = 2 * n_freq - 2
    vmem = pl.BlockSpec(memory_space=pltpu.VMEM)
    hbm = pl.BlockSpec(memory_space=pltpu.MemorySpace.HBM)
    f32, bf16 = jnp.float32, jnp.bfloat16
    return pl.pallas_call(
        functools.partial(kernel, n_pos, n_freq),
        out_shape=jax.ShapeDtypeStruct(baseline.shape, f32),
        in_specs=[hbm] * 5,
        out_specs=vmem,
        scratch_shapes=[
            pltpu.VMEM(footprint.shape[::-1], jnp.int32),
            pltpu.VMEM((1, rank), f32),
            pltpu.VMEM(conduct.shape, f32),
            pltpu.VMEM(baseline.shape, f32),
            pltpu.SemaphoreType.DMA((4,)),
            pltpu.VMEM((pos_local, rows, LANES), f32),
            pltpu.VMEM((pos_local, rows, LANES), f32),
            pltpu.VMEM(basis.shape, bf16),
            pltpu.VMEM((doubled // 2 // LANES, freq_local, rows, 2 * LANES), bf16),
            pltpu.VMEM((messages + 2, 2, rows, LANES), f32),
            pltpu.VMEM((messages, 2, rows, LANES), f32),
            pltpu.VMEM((PARTS, outs, LANES), f32),
            pltpu.VMEM((PARTS, outs, LANES), f32),
            pltpu.VMEM((1, LANES), f32),
            pltpu.VMEM((3 * n_freq, 1, LANES), f32),
            pltpu.VMEM((16, LANES), f32),
            pltpu.VMEM((9, 16, LANES), f32),
            pltpu.SemaphoreType.DMA((pos_local, freq_local)),
            pltpu.SemaphoreType.DMA,
            pltpu.SemaphoreType.DMA((messages, PARTS)),
            pltpu.SemaphoreType.DMA,
            pltpu.SemaphoreType.DMA((PARTS,)),
            pltpu.SemaphoreType.DMA,
            pltpu.SemaphoreType.DMA,
            pltpu.SemaphoreType.DMA,
            pltpu.SemaphoreType.DMA,
            pltpu.SemaphoreType.REGULAR((len(digits_of(n_pos)) + n_freq // 2 - 2,)),
        ],
        compiler_params=pltpu.CompilerParams(
            collective_id=0, has_side_effects=True, vmem_limit_bytes=50 * 1024 * 1024
        ),
    )(*[pltpu.with_memory_space_constraint(x, pltpu.MemorySpace.HBM) for x in (footprint.T, weights.reshape(1, rank), conduct, baseline, basis)])


def solution(mesh):
    return jax.shard_map(
        body,
        mesh=mesh,
        in_specs=(P(), P("pos", "freq", None, None), P(), P(None, "pos", "freq"), P("pos", "freq")),
        out_specs=P("pos", "freq"),
        check_vma=False,
    )
```

```python
import functools
import itertools

import jax
import jax.numpy as jnp
from jax import lax
from jax.experimental import pallas as pl
from jax.experimental.pallas import tpu as pltpu
from jax.sharding import PartitionSpec as P

TH = 4
TW = 8
CELLS = TH * TW
TILE_DEV = 32
PASSES = 3
CAP = 4
EPS = 1e-06
MESH = pl.DeviceIdType.MESH

UNIT = 0.025
CELL = 28
PITCH = 5
TOP = 160
SIN_POLY = (-4.547240826688576, 9.23637803174852, -5.615372827081364)
SCALE_SQ = 0.6259964781564749
DOUBLE = (2.0 + 1e-6) / SCALE_SQ
LANES = 128


def green_block(cross, depth_sq, turns):
    square = cross * cross + depth_sq
    dist = square * lax.rsqrt(square)
    root = lax.rsqrt(dist)
    amp = root * (TOP**0.5)
    scaled_amp = root * (TOP**0.5 * SCALE_SQ)
    out = []
    for rate in turns:
        phase = dist * rate
        x = jnp.round(phase) - phase
        z = x * x
        s = x * (((z + SIN_POLY[0]) * z + SIN_POLY[1]) * z + SIN_POLY[2])
        w = DOUBLE - s * s
        u = w * scaled_amp
        out.append(((u - amp).astype(jnp.bfloat16), (u * s * lax.rsqrt(w)).astype(jnp.bfloat16)))
    return out


def make_unit(lat_ref, dep_ref, basis_v, green_s, rates, elements):
    rows = lat_ref.shape[1]

    def unit(col, p, base=0, height=rows):
        total = None
        for tile in range(elements // LANES):
            start = tile * LANES
            shift = (2 * CELL * col + (PITCH * (elements - 1) - 2 * PITCH * start)).astype(jnp.float32) * 0.5
            for rg in range(base // 16, (base + height) // 16):
                span = pl.ds(rg * 16, 16)
                values = green_block(lat_ref[p, span, :] + shift, dep_ref[p, span, :], rates)
                for f, (cosine, sine) in enumerate(values):
                    green_s[tile, f, span, 0:LANES] = cosine
                    green_s[tile, f, span, LANES : 2 * LANES] = sine
            for f in range(len(rates)):
                right = jnp.concatenate(
                    [
                        basis_v[p, f, start : start + LANES, :],
                        basis_v[p, f, elements + start : elements + start + LANES, :],
                    ],
                    axis=0,
                )
                part = jnp.dot(
                    green_s[tile, f, base : base + height, :], right, preferred_element_type=jnp.float32
                )
                total = part if total is None else total + part
        return total

    return unit


def split3(x):
    hi = x.astype(jnp.bfloat16)
    rest = x - hi.astype(jnp.float32)
    mid = rest.astype(jnp.bfloat16)
    low = (rest - mid.astype(jnp.float32)).astype(jnp.bfloat16)
    return hi, mid, low


PARTS = 4


def digits_of(n_pos):
    return {32: (4, 4, 2), 8: (2, 2, 2)}[n_pos]


def walks_of(pos, n_pos):
    sizes = digits_of(n_pos)
    tables = []
    below = n_pos
    for size in sizes:
        below = below // size
        digit = pos // below % size
        tables.append([(digit + move) % size * below for move in range(size)])
    moves = list(itertools.product(*[range(size) for size in sizes]))[1:]
    moves.sort(key=lambda m: -sum(min(d, z - d) for d, z in zip(m, sizes)))
    lines = []
    for i, size in enumerate(sizes):
        rest = sum(table[0] for j, table in enumerate(tables) if j != i)
        lines.append([rest + tables[i][d] for d in sorted({1, size - 1})])
    return [sum(table[d] for table, d in zip(tables, m)) for m in moves], lines


def kernel(
    n_pos,
    n_freq,
    foot_in,
    weight_in,
    conduct_in,
    base_in,
    basis_ref,
    out_ref,
    foot_ref,
    weight_ref,
    conduct_ref,
    base_ref,
    in_sem,
    lat_v,
    dep_v,
    basis_v,
    green_s,
    send_b,
    recv_b,
    packed,
    arrived,
    value_b,
    value_r,
    halo_b,
    halo_r,
    basis_sem,
    ring_send,
    ring_recv,
    a2a_send,
    a2a_recv,
    val_send,
    val_recv,
    halo_send,
    halo_recv,
    rounds,
):
    pos = lax.axis_index("pos")
    freq = lax.axis_index("freq")
    pos_local, freq_local, doubled, rank = basis_ref.shape
    elements = doubled // 2
    freqs = freq_local * n_freq
    foot = foot_ref.shape[0]
    rows = foot * TH
    pair = rows // 2
    entries = pos_local * foot
    positions = pos_local * n_pos
    half = n_freq // 2
    messages = 4 * half - 2
    iota = lax.broadcasted_iota
    f32, bf16, i32 = jnp.float32, jnp.bfloat16, jnp.int32

    basis_loads = [
        [
            pltpu.make_async_copy(basis_ref.at[p, f], basis_v.at[p, f], basis_sem.at[p, f])
            for f in range(freq_local)
        ]
        for p in range(pos_local)
    ]
    rows_at = {dp: (pos + dp + n_pos) % n_pos if dp else pos for dp in (-1, 0, 1)}
    cols_at = [(freq + df) % n_freq for df in range(n_freq)]

    def other(dp, df):
        return (rows_at[dp], cols_at[df % n_freq] if isinstance(df, int) else (freq + df + n_freq) % n_freq)

    barrier = pltpu.get_barrier_semaphore()
    walks, lines = walks_of(pos, n_pos)
    greeted = [other(0, 1), other(0, -1)] + [(target, freq) for line in lines for target in line]
    for peer in greeted:
        pl.semaphore_signal(barrier, inc=1, device_id=peer, device_id_type=MESH)

    stages = [[other(0, 1), other(0, -1)]] * (n_freq // 2 - 1)
    for size, line in zip(digits_of(n_pos), lines):
        again = max(1, size // 2 - 1) if line is lines[0] else max(1, size // 2)
        stages += [[(target, freq) for target in line]] * again

    def round_signal(i):
        for peer in stages[i]:
            pl.semaphore_signal(rounds.at[i], inc=1, device_id=peer, device_id_type=MESH)

    def round_wait(i):
        pl.semaphore_wait(rounds.at[i], len(stages[i]))

    foot_load, *small_loads = [
        pltpu.make_async_copy(src, dst, in_sem.at[i])
        for i, (src, dst) in enumerate(
            (
                (foot_in, foot_ref),
                (conduct_in, conduct_ref),
                (base_in, base_ref),
                (weight_in, weight_ref),
            )
        )
    ]
    foot_load.start()
    for p in range(pos_local):
        for copy in basis_loads[p]:
            copy.start()
    for copy in small_loads:
        copy.start()

    def wait_all(ref, sem):
        pltpu.make_async_copy(ref, ref, sem).wait()

    near = [(dp, df) for dp in (-1, 0, 1) for df in range(n_freq) if (dp, df) != (0, 0)]
    near.sort(key=lambda d: -min(d[1], n_freq - d[1]) - abs(d[0]) * 0.5)

    expand = iota(i32, (rows, foot), 0) % foot == iota(i32, (rows, foot), 1)
    expand = jnp.where(expand, 1.0, 0.0).astype(bf16)
    foot_load.wait()
    foot_all = foot_ref[...]
    foot_owner = (foot_all // TILE_DEV).astype(f32)
    foot_local = (foot_all % TILE_DEV).astype(f32)
    owner_of = jnp.dot(expand, foot_owner.astype(bf16), preferred_element_type=f32)
    local_of = jnp.dot(expand, foot_local.astype(bf16), preferred_element_type=f32)
    corner = iota(i32, (rows, 1), 0) // foot
    which = iota(i32, (rows, positions), 1)

    def locate(p):
        position = pos * pos_local + p
        owner = jnp.sum(jnp.where(which == position, owner_of, 0.0), axis=1, keepdims=True)
        local = jnp.sum(jnp.where(which == position, local_of, 0.0), axis=1, keepdims=True)
        depth = (TOP + CELL * (owner.astype(i32) * TH + corner)).astype(f32)
        centre = position * (CELL * TW * TILE_DEV // positions)
        lateral = CELL * TW * local.astype(i32) - centre
        lat_v[p] = (lateral - PITCH * iota(i32, (rows, LANES), 1)).astype(f32)
        dep_v[p] = jnp.broadcast_to(depth * depth, (rows, LANES))

    locate(0)

    rates = [
        (freqs // 2 + freq * freq_local + f).astype(f32) * (UNIT / freqs) for f in range(freq_local)
    ]
    unit = make_unit(lat_v, dep_v, basis_v, green_s, rates, elements)

    def compute(u, base=0, height=rows):
        way = 1 - 2 * (u % 2)
        dist = half - (u + 2) // 4
        p = (u + 1) // 2 % 2
        done = unit((freq + way * dist + n_freq) % n_freq, p, base, height)
        for h in range(2):
            send_b[u, h, base : base + height, :] = done[:, h * LANES : (h + 1) * LANES]

    def ring_copy(u):
        return pltpu.make_async_remote_copy(
            src_ref=send_b.at[u],
            dst_ref=recv_b.at[u],
            send_sem=ring_send,
            recv_sem=ring_recv.at[u, 0],
            device_id=other(0, 1 - 2 * lax.rem(u, 2)),
            device_id_type=MESH,
        )

    def ring_part(u, c):
        span = pl.ds((c % 2) * pair, pair)
        return pltpu.make_async_remote_copy(
            src_ref=send_b.at[u, c // 2, span, :],
            dst_ref=recv_b.at[u, c // 2, span, :],
            send_sem=ring_send,
            recv_sem=ring_recv.at[u, c],
            device_id=other(0, 1 - 2 * lax.rem(u, 2)),
            device_id_type=MESH,
        )

    def ring_early(u, base):
        span = pl.ds(base, pair)
        return pltpu.make_async_remote_copy(
            src_ref=send_b.at[u, :, span, :],
            dst_ref=recv_b.at[u, :, span, :],
            send_sem=ring_send,
            recv_sem=ring_recv.at[u, 0],
            device_id=other(0, 1 - 2 * u),
            device_id_type=MESH,
        )

    for copy in basis_loads[0]:
        copy.wait()
    compute(0, 0, pair)
    pl.semaphore_wait(barrier, len(greeted))
    ring_early(0, 0).start()
    for p in range(1, pos_local):
        locate(p)
        for copy in basis_loads[p]:
            copy.wait()
    for u, base in ((1, 0), (0, pair), (1, pair)):
        compute(u, base, pair)
        ring_early(u, base).start()

    for copy in small_loads:
        copy.wait()
    cols = base_ref.shape[1]
    halo_b[...] = jnp.zeros(halo_b.shape, f32)
    halo_b[0:TH, 0:cols] = conduct_ref[0]
    halo_b[TH : 2 * TH, 0:cols] = conduct_ref[1]
    halo_b[2 * TH : 3 * TH, 0:cols] = base_ref[...]
    halo_peers = [(dp, df) for dp in (-1, 0, 1) for df in (-1, 0, 1) if (dp, df) != (0, 0)]

    def halo_copy(i, dp, df):
        return pltpu.make_async_remote_copy(
            src_ref=halo_b,
            dst_ref=halo_r.at[(1 - dp) * 3 + (1 - df)],
            send_sem=halo_send,
            recv_sem=halo_recv,
            device_id=other(dp, df),
            device_id_type=MESH,
        )

    @pl.loop(2, messages + 2)
    def _(u):
        compute(u)

        @pl.when((u >= 4) & (u < messages))
        def _():
            ring_copy(u - 4).wait_recv()
            send_b[u] += recv_b[u - 4]

        @pl.when(u < messages - 4)
        def _():
            ring_copy(u).start()

        @pl.when((u >= messages - 4) & (u < messages))
        def _():
            ring_part(u, 0).start()
            ring_part(u, 1).start()

        @pl.when((u >= messages - 2) & (u < messages))
        def _():
            for c in range(2, PARTS):
                ring_part(u - 2, c).start()
                ring_part(u, c).start()

        for i in range(len(stages)):

            @pl.when(u == 4 + i)
            def _():
                if i > 0:
                    round_wait(i - 1)
                round_signal(i)

        @pl.when(u == 4 + len(stages))
        def _():
            round_wait(len(stages) - 1)
            for i, (dp, df) in enumerate(halo_peers):
                halo_copy(i, dp, df).start()

    outs = n_pos * CAP * 2
    width = pos_local * 2 * foot
    picks = iota(i32, (foot, positions), 1)
    owner_col = jnp.concatenate(
        [
            jnp.sum(jnp.where(picks == pos * pos_local + p, foot_owner, 0.0), axis=1, keepdims=True)
            for p in range(pos_local)
        ],
        axis=0,
    )
    lane = iota(i32, (entries, width), 1)
    entry_of_lane = lane // (2 * foot) * foot + lane % foot
    entry = iota(i32, (entries, width), 0)
    owner_row = jnp.sum(jnp.where(entry == entry_of_lane, owner_col, 0.0), axis=0, keepdims=True)
    same = (owner_col == owner_row) & (entry < entry_of_lane)
    order_row = jnp.sum(jnp.where(same, 1.0, 0.0), axis=0, keepdims=True)
    slot_row = owner_row * CAP + order_row
    to_row = iota(i32, (outs, width), 0)
    from_lane = iota(i32, (outs, width), 1)
    slot_out = (to_row // (2 * CAP) * CAP + to_row % CAP).astype(f32)
    gather = (slot_out == slot_row) & (to_row // CAP % 2 == from_lane // foot % 2)
    gather = jnp.where(gather, 1.0, 0.0).astype(bf16)
    gather = jnp.concatenate([gather] * 3, axis=1)

    mine = foot_owner == pos.astype(f32)
    mine_b = jnp.where(mine, 1.0, 0.0).astype(bf16)
    lower = iota(i32, (foot, foot), 1) < iota(i32, (foot, foot), 0)
    from_p = iota(i32, (positions, positions), 0)
    to_p = iota(i32, (positions, positions), 1)
    later = (from_p // pos_local == to_p // pos_local) & (from_p < to_p)
    moved = jnp.dot(mine_b, jnp.where(later, 1.0, 0.0).astype(bf16), preferred_element_type=f32)
    ahead = jnp.dot(
        jnp.where(lower, 1.0, 0.0).astype(bf16), mine_b, preferred_element_type=f32
    ) + jnp.sum(moved, axis=0, keepdims=True)
    found = jnp.concatenate(
        [
            jnp.sum(jnp.where(mine & (ahead == s), foot_local + 1.0, 0.0), axis=0, keepdims=True)
            for s in range(CAP)
        ],
        axis=0,
    )
    block_of = iota(i32, (positions, outs), 0) // pos_local
    block_to = iota(i32, (positions, outs), 1) // (2 * CAP)
    table = jnp.dot(
        found.astype(bf16),
        jnp.where(block_of == block_to, 1.0, 0.0).astype(bf16),
        preferred_element_type=f32,
    )
    turn = iota(i32, (CAP, outs), 1) % CAP == iota(i32, (CAP, outs), 0)
    tile_in = jnp.sum(jnp.where(turn, table, 0.0), axis=0, keepdims=True)
    row_in = iota(i32, (1, outs), 1) // CAP % 2
    target_row = jnp.where(tile_in > 0.0, tile_in - 1.0 + (TILE_DEV * row_in).astype(f32), -1.0)
    place = iota(i32, (2 * TILE_DEV, outs), 0).astype(f32) == target_row
    place = jnp.where(place, 1.0, 0.0).astype(bf16)
    place = jnp.concatenate([place] * 3, axis=1)

    wait_all(halo_r.at[pl.ds(0, 8)], halo_recv)
    lane16 = iota(i32, (16, LANES), 1)
    row16 = iota(i32, (16, LANES), 0)
    strips = []
    for dp in (-1, 0, 1):
        left = halo_r[(dp + 1) * 3]
        centre = halo_b[...] if dp == 0 else halo_r[(dp + 1) * 3 + 1]
        right = halo_r[(dp + 1) * 3 + 2]
        strip = jnp.where(
            lane16 < PASSES,
            pltpu.roll(left, LANES - cols + PASSES, 1),
            jnp.where(
                lane16 < cols + PASSES,
                pltpu.roll(centre, PASSES, 1),
                pltpu.roll(right, cols + PASSES, 1),
            ),
        )
        strips.append(strip)
    grid_row = row16 + TH * (pos - 1)
    grid_col = lane16 + (cols * freq - PASSES)
    inside = (grid_row >= 0) & (grid_row < TH * n_pos) & (grid_col >= 0) & (grid_col < TILE_DEV * TW)
    inside = inside & (row16 < 3 * TH) & (lane16 < cols + 2 * PASSES)

    def widened(a):
        pieces = [strip[a * TH : (a + 1) * TH, :] for strip in strips]
        tall = jnp.concatenate(pieces + [pieces[0]], axis=0)
        return jnp.where(inside, tall, 0.0)

    across_k = widened(0)
    along_k = widened(1)
    ground = widened(2)
    south_k = jnp.minimum(across_k, pltpu.roll(across_k, 15, 0))
    north_k = jnp.minimum(across_k, pltpu.roll(across_k, 1, 0))
    east_k = jnp.minimum(along_k, pltpu.roll(along_k, LANES - 1, 1))
    west_k = jnp.minimum(along_k, pltpu.roll(along_k, 1, 1))

    block = 2 * CAP
    own_block = pl.ds(pl.multiple_of(pos * block, block), block)

    def owner_copy(target, c):
        return pltpu.make_async_remote_copy(
            src_ref=packed.at[c, pl.ds(pl.multiple_of(target * block, block), block), :],
            dst_ref=arrived.at[c, own_block, :],
            send_sem=a2a_send,
            recv_sem=a2a_recv.at[c],
            device_id=(target, freq),
            device_id_type=MESH,
        )

    for c in range(PARTS):
        span = pl.ds((c % 2) * pair, pair)
        sums = []
        for own, right, left in (
            (messages + 1, messages - 2, messages - 3),
            (messages, messages - 4, messages - 1),
        ):
            ring_part(right, c).wait_recv()
            ring_part(left, c).wait_recv()
            sums.append(send_b[own, c // 2, span, :] + recv_b[right, c // 2, span, :] + recv_b[left, c // 2, span, :])
        stacked = jnp.concatenate(split3(jnp.concatenate(sums, axis=0)), axis=0)
        packed[c] = jnp.dot(gather, stacked, preferred_element_type=f32)

        for target in walks:
            owner_copy(target, c).start()
        pltpu.make_async_copy(
            packed.at[c, own_block, :], arrived.at[c, own_block, :], a2a_recv.at[c]
        ).start()

    energies = [None, None]
    for c in range(PARTS):
        wait_all(arrived.at[c], a2a_recv.at[c])
        stacked = jnp.concatenate(split3(arrived[c]), axis=0)
        compound = jnp.dot(place, stacked, preferred_element_type=f32)
        scaled = compound * compound * weight_ref[0:1, (c // 2) * LANES : (c // 2 + 1) * LANES]
        energies[c % 2] = scaled if energies[c % 2] is None else energies[c % 2] + scaled
    value = jnp.zeros((1, LANES), f32)
    for pair_at, energy in enumerate(energies):
        energy = jnp.sum(energy, axis=1, keepdims=True)
        on = iota(i32, (2 * TILE_DEV, LANES), 1) == iota(i32, (2 * TILE_DEV, LANES), 0) + pair_at * 2 * TILE_DEV
        value = value + jnp.sum(jnp.where(on, energy, 0.0), axis=0, keepdims=True)
    value_b[...] = jnp.sqrt(value / rank + EPS)

    def value_copy(i, dp, df):
        return pltpu.make_async_remote_copy(
            src_ref=value_b,
            dst_ref=value_r.at[(1 - dp) * n_freq + freq],
            send_sem=val_send,
            recv_sem=val_recv,
            device_id=other(dp, df),
            device_id_type=MESH,
        )

    for i, (dp, df) in enumerate(near):
        value_copy(i, dp, df).start()

    value_r[n_freq + freq] = value_b[...]

    wait_all(send_b.at[pl.ds(0, messages)], ring_send)
    wait_all(packed.at[:, pl.ds(0, (n_pos - 1) * block), :], a2a_send)
    wait_all(halo_r.at[pl.ds(0, 8)], halo_send)

    from_r = iota(i32, (LANES, TH * LANES), 0)
    to_n = iota(i32, (LANES, TH * LANES), 1)
    to_col = to_n % LANES + (cols * freq - PASSES) + TW
    chosen = (from_r // TILE_DEV == to_n // LANES) & (from_r % TILE_DEV == to_col // TW - 1)
    spread = jnp.where(chosen, 1.0, 0.0).astype(bf16)
    sub24 = iota(i32, (3 * TW, TH * LANES), 0)
    col24 = iota(i32, (3 * TW, TH * LANES), 1)
    keep = (col24 % LANES + (cols * freq - PASSES) + TW) % TW == sub24 % TW
    sub8 = iota(i32, (TW, LANES), 0)

    wait_all(value_r.at[pl.ds(0, len(near))], val_recv)

    groups = []
    for o in range(3):
        group = jnp.broadcast_to(value_r[o * n_freq], (TW, LANES))
        for col in range(1, n_freq):
            group = jnp.where(sub8 == col, value_r[o * n_freq + col], group)
        groups.append(group)
    wide = None
    for piece in split3(jnp.concatenate(groups, axis=0)):
        part = jnp.dot(piece, spread, preferred_element_type=f32)
        wide = part if wide is None else wide + part
    wide = jnp.where(keep, wide, 0.0)
    field = jnp.zeros((16, LANES), f32)
    for o in range(3):
        summed = jnp.sum(wide[o * TW : (o + 1) * TW, :], axis=0, keepdims=True)
        for r in range(TH):
            field = jnp.where(row16 == o * TH + r, summed[:, r * LANES : (r + 1) * LANES], field)
    u = jnp.where(inside, field + ground, 0.0)
    for sweep in range(PASSES):
        north = north_k * (pltpu.roll(u, 1, 0) - u)
        south = south_k * (pltpu.roll(u, 15, 0) - u)
        west = west_k * (pltpu.roll(u, 1, 1) - u)
        east = east_k * (pltpu.roll(u, LANES - 1, 1) - u)
        u = u + north + south + west + east
    u = pltpu.roll(u, LANES - PASSES, 1)
    out_ref[...] = u[TH : 2 * TH, :cols]

    wait_all(value_r.at[pl.ds(0, len(near))], val_send)


def body(footprint, basis, weights, conduct, baseline):
    pos_local, freq_local, doubled, rank = basis.shape
    foot = footprint.shape[1]
    n_pos = lax.axis_size("pos")
    n_freq = lax.axis_size("freq")
    rows = foot * TH
    outs = n_pos * CAP * 2
    messages = 2 * n_freq - 2
    vmem = pl.BlockSpec(memory_space=pltpu.VMEM)
    hbm = pl.BlockSpec(memory_space=pltpu.MemorySpace.HBM)
    f32, bf16 = jnp.float32, jnp.bfloat16
    return pl.pallas_call(
        functools.partial(kernel, n_pos, n_freq),
        out_shape=jax.ShapeDtypeStruct(baseline.shape, f32),
        in_specs=[hbm] * 5,
        out_specs=vmem,
        scratch_shapes=[
            pltpu.VMEM(footprint.shape[::-1], jnp.int32),
            pltpu.VMEM((1, rank), f32),
            pltpu.VMEM(conduct.shape, f32),
            pltpu.VMEM(baseline.shape, f32),
            pltpu.SemaphoreType.DMA((4,)),
            pltpu.VMEM((pos_local, rows, LANES), f32),
            pltpu.VMEM((pos_local, rows, LANES), f32),
            pltpu.VMEM(basis.shape, bf16),
            pltpu.VMEM((doubled // 2 // LANES, freq_local, rows, 2 * LANES), bf16),
            pltpu.VMEM((messages + 2, 2, rows, LANES), f32),
            pltpu.VMEM((messages, 2, rows, LANES), f32),
            pltpu.VMEM((PARTS, outs, LANES), f32),
            pltpu.VMEM((PARTS, outs, LANES), f32),
            pltpu.VMEM((1, LANES), f32),
            pltpu.VMEM((3 * n_freq, 1, LANES), f32),
            pltpu.VMEM((16, LANES), f32),
            pltpu.VMEM((9, 16, LANES), f32),
            pltpu.SemaphoreType.DMA((pos_local, freq_local)),
            pltpu.SemaphoreType.DMA,
            pltpu.SemaphoreType.DMA((messages, PARTS)),
            pltpu.SemaphoreType.DMA,
            pltpu.SemaphoreType.DMA((PARTS,)),
            pltpu.SemaphoreType.DMA,
            pltpu.SemaphoreType.DMA,
            pltpu.SemaphoreType.DMA,
            pltpu.SemaphoreType.DMA,
            pltpu.SemaphoreType.REGULAR((16,)),
        ],
        compiler_params=pltpu.CompilerParams(
            collective_id=0, has_side_effects=True, vmem_limit_bytes=50 * 1024 * 1024
        ),
    )(*[pltpu.with_memory_space_constraint(x, pltpu.MemorySpace.HBM) for x in (footprint.T, weights.reshape(1, rank), conduct, baseline, basis)])


def solution(mesh):
    return jax.shard_map(
        body,
        mesh=mesh,
        in_specs=(P(), P("pos", "freq", None, None), P(), P(None, "pos", "freq"), P("pos", "freq")),
        out_specs=P("pos", "freq"),
        check_vma=False,
    )
```
